32 devices in a mesh: dp: 4 (over z), field: 8 (over y, x, core).
Axes of the slice: x: 2, y: 2, z: 4, core: 2. Of those that a mesh axis runs over, the one named last changes fastest.
Arguments:
- bin_tokens: int32 [256, 10, 32], P('dp', None, 'field'), may hold values from 0 to 99
- targets: int32 [256, 10, 32], P('dp', None, 'field'), may hold values from 0 to 99
- valid_steps: int32 [256], P('dp'), may hold values from 1 to 10, as said below
- step_count: int32 [], replicated, may hold values from 2 to 4
- embed_master: float32 [32, 100, 128], P('field'), may hold values from -5 to 5
- embed_first: float32 [32, 100, 128], P('field'), may hold values from -4 to 4
- embed_second: float32 [32, 100, 128], P('field'), may hold values from 0.576 to 2.304
- position_master: float32 [10, 32, 128], P(None, 'field'), may hold values from -3.5 to 3.5
- position_first: float32 [10, 32, 128], P(None, 'field'), may hold values from -14 to 14
- position_second: float32 [10, 32, 128], P(None, 'field'), may hold values from 5.76 to 23.04
- head_master: float32 [32, 128, 100], P('field'), may hold values from -0.875 to 0.875
- head_first: float32 [32, 128, 100], P('field'), may hold values from -32 to 32
- head_second: float32 [32, 128, 100], P('field'), may hold values from 25.6 to 102.4
- inproj_master: float32 [128, 384], P('field'), may hold values from -0.5 to 0.5
- inproj_first: float32 [128, 384], P('field'), may hold values from -80 to 80
- inproj_second: float32 [128, 384], P('field'), may hold values from 204.8 to 819.2
- outproj_master: float32 [128, 128], P('field'), may hold values from -3 to 3
- outproj_first: float32 [128, 128], P('field'), may hold values from -48 to 48
- outproj_second: float32 [128, 128], P('field'), may hold values from 73.728 to 294.912
- expand_master: float32 [128, 512], P('field'), may hold values from -0.5 to 0.5
- expand_first: float32 [128, 512], P('field'), may hold values from -64 to 64
- expand_second: float32 [128, 512], P('field'), may hold values from 131.072 to 524.288
- shrink_master: float32 [512, 128], P('field'), may hold values from -0.25 to 0.25
- shrink_first: float32 [512, 128], P('field'), may hold values from -160 to 160
- shrink_second: float32 [512, 128], P('field'), may hold values from 819.2 to 3276.8
- vector_master: float32 [12, 128], P(None, 'field'), may hold values from -1.5 to 1.5, as said below
- vector_first: float32 [12, 128], P(None, 'field'), may hold values from -256 to 256
- vector_second: float32 [12, 128], P(None, 'field'), may hold values from 1843.2 to 7372.8
Outputs:
- losses: float32 [256, 32], P('dp', 'field')
- input_grad: float32 [256, 10, 32, 128], P('dp', None, 'field')
- embed_first_new: float32 [32, 100, 128], P('field')
- embed_second_new: float32 [32, 100, 128], P('field')
- embed_master_new: float32 [32, 100, 128], P('field')
- embed_copy: bfloat16 [32, 100, 128], P('field')
- position_first_new: float32 [10, 32, 128], P(None, 'field')
- position_second_new: float32 [10, 32, 128], P(None, 'field')
- position_master_new: float32 [10, 32, 128], P(None, 'field')
- position_copy: bfloat16 [10, 32, 128], P(None, 'field')
- head_first_new: float32 [32, 128, 100], P('field')
- head_second_new: float32 [32, 128, 100], P('field')
- head_master_new: float32 [32, 128, 100], P('field')
- head_copy: bfloat16 [32, 128, 100], P('field')
- inproj_first_new: float32 [128, 384], P('field')
- inproj_second_new: float32 [128, 384], P('field')
- inproj_master_new: float32 [128, 384], P('field')
- inproj_copy: bfloat16 [128, 384], P('field')
- outproj_first_new: float32 [128, 128], P('field')
- outproj_second_new: float32 [128, 128], P('field')
- outproj_master_new: float32 [128, 128], P('field')
- outproj_copy: bfloat16 [128, 128], P('field')
- expand_first_new: float32 [128, 512], P('field')
- expand_second_new: float32 [128, 512], P('field')
- expand_master_new: float32 [128, 512], P('field')
- expand_copy: bfloat16 [128, 512], P('field')
- shrink_first_new: float32 [512, 128], P('field')
- shrink_second_new: float32 [512, 128], P('field')
- shrink_master_new: float32 [512, 128], P('field')
- shrink_copy: bfloat16 [512, 128], P('field')
- vector_first_new: float32 [12, 128], P(None, 'field')
- vector_second_new: float32 [12, 128], P(None, 'field')
- vector_master_new: float32 [12, 128], P(None, 'field')
- vector_copy: bfloat16 [12, 128], P(None, 'field')
The draws below stay inside these ranges and needn't reach their ends.
Inputs may be any that keep to these rules, and one draw needn't show every extreme that they name: `valid_steps`: in every draw some window has all 10 steps live. `vector_master`: rows 0 and 5 lie within 0.7 to 1.3.
All inputs are finite; a program needn't handle non-finite values.
Results may differ from the reference program's by a relative error of at most 0.01.
The reference program's roundings to bfloat16 on the way count: a program that leaves them out, or rounds other values in their place, can miss the bound.
Values may be sent and summed in bfloat16 or wider, within the bound.
A program may use at most 128 MiB of HBM per device.

```python
import math
from functools import partial
import jax
import jax.numpy as jnp
from jax import lax

D = 128
FF = 512
HEADS = 4
BINS = 100
FIELDS = 32
STEPS = 10
WIN_DEV = 8
WINDOWS = 256
TOKENS = 81920


def draw_valid_steps(key, part):
    first, second = jax.random.split(key)
    lengths = jax.random.randint(first, (WINDOWS,), 1, STEPS + 1)
    entire = jax.random.randint(second, (WINDOWS,), 0, 2)
    lengths = jnp.where(entire == 1, STEPS, lengths)
    return lengths.at[0].set(STEPS).astype(jnp.int32)


def draw_vector_master(key, part):
    first, second = jax.random.split(jax.random.fold_in(key, 7))
    gain_draw = 1.0 + 0.3 * jax.random.uniform(first, (12, D), jnp.float32, -1.0, 1.0)
    shifts = jnp.clip(0.3 * jax.random.normal(second, (12, D), jnp.float32), -1.5, 1.5)
    row_index = jnp.arange(12)[:, None]
    gain_rows = (row_index == 0) | (row_index == 5)
    return jnp.where(gain_rows, gain_draw, shifts).astype(jnp.float32)


def plant(values, stream_key, low, high):
    index_at = [jax.random.randint(jax.random.fold_in(stream_key, axis), (), 0, length) for axis, length in enumerate(values.shape)]
    widest = values.shape.index(max(values.shape))
    beside = index_at[:widest] + [(index_at[widest] + 1) % values.shape[widest]] + index_at[widest + 1:]
    return values.at[tuple(index_at)].set(low).at[tuple(beside)].set(high)


def steps_of(own_key, extent, cuts, least, top_value):
    def one(axis_at, blocks):
        heights = jax.random.uniform(jax.random.fold_in(jax.random.fold_in(own_key, 6), axis_at), (blocks,), jnp.float32, least / len(cuts), top_value / len(cuts))
        return jnp.repeat(jnp.exp(heights), extent[axis_at] // blocks).reshape((-1,) + (1,) * (len(extent) - axis_at - 1))

    factor_of = one(*cuts[0])
    for cut in cuts[1:]:
        factor_of = factor_of * one(*cut)
    return factor_of


def gaussian(own_key, dims, scale, reach, pieces=(), kind=jnp.bfloat16):
    gain = steps_of(own_key, dims, pieces, -0.22, 0.18) if pieces else 1.0
    values = jax.random.normal(own_key, dims, jnp.float32) * scale * gain
    return jnp.minimum(jnp.maximum(values, -reach), reach).astype(kind)


def setup_inputs(seed: int = 0) -> dict:
    key_list = jax.random.split(jax.random.key(seed), 29)
    return {
        "bin_tokens": plant(jax.random.randint(key_list[0], (WINDOWS, STEPS, FIELDS), 0, BINS), jax.random.fold_in(key_list[0], 1), 0, BINS - 1).astype(jnp.int32),
        "targets": plant(jax.random.randint(key_list[1], (WINDOWS, STEPS, FIELDS), 0, BINS), jax.random.fold_in(key_list[1], 1), 0, BINS - 1).astype(jnp.int32),
        "valid_steps": draw_valid_steps(jax.random.fold_in(key_list[28], 71), 0),
        "step_count": jax.random.randint(key_list[3], (), 2, 5).astype(jnp.int32),
        "embed_master": gaussian(key_list[4], (FIELDS, BINS, D), 0.8, 5.0, ((0, 8),), jnp.float32),
        "embed_first": gaussian(key_list[5], (FIELDS, BINS, D), (0.15 * (WINDOWS * STEPS / BINS) ** 0.5), 4.0, ((0, 8),), jnp.float32),
        "embed_second": jnp.clip(jnp.exp(math.log(2.304) - 1.3862944 * jax.random.uniform(key_list[6], (FIELDS, BINS, D), jnp.float32) ** steps_of(key_list[6], (FIELDS, BINS, D), ((0, 8),), -0.2, 0.2)), 0.576, 2.304),
        "position_master": gaussian(key_list[7], (STEPS, FIELDS, D), 0.6, 3.5, ((1, 8),), jnp.float32),
        "position_first": gaussian(key_list[8], (STEPS, FIELDS, D), (0.15 * WINDOWS ** 0.5), 14.0, ((1, 8),), jnp.float32),
        "position_second": jnp.clip(jnp.exp(math.log(23.04) - 1.3862944 * jax.random.uniform(key_list[9], (STEPS, FIELDS, D), jnp.float32) ** steps_of(key_list[9], (STEPS, FIELDS, D), ((1, 8),), -0.2, 0.2)), 5.76, 23.04),
        "head_master": gaussian(key_list[10], (FIELDS, D, BINS), (1.6 * D ** -0.5), 0.875, ((0, 8),), jnp.float32),
        "head_first": gaussian(key_list[11], (FIELDS, D, BINS), (0.1 * (WINDOWS * STEPS) ** 0.5), 32.0, ((0, 8),), jnp.float32),
        "head_second": jnp.clip(jnp.exp(math.log(102.4) - 1.3862944 * jax.random.uniform(key_list[12], (FIELDS, D, BINS), jnp.float32) ** steps_of(key_list[12], (FIELDS, D, BINS), ((0, 8),), -0.2, 0.2)), 25.6, 102.4),
        "inproj_master": gaussian(key_list[13], (D, 3 * D), D ** -0.5, 0.5, ((0, 8),), jnp.float32),
        "inproj_first": gaussian(key_list[14], (D, 3 * D), (0.05 * TOKENS ** 0.5), 80.0, ((0, 8),), jnp.float32),
        "inproj_second": jnp.clip(jnp.exp(math.log(819.2) - 1.3862944 * jax.random.uniform(key_list[15], (D, 3 * D), jnp.float32) ** steps_of(key_list[15], (D, 3 * D), ((0, 8),), -0.2, 0.2)), 204.8, 819.2),
        "outproj_master": gaussian(key_list[16], (D, D), (D // 32) ** -0.5, 3.0, ((0, 8),), jnp.float32),
        "outproj_first": gaussian(key_list[17], (D, D), (0.03 * TOKENS ** 0.5), 48.0, ((0, 8),), jnp.float32),
        "outproj_second": jnp.clip(jnp.exp(math.log(294.912) - 1.3862944 * jax.random.uniform(key_list[18], (D, D), jnp.float32) ** steps_of(key_list[18], (D, D), ((0, 8),), -0.2, 0.2)), 73.728, 294.912),
        "expand_master": gaussian(key_list[19], (D, FF), D ** -0.5, 0.5, ((0, 8),), jnp.float32),
        "expand_first": gaussian(key_list[20], (D, FF), (0.04 * TOKENS ** 0.5), 64.0, ((0, 8),), jnp.float32),
        "expand_second": jnp.clip(jnp.exp(math.log(524.288) - 1.3862944 * jax.random.uniform(key_list[21], (D, FF), jnp.float32) ** steps_of(key_list[21], (D, FF), ((0, 8),), -0.2, 0.2)), 131.072, 524.288),
        "shrink_master": gaussian(key_list[22], (FF, D), FF ** -0.5, 0.25, ((0, 8),), jnp.float32),
        "shrink_first": gaussian(key_list[23], (FF, D), (0.1 * TOKENS ** 0.5), 160.0, ((0, 8),), jnp.float32),
        "shrink_second": jnp.clip(jnp.exp(math.log(3276.8) - 1.3862944 * jax.random.uniform(key_list[24], (FF, D), jnp.float32) ** steps_of(key_list[24], (FF, D), ((0, 8),), -0.2, 0.2)), 819.2, 3276.8),
        "vector_master": draw_vector_master(jax.random.fold_in(key_list[28], 71), 0),
        "vector_first": gaussian(key_list[26], (12, D), (0.15 * TOKENS ** 0.5), 256.0, ((1, 8),), jnp.float32),
        "vector_second": jnp.clip(jnp.exp(math.log(7372.8) - 1.3862944 * jax.random.uniform(key_list[27], (12, D), jnp.float32) ** steps_of(key_list[27], (12, D), ((1, 8),), -0.2, 0.2)), 1843.2, 7372.8),
    }


highest = lax.Precision.HIGHEST

@jax.custom_vjp
def low(v):
    return lax.optimization_barrier(v.astype(jnp.bfloat16)).astype(jnp.float32)

@jax.custom_vjp
def low_back(v):
    return v

def low_keep(v):
    return (low(v), None)

def low_pass(kept, grad):
    return (grad,)

def back_keep(v):
    return (v, None)

def back_low(kept, grad):
    return (low(grad),)
low.defvjp(low_keep, low_pass)
low_back.defvjp(back_keep, back_low)

def layer_norm(values, gain_row, shift_row):
    centred = values - lax.optimization_barrier(jnp.mean(values, axis=-1, keepdims=True))
    spread = lax.optimization_barrier(jnp.mean(centred * centred, axis=-1, keepdims=True))
    return centred * lax.rsqrt(spread + 1e-05) * gain_row + shift_row

def window_block(stream, weights):
    inproj, outproj, expand, shrink, vector = weights
    model_width = stream.shape[-1]
    head_width = model_width // HEADS
    scale_factor = head_width ** (-0.5)
    row_count = stream.shape[1]
    split_shape = (stream.shape[0], row_count, HEADS, head_width)
    norm_one = low(layer_norm(stream, vector[0], vector[1]))
    mixed_rows = jnp.einsum('wrd,de->wre', norm_one, inproj, precision=highest)
    queries = low(low_back(mixed_rows[..., :model_width] + vector[2]))
    key_rows = low(low_back(mixed_rows[..., model_width:2 * model_width]))
    valued = low(low_back(mixed_rows[..., 2 * model_width:] + vector[3]))
    scores = jnp.einsum('wqhc,wkhc->whqk', queries.reshape(split_shape), key_rows.reshape(split_shape), precision=highest)
    scores = low_back(scores * scale_factor)
    positions = jnp.arange(row_count, dtype=jnp.int32)
    causal = positions[:, None] >= positions[None, :]
    scores = jnp.where(causal, scores, -1e+30)
    attend = low(jax.nn.softmax(scores, axis=-1))
    gathered = jnp.einsum('whqk,wkhc->wqhc', attend, valued.reshape(split_shape), precision=highest)
    gathered = low(low_back(gathered.reshape(stream.shape)))
    branch = low_back(jnp.einsum('wrd,de->wre', gathered, outproj, precision=highest) + vector[4])
    residual = stream + branch
    norm_two = low(layer_norm(residual, vector[5], vector[6]))
    upward = low_back(jnp.einsum('wrd,df->wrf', norm_two, expand, precision=highest) + vector[8:12].reshape(-1))
    active = low(jax.nn.gelu(upward, approximate=False))
    result = residual + jnp.einsum('wrf,fd->wrd', active, shrink, precision=highest) + vector[7]
    return low(low_back(result))

def forward(perturb, weights, bin_tokens, targets, live_mask):
    embed_low = low(weights[0])
    position_low = low(weights[1])
    head_low = low(weights[2])
    shared = tuple((low(piece) for piece in weights[3:]))
    bin_axis = jnp.arange(embed_low.shape[1], dtype=jnp.int32)
    token_hot = (bin_tokens[..., None] == bin_axis).astype(jnp.float32)
    embedded = jnp.einsum('wsfb,fbd->wsfd', token_hot, embed_low, precision=highest) + position_low[None]
    sent_rows = low(low_back(embedded + perturb))
    windows_all, steps_count, fields_count, model_width = sent_rows.shape
    blocks = sent_rows.reshape(windows_all // WIN_DEV, WIN_DEV, steps_count * fields_count, model_width)
    mapped = lax.map(jax.checkpoint(partial(window_block, weights=shared)), blocks)
    result = mapped.reshape(windows_all, steps_count, fields_count, model_width)
    logits = low_back(jnp.einsum('wsfd,fdb->wsfb', result, head_low, precision=highest))
    target_hot = (targets[..., None] == bin_axis).astype(jnp.float32)
    per_token = jax.nn.logsumexp(logits, axis=-1) - lax.optimization_barrier(jnp.sum(logits * target_hot, axis=-1))
    losses = lax.optimization_barrier(jnp.sum(per_token * live_mask[:, :, None], axis=1))
    return (jnp.sum(losses), losses)

def rate_table():
    return (0.8, 0.6, 1.6 * D ** (-0.5), D ** (-0.5), (D // 32) ** (-0.5), D ** (-0.5), FF ** (-0.5), 0.3)

def adam_step(master, first, second, gradient, step_rate, correction):
    first_new = 0.5 * first + 0.5 * gradient
    second_new = 0.5 * second + 0.5 * gradient * gradient
    master_new = master - step_rate * (first_new / correction / (jnp.sqrt(second_new / correction) + 1e-08) + 0.1 * master)
    return (first_new, second_new, master_new, master_new.astype(jnp.bfloat16))

def reference(bin_tokens, targets, valid_steps, step_count, embed_master, embed_first, embed_second, position_master, position_first, position_second, head_master, head_first, head_second, inproj_master, inproj_first, inproj_second, outproj_master, outproj_first, outproj_second, expand_master, expand_first, expand_second, shrink_master, shrink_first, shrink_second, vector_master, vector_first, vector_second):
    steps_axis = jnp.arange(STEPS, dtype=jnp.int32)
    live_mask = (steps_axis[None, :] < valid_steps[:, None]).astype(jnp.float32)
    masters = (embed_master, position_master, head_master, inproj_master, outproj_master, expand_master, shrink_master, vector_master)
    firsts = (embed_first, position_first, head_first, inproj_first, outproj_first, expand_first, shrink_first, vector_first)
    seconds = (embed_second, position_second, head_second, inproj_second, outproj_second, expand_second, shrink_second, vector_second)
    perturb = jnp.zeros((WINDOWS, STEPS, FIELDS, D), jnp.float32)
    objective, pullback, losses = jax.vjp(lambda offset, weights: forward(offset, weights, bin_tokens, targets, live_mask), perturb, masters, has_aux=True)
    input_grad, gradients = pullback(jnp.ones_like(objective))
    correction = 1.0 - jnp.power(0.5, step_count.astype(jnp.float32))
    step_rates = rate_table()
    updates = [adam_step(masters[index], firsts[index], seconds[index], gradients[index], step_rates[index], correction) for index in range(8)]
    return (losses, input_grad, updates[0][0], updates[0][1], updates[0][2], updates[0][3], updates[1][0], updates[1][1], updates[1][2], updates[1][3], updates[2][0], updates[2][1], updates[2][2], updates[2][3], updates[3][0], updates[3][1], updates[3][2], updates[3][3], updates[4][0], updates[4][1], updates[4][2], updates[4][3], updates[5][0], updates[5][1], updates[5][2], updates[5][3], updates[6][0], updates[6][1], updates[6][2], updates[6][3], updates[7][0], updates[7][1], updates[7][2], updates[7][3])
```

```python
import functools
import types
import jax
import jax.numpy as jnp
from jax import lax
from jax.experimental import pallas as pl
from jax.experimental.pallas import tpu as pltpu
from jax.sharding import PartitionSpec as P

F32 = jnp.float32
BF16 = jnp.bfloat16
HEADS = 4
NEG = -1e30


def mm(a, b):
    return jnp.dot(a, b, preferred_element_type=F32)


def mm_nt(a, b):
    return lax.dot_general(a, b, (((1,), (1,)), ((), ())), preferred_element_type=F32)


def mm_tn(a, b):
    return lax.dot_general(a, b, (((0,), (0,)), ((), ())), preferred_element_type=F32)


def head_lanes(shape, head):
    lane = lax.broadcasted_iota(jnp.int32, shape, 1)
    return (lane >= head * 32) & (lane < (head + 1) * 32)


def spread_heads(value):
    parts = []
    for head in range(HEADS):
        parts.append(jnp.where(head_lanes((256, 128), head), value[:256], 0.0))
    for head in range(HEADS):
        parts.append(jnp.where(head_lanes((64, 128), head), value[256:], 0.0))
    return jnp.concatenate(parts, axis=0).astype(BF16)


def join_heads(tall):
    out = tall[0:64]
    for head in range(1, HEADS):
        out = jnp.where(head_lanes((64, 128), head), tall[head * 64 : (head + 1) * 64], out)
    return out


def norm_stats(v):
    mean = jnp.mean(v, axis=-1, keepdims=True)
    c = v - mean
    spread = jnp.mean(c * c, axis=-1, keepdims=True)
    inv = lax.rsqrt(spread + 1e-05)
    return c * inv, jnp.broadcast_to(inv, v.shape)


def norm_back(grad, gain, unit, inv):
    e = grad * gain
    m1 = jnp.mean(e, axis=-1, keepdims=True)
    m2 = jnp.mean(e * unit, axis=-1, keepdims=True)
    return inv * (e - m1 - unit * m2)


SCALE = 32 ** (-0.5)
LOG2E = 1.4426950408889634


def causal_square(n):
    k = lax.broadcasted_iota(jnp.int32, (n, n), 0)
    q = lax.broadcasted_iota(jnp.int32, (n, n), 1)
    return k <= q


def soft_cols(pieces):
    peak = functools.reduce(jnp.maximum, [jnp.max(p, axis=0, keepdims=True) for p in pieces])
    shift = peak * (SCALE * LOG2E)
    es = [jnp.exp2(p * (SCALE * LOG2E) - shift) for p in pieces]
    total = functools.reduce(lambda a, b: a + b, [jnp.sum(e, axis=0, keepdims=True) for e in es])
    inv = 1.0 / total
    return [e * inv for e in es]


def forward_window(w, r, take):
    rows = pl.ds(w * 320, 320)
    vec = r.vec
    take(w)
    yield
    x = r.x[rows, :]
    unit, inv = norm_stats(x)
    r.unit1[rows, :] = unit
    r.inv1[rows, :] = inv
    n1 = (unit * vec[0:1, :] + vec[1:2, :]).astype(BF16)
    r.n1[rows, :] = n1
    yield
    mixed = mm(n1, r.w_in[...])
    q = mixed[:, 0:128] + vec[2:3, :]
    k = mixed[:, 128:256]
    v = mixed[:, 256:384] + vec[3:4, :]
    yield
    qm = spread_heads(q)
    kb = k.astype(BF16)
    vb = v.astype(BF16)
    r.qm[w] = qm
    r.k[rows, :] = kb
    r.v[rows, :] = vb
    vt = v.T.astype(BF16)
    yield
    mask128 = causal_square(128)
    ot_parts = []
    for head in range(HEADS):
        s = mm_nt(kb[0:256], qm[head * 256 : (head + 1) * 256])
        yield
        s00 = jnp.where(mask128, s[0:128, 0:128], NEG)
        (p00,) = soft_cols([s00])
        r.pa[w, head, 0:128, 0:128] = p00
        yield
        s11 = jnp.where(mask128, s[128:256, 128:256], NEG)
        p01, p11 = soft_cols([s[0:128, 128:256], s11])
        r.pa[w, head, 0:128, 128:256] = p01
        r.pd[w, head] = p11
        yield
        b11 = p11.astype(BF16)
        pb = jnp.concatenate(
            [
                jnp.concatenate([p00.astype(BF16), p01.astype(BF16)], axis=1),
                jnp.concatenate([jnp.zeros((128, 128), BF16), b11], axis=1),
            ],
            axis=0,
        )
        ot_parts.append(mm(vt[head * 32 : (head + 1) * 32, 0:256], pb))
        yield
    ot = jnp.concatenate(ot_parts, axis=0)
    sb = mm_nt(kb, qm[1024:1280])
    yield
    kk = lax.broadcasted_iota(jnp.int32, (64, 256), 0)
    qq = lax.broadcasted_iota(jnp.int32, (64, 256), 1) % 64
    pbs = []
    for half in range(2):
        cols = slice(half * 128, (half + 1) * 128)
        s_low = jnp.where((kk <= qq)[:, cols], sb[256:320, cols], NEG)
        p_top, p_low = soft_cols([sb[0:256, cols], s_low])
        r.pb[w, 0:256, cols] = p_top
        r.pb[w, 256:320, cols] = p_low
        pbs.append(jnp.concatenate([p_top.astype(BF16), p_low.astype(BF16)], axis=0))
        yield
    pbb = jnp.concatenate(pbs, axis=1)
    otb = mm(vt, pbb)
    yield
    o_tail = join_heads(otb.T)
    o = jnp.concatenate([ot.T, o_tail], axis=0).astype(BF16)
    r.o[rows, :] = o
    yield
    x1 = x + mm(o, r.w_out[...]) + vec[4:5, :]
    yield
    unit, inv = norm_stats(x1)
    r.unit2[rows, :] = unit
    r.inv2[rows, :] = inv
    n2 = (unit * vec[5:6, :] + vec[6:7, :]).astype(BF16)
    r.n2[rows, :] = n2
    yield
    y = x1 + vec[7:8, :]
    for part in range(4):
        cols = slice(part * 128, (part + 1) * 128)
        u = mm(n2, r.w_up[:, cols]) + vec[8 + part : 9 + part, :]
        yield
        phi = 0.5 * (1.0 + lax.erf(u * 0.7071067811865476))
        a = (u * phi).astype(BF16)
        r.a[rows, cols] = a
        r.slope[rows, cols] = phi + u * jnp.exp2(u * u * (-0.5 * LOG2E)) * 0.3989422804014327
        yield
        y = y + mm(a, r.w_down[part * 128 : (part + 1) * 128, :])
        yield
    r.y[rows, :] = y.astype(BF16).astype(F32)


def head_field(f, live, keep, r):
    W, T = r.W, live.shape[1]
    starts = [pl.ds(step * 32 + f, W, stride=320) for step in range(T // W)]
    yf = jnp.concatenate([r.y[at, :] for at in starts], axis=0).astype(BF16)
    wt = r.hr[f]
    lt = mm_nt(wt, yf)
    yield
    bins = lax.broadcasted_iota(jnp.int32, lt.shape, 0)
    lt = jnp.where(bins < r.bins, lt, NEG)
    peak = jnp.max(lt, axis=0, keepdims=True)
    e = jnp.exp(lt - peak)
    yield
    total = jnp.sum(e, axis=0, keepdims=True)
    lse = peak + jnp.log(total)
    hot = bins == r.tgt[f][:, :T]
    picked = jnp.sum(jnp.where(hot, lt, 0.0), axis=0, keepdims=True)
    r.loss[pl.ds(f, 1), 0:T] = (lse - picked) * live
    yield
    dl = (jnp.exp(lt - lse) - hot.astype(F32)) * live
    yield
    keep(mm(dl.astype(BF16), yf))
    yield
    dy = mm(dl.T.astype(BF16), wt)
    yield
    dy = dy.astype(BF16).astype(F32)
    for step, at in enumerate(starts):
        r.dy[at, :] = dy[step * W : (step + 1) * W]


def colsum(v):
    return jnp.sum(v, axis=0, keepdims=True)


def backward_window(w, r, give):
    rows = pl.ds(w * 320, 320)
    vec = r.vec
    gv = r.g_vec
    dy = r.dy[rows, :]
    dyb = dy.astype(BF16)
    gv[7:8, :] += colsum(dy)
    dn2 = jnp.zeros((320, 128), F32)
    n2 = r.n2[rows, :]
    dyt = dy.T.astype(BF16)
    n2t = n2.astype(F32).T.astype(BF16)
    yield
    for part in range(4):
        cols = slice(part * 128, (part + 1) * 128)
        a = r.a[rows, cols]
        da = mm_nt(dyb, r.w_down[part * 128 : (part + 1) * 128, :])
        du = (da * r.slope[rows, cols]).astype(BF16)
        gv[8 + part : 9 + part, :] += colsum(du.astype(F32))
        r.g_downt[:, cols] += mm(dyt, a)
        r.g_up[:, cols] += mm(n2t, du)
        dn2 = dn2 + mm_nt(du, r.w_up[:, cols])
        yield
    unit = r.unit2[rows, :]
    gv[5:6, :] += colsum(dn2 * unit)
    gv[6:7, :] += colsum(dn2)
    dx1 = dy + norm_back(dn2, vec[5:6, :], unit, r.inv2[rows, :])
    yield
    db = dx1.astype(BF16)
    gv[4:5, :] += colsum(db.astype(F32))
    ot = r.o[rows, :].astype(F32).T.astype(BF16)
    r.g_out[...] += mm(ot, db)
    do = mm_nt(db, r.w_out[...])
    yield
    dom = spread_heads(do)
    kb = r.k[rows, :]
    vb = r.v[rows, :]
    kt = kb.astype(F32).T.astype(BF16)
    dv = jnp.zeros((256, 128), F32)
    dk = jnp.zeros((256, 128), F32)
    dqt = []
    yield
    for head in range(HEADS):
        part = slice(head * 256, (head + 1) * 256)
        p00 = r.pa[w, head, 0:128, 0:128]
        p01 = r.pa[w, head, 0:128, 128:256]
        p11 = r.pd[w, head]
        dp = mm_nt(vb[0:256], dom[part])
        yield
        d0 = p00 * dp[0:128, 0:128]
        d1a = p01 * dp[0:128, 128:256]
        d1b = p11 * dp[128:256, 128:256]
        t0 = colsum(d0)
        t1 = colsum(d1a) + colsum(d1b)
        ds00 = (d0 - p00 * t0).astype(BF16)
        ds01 = (d1a - p01 * t1).astype(BF16)
        ds11 = (d1b - p11 * t1).astype(BF16)
        yield
        zero = jnp.zeros((128, 128), BF16)
        pb = jnp.concatenate(
            [
                jnp.concatenate([p00.astype(BF16), p01.astype(BF16)], axis=1),
                jnp.concatenate([zero, p11.astype(BF16)], axis=1),
            ],
            axis=0,
        )
        dsb = jnp.concatenate(
            [jnp.concatenate([ds00, ds01], axis=1), jnp.concatenate([zero, ds11], axis=1)], axis=0
        )
        dv = dv + mm(pb, dom[part])
        dk = dk + mm(dsb, r.qm[w, part, :])
        dqt.append(mm(kt[head * 32 : (head + 1) * 32, 0:256], dsb))
        yield
    pt = r.pb[w]
    dp = mm_nt(vb, dom[1024:1280])
    yield
    d = pt * dp
    dsb = (d - pt * colsum(d)).astype(BF16)
    yield
    dvb = mm(pt.astype(BF16), dom[1024:1280])
    dkb = mm(dsb, r.qm[w, 1024:1280, :])
    yield
    dq_tail = join_heads(mm(kt, dsb).T)
    dq = jnp.concatenate([jnp.concatenate(dqt, axis=0).T, dq_tail], axis=0) * SCALE
    dv = jnp.concatenate([dv + dvb[0:256], dvb[256:320]], axis=0)
    dk = jnp.concatenate([dk + dkb[0:256], dkb[256:320]], axis=0) * SCALE
    dq = dq.astype(BF16)
    dk = dk.astype(BF16)
    dv = dv.astype(BF16)
    yield
    gv[2:3, :] += colsum(dq.astype(F32))
    gv[3:4, :] += colsum(dv.astype(F32))
    dm = jnp.concatenate([dq, dk, dv], axis=1)
    n1t = r.n1[rows, :].astype(F32).T.astype(BF16)
    r.g_in[...] += mm(n1t, dm)
    dn1 = mm_nt(dm, r.w_in[...])
    yield
    unit = r.unit1[rows, :]
    gv[0:1, :] += colsum(dn1 * unit)
    gv[1:2, :] += colsum(dn1)
    dx = dx1 + norm_back(dn1, vec[0:1, :], unit, r.inv1[rows, :])
    r.dx[rows, :] = dx
    yield
    give(w)


def weave(gens, skew, hooks=()):
    live = [[g, i * skew] for i, g in enumerate(gens)]
    hooks = dict(hooks)
    turn = 0
    while live:
        if turn in hooks:
            hooks.pop(turn)()
        for item in list(live):
            if item[1] > 0:
                item[1] -= 1
                continue
            try:
                next(item[0])
            except StopIteration:
                live.remove(item)
        turn += 1
    for left in sorted(hooks):
        hooks[left]()


BAND = 112
MESH = pl.DeviceIdType.MESH


def plan_rows(n, parts):
    plan, row = [], 0
    for name in parts:
        total, blocks = ((128, 3), (128, 1), (128, 4), (512, 1))[name]
        size = total // n
        for block in range(blocks):
            plan.append((name, row, size, block))
            row += size
    return plan, -(-row // 16) * 16


def remote(src, dst, sems, slot, target):
    return pltpu.make_async_remote_copy(
        src_ref=src,
        dst_ref=dst,
        send_sem=sems.at[(0, *slot)],
        recv_sem=sems.at[(1, *slot)],
        device_id=target,
        device_id_type=MESH,
    )


def lane_pick(me, width):
    row = lax.broadcasted_iota(jnp.int32, (width, 128), 0)
    lane = lax.broadcasted_iota(jnp.int32, (width, 128), 1)
    return lane == row + me * width


def cut(i, size):
    return slice(i * size, (i + 1) * size)


def layout(cfg):
    n, m, F, W, S, bins = cfg
    CH = -(-S * F // 8) * 8
    plan, R = plan_rows(n, (0, 1, 2, 3))
    early, RE = plan_rows(n, (2, 3))
    late, RL = plan_rows(n, (0, 1))
    CA = -(-(F * BAND + RE) // (16 * m)) * 16
    CB = -(-(F * BAND + RL + 16) // (16 * m)) * 16
    return types.SimpleNamespace(CH=CH, plan=plan, R=R, early=early, RE=RE, late=late, RL=RL, CA=CA, CB=CB)


def step_kernel(cfg, names, *refs):
    r = types.SimpleNamespace(**dict(zip(names, refs)))
    n, m, F, W, S, bins = cfg
    z = layout(cfg)
    CH, T, G, fields = z.CH, S * W, n * W, n * F
    r.bins, r.W = bins, W
    me, my = lax.axis_index("field"), lax.axis_index("dp")
    chips = n // 2
    core, chip = lax.rem(me, 2), me // 2
    partner = {"field": me + 1 - 2 * core}
    other = lambda k: lax.rem(chip + k, chips)
    back = lambda k: lax.rem(chip + chips - k, chips)
    far = lambda k: {"field": other(k) * 2 + core}
    peer = lambda o: lax.rem(me + o, n)
    field_at = lambda o: {"field": peer(o)}
    dp_at = lambda o: {"dp": lax.rem(my + o, m)}

    barrier = pltpu.get_barrier_semaphore()
    for o in range(1, n):
        pl.semaphore_signal(barrier, 1, device_id=field_at(o), device_id_type=MESH)
    for o in range(1, m):
        pl.semaphore_signal(barrier, 1, device_id=dp_at(o), device_id_type=MESH)

    masters = (r.inproj, r.outproj, r.expand, r.shrink)
    for name, row, size, block in z.plan:
        r.wf[row : row + size, :] = masters[name][:, cut(block, 128)]
    r.wf[z.R : z.R + 16, :] = jnp.zeros((16, 128), F32)
    r.wf[z.R : z.R + 12, :] = mm(r.vector[...].astype(BF16), lane_pick(me, 128 // n).astype(BF16))
    r.ws[...] = r.wf[...].astype(BF16)
    for f in range(F):
        r.tab[f, BAND - 16 :, :] = jnp.zeros((32, 128), F32)
        r.tab[f, 0:bins, :] = r.embed[pl.ds(f, bins, stride=F), :]
        r.tab[f, bins : bins + S, :] = r.position[pl.ds(f, S, stride=F), :]
        r.hf[f, BAND - 16 :, :] = jnp.zeros((16, 128), F32)
        r.hf[f, 0:bins, :] = r.head[pl.ds(f, bins, stride=F), :]
        r.hs[f] = r.hf[f].astype(BF16)

    pl.semaphore_wait(barrier, n - 1 + m - 1)

    remote(r.ws, r.wr.at[me], r.w_sem, (0,), partner).start()
    for k in range(1, chips):
        remote(r.ws, r.wr.at[me], r.w_sem, (k,), far(k)).start()
    r.wr[me] = r.ws[...]

    row = lax.broadcasted_iota(jnp.int32, (128, S * G), 0)
    step_row = lax.broadcasted_iota(jnp.int32, (1, S * G), 1) // G + bins
    for f in range(F):
        for s in range(S):
            r.row[f, :, cut(s, G)] = r.tok[s, f : f + 1, :]
        hot = ((row == r.row[f]) | (row == step_row)).astype(F32).astype(BF16)
        r.hot[f] = hot
        made = mm_tn(hot, r.tab[f].astype(BF16))
        for s in range(S):
            for d in range(n):
                at = s * G + d * W
                r.xsf[pl.ds(d * W * CH + s * F + f, W, stride=CH), :] = made[at : at + W]
    if S * F < CH:
        for g in range(G):
            r.xsf[g * CH + S * F : (g + 1) * CH, :] = jnp.zeros((CH - S * F, 128), F32)
    for d in range(n):
        for w in range(W):
            r.xs[d, w] = r.xsf[cut(d * W + w, CH), :].astype(BF16)
    for w in range(W):
        for o in range(1, n):
            remote(r.xs.at[peer(o), w], r.xr.at[w, me], r.x_sem, (w, o), field_at(o)).start()
    for w in range(W):
        r.xr[w, me] = r.xs[me, w]

    lane = lax.broadcasted_iota(jnp.int32, (1, 128), 1)
    for d in range(n):
        tile, off = d * W // 128, d * W % 128
        for f in range(F):
            total = jnp.zeros((1, 128), jnp.int32)
            for s in range(S):
                got = r.tgi[s, f : f + 1, tile * 128 : min(G, (tile + 1) * 128)]
                if G < 128:
                    got = jnp.concatenate([got] * (128 // G), axis=1)
                turn = (s * W - off) % 128
                got = pltpu.roll(got, turn, 1) if turn else got
                total = jnp.where((lane >= s * W) & (lane < (s + 1) * W), got, total)
            r.tgs[d, f] = total
    there = pl.ds(me * F, F)
    for o in range(1, n):
        remote(r.tgs.at[peer(o)], r.tgt.at[there], r.t_sem, (o,), field_at(o)).start()
    remote(r.hs, r.hr.at[there], r.h_sem, (0,), partner).start()
    for k in range(1, chips):
        remote(r.hs, r.hr.at[there], r.h_sem, (k,), far(k)).start()
    for f in range(F):
        r.tgt[me * F + f] = r.tgs[me, f]
        r.hr[me * F + f] = r.hs[f]

    for k in range(1, chips):
        remote(r.ws, r.wr.at[me], r.w_sem, (k,), far(k)).wait_recv()
        slot = r.wr.at[back(k) * 2 + core]
        remote(slot, slot, r.wf_sem, (k,), partner).start()
    remote(r.ws, r.wr.at[me], r.w_sem, (0,), partner).wait_recv()
    for k in range(1, chips):
        remote(r.ws, r.wr.at[me], r.wf_sem, (k,), partner).wait_recv()
    full = (r.w_in, r.w_out, r.w_up, r.w_down)
    wide = (r.g_in, r.g_out, r.g_up, r.g_down)
    vec = jnp.zeros((16, 128), F32)
    for i in range(n):
        shard = r.wr[i].astype(F32)
        vec = vec + shard[z.R :]
        for name, row, size, block in z.plan:
            to = full if size % 16 == 0 else wide
            piece = shard[row : row + size]
            to[name][cut(i, size), cut(block, 128)] = piece.astype(to[name].dtype)
    for name, row, size, block in z.plan:
        if size % 16:
            full[name][:, cut(block, 128)] = wide[name][:, cut(block, 128)].astype(BF16)
    r.vec[...] = vec
    for g in (r.g_in, r.g_out, r.g_up, r.g_downt, r.g_vec):
        g[...] = jnp.zeros(g.shape, F32)

    def take(w):
        for o in range(1, n):
            remote(r.xs.at[0, 0], r.xr.at[w, 0], r.x_sem, (w, o), field_at(o)).wait_recv()
        for i in range(n):
            r.xf[cut(w * n + i, CH), :] = r.xr[w, i].astype(F32)
        for s in range(S):
            for f in range(F):
                got = r.xf[pl.ds(w * n * CH + s * F + f, n, stride=CH), :]
                r.x[pl.ds(w * 320 + s * fields + f, n, stride=F), :] = got

    weave([forward_window(w, r, take) for w in range(W)], SKEW_F)

    for o in range(1, n):
        remote(r.tgs.at[0], r.tgt.at[there], r.t_sem, (o,), field_at(o)).wait_recv()
    lane = lax.broadcasted_iota(jnp.int32, (1, T), 1)
    live = jnp.zeros((1, T), F32)
    for w in range(W):
        inside = (lane // W).astype(F32) < r.valid[me * W + w].astype(F32)
        live = jnp.where(inside & (lane % W == w), 1.0, live)
    r.loss[...] = jnp.zeros_like(r.loss)
    for k in range(1, chips):
        remote(r.hs, r.hr.at[there], r.h_sem, (k,), far(k)).wait_recv()
        slot = r.hr.at[pl.ds((back(k) * 2 + core) * F, F)]
        remote(slot, slot, r.hf_sem, (k,), partner).start()

    def keeper(ref, c, f):
        def keep(v):
            ref[c, f] = v.astype(ref.dtype)

        return keep

    def heads(which, ref):
        gens = []
        for k in range(chips):
            c = other(k)
            for f in range(F):
                gens.append(head_field((c * 2 + which) * F + f, live, keeper(ref, c, f), r))
        weave(gens, SKEW_H)

    heads(core, r.gho)
    remote(r.hs, r.hr.at[there], r.h_sem, (0,), partner).wait_recv()
    for k in range(1, chips):
        remote(r.hs, r.hr.at[there], r.hf_sem, (k,), partner).wait_recv()
    heads(1 - core, r.ghp)
    remote(r.ghp, r.ghq, r.gp_sem, (0,), partner).start()

    GL = r.lss.shape[-1]
    row = lax.broadcasted_iota(jnp.int32, (128, GL), 0)
    col = lax.broadcasted_iota(jnp.int32, (128, GL), 1)
    group = ((row < T) & (col == me * W + row % W)).astype(F32)
    sums = jnp.dot(r.loss[...], group, preferred_element_type=F32, precision=lax.Precision.HIGHEST)
    for f in range(fields):
        r.lss[f] = sums[f : f + 1, :]
    for o in range(1, n):
        remote(r.lss.at[pl.ds(peer(o) * F, F)], r.lsr.at[me], r.ls_sem, (o,), field_at(o)).start()
    r.lsr[me] = r.lss[there]

    def give(w):
        for s in range(S):
            for f in range(F):
                got = r.dx[pl.ds(w * 320 + s * fields + f, n, stride=F), :]
                r.dxf[pl.ds(w * n * CH + s * F + f, n, stride=CH), :] = got
        for i in range(n):
            if S * F < CH:
                r.dxf[(w * n + i) * CH + S * F : (w * n + i + 1) * CH, :] = jnp.zeros((CH - S * F, 128), F32)
            r.dxs[w, i] = r.dxf[cut(w * n + i, CH), :].astype(BF16)
        for o in range(1, n):
            remote(r.dxs.at[w, peer(o)], r.dxr.at[me, w], r.dx_sem, (w, o), field_at(o)).start()
        r.dxr[me, w] = r.dxs[w, me]

    def pair_heads():
        remote(r.ghp, r.ghq, r.gp_sem, (0,), partner).wait_recv()
        for c in range(chips):
            for f in range(F):
                r.ghs[c, f] = (r.gho[c, f] + r.ghq[c, f].astype(F32)).astype(BF16)
        for k in range(1, chips):
            remote(r.ghs.at[other(k)], r.ghr.at[chip], r.gh_sem, (k,), far(k)).start()
        r.ghr[chip] = r.ghs[chip]

    grads = (r.g_in, r.g_out, r.g_up, r.g_down)

    def send_grads(plan, f32_ref, send, recv, sem):
        for i in range(n):
            for name, row, size, block in plan:
                f32_ref[row : row + size, :] = grads[name][cut(i, size), cut(block, 128)]
            send[i] = f32_ref[...].astype(BF16)
        for o in range(1, n):
            remote(send.at[peer(o)], recv.at[me], sem, (o,), field_at(o)).start()
        recv[me] = send[me]

    def send_early():
        r.g_down[...] = r.g_downt[...].T
        send_grads(z.early, r.gef, r.ges, r.ger, r.ge_sem)

    def total_of(ref, count):
        total = ref[0].astype(F32)
        for i in range(1, count):
            total = total + ref[i].astype(F32)
        return total

    def dp_first(total, send, recv, sem):
        C = send.shape[1]
        for i in range(m):
            send[i] = total[cut(i, C), :].astype(BF16)
        for o in range(1, m):
            remote(send.at[lax.rem(my + o, m)], recv.at[my], sem, (o,), dp_at(o)).start()
        recv[my] = send[my]

    def dp_second(send, recv, sem, last, out, last_sem):
        for o in range(1, m):
            remote(send.at[0], recv.at[my], sem, (o,), dp_at(o)).wait_recv()
        last[...] = total_of(recv, m).astype(BF16)
        for o in range(1, m):
            remote(last, out.at[my], last_sem, (o,), dp_at(o)).start()
        out[my] = last[...]

    def sum_early():
        for k in range(1, chips):
            remote(r.ghs.at[0], r.ghr.at[chip], r.gh_sem, (k,), far(k)).wait_recv()
        for f in range(F):
            total = r.ghr[0, f].astype(F32)
            for c in range(1, chips):
                total = total + r.ghr[c, f].astype(F32)
            r.suma[pl.ds(f, BAND, stride=F), :] = total
        for o in range(1, n):
            remote(r.ges.at[0], r.ger.at[me], r.ge_sem, (o,), field_at(o)).wait_recv()
        r.suma[F * BAND : F * BAND + z.RE, :] = total_of(r.ger, n)
        if m * z.CA > F * BAND + z.RE:
            r.suma[F * BAND + z.RE :, :] = jnp.zeros((m * z.CA - F * BAND - z.RE, 128), F32)
        dp_first(r.suma, r.a1s, r.a1r, r.a1_sem)

    hooks = {2: pair_heads, EARLY: send_early, LATER: sum_early}
    weave([backward_window(w, r, give) for w in range(W)], SKEW_B, hooks)

    send_grads(z.late, r.glf, r.gls, r.glr, r.gl_sem)
    r.gvs[...] = r.g_vec[...].astype(BF16)
    for o in range(1, n):
        remote(r.gvs, r.gvr.at[me], r.gv_sem, (o,), field_at(o)).start()
    r.gvr[me] = r.gvs[...]
    for w in range(W):
        for o in range(1, n):
            remote(r.dxs.at[w, 0], r.dxr.at[me, w], r.dx_sem, (w, o), field_at(o)).wait_recv()
    for g in range(G):
        r.dxw[cut(g, CH), :] = r.dxr[g // W, g % W].astype(F32)
    for f in range(F):
        rows = [r.dxw[pl.ds(s * F + f, G, stride=CH), :] for s in range(S)]
        total = mm(r.hot[f], jnp.concatenate(rows, axis=0).astype(BF16))
        r.sumb[pl.ds(f, BAND, stride=F), :] = total[:BAND]
    for o in range(1, n):
        remote(r.gls.at[0], r.glr.at[me], r.gl_sem, (o,), field_at(o)).wait_recv()
        remote(r.gvs, r.gvr.at[me], r.gv_sem, (o,), field_at(o)).wait_recv()
    base = F * BAND
    r.sumb[base : base + z.RL, :] = total_of(r.glr, n)
    r.sumb[base + z.RL : base + z.RL + 16, :] = total_of(r.gvr, n)
    if m * z.CB > base + z.RL + 16:
        r.sumb[base + z.RL + 16 :, :] = jnp.zeros((m * z.CB - base - z.RL - 16, 128), F32)
    dp_first(r.sumb, r.b1s, r.b1r, r.b1_sem)
    dp_second(r.a1s, r.a1r, r.a1_sem, r.a2s, r.a2r, r.a2_sem)
    dp_second(r.b1s, r.b1r, r.b1_sem, r.b2s, r.b2r, r.b2_sem)

    for o in range(1, m):
        remote(r.a1s.at[0], r.a1r.at[my], r.a1_sem, (o,), dp_at(o)).wait_send()
        remote(r.b1s.at[0], r.b1r.at[my], r.b1_sem, (o,), dp_at(o)).wait_send()
        remote(r.a2s, r.a2r.at[my], r.a2_sem, (o,), dp_at(o)).wait()
        remote(r.b2s, r.b2r.at[my], r.b2_sem, (o,), dp_at(o)).wait()
    remote(r.ws, r.wr.at[me], r.w_sem, (0,), partner).wait_send()
    remote(r.hs, r.hr.at[there], r.h_sem, (0,), partner).wait_send()
    remote(r.ghp, r.ghq, r.gp_sem, (0,), partner).wait_send()
    for k in range(1, chips):
        remote(r.ws, r.wr.at[me], r.w_sem, (k,), far(k)).wait_send()
        remote(r.ws, r.wr.at[me], r.wf_sem, (k,), partner).wait_send()
        remote(r.hs, r.hr.at[there], r.h_sem, (k,), far(k)).wait_send()
        remote(r.hs, r.hr.at[there], r.hf_sem, (k,), partner).wait_send()
        remote(r.ghs.at[0], r.ghr.at[chip], r.gh_sem, (k,), far(k)).wait_send()
    for o in range(1, n):
        remote(r.tgs.at[0], r.tgt.at[there], r.t_sem, (o,), field_at(o)).wait_send()
        remote(r.lss.at[there], r.lsr.at[me], r.ls_sem, (o,), field_at(o)).wait()
        remote(r.ges.at[0], r.ger.at[me], r.ge_sem, (o,), field_at(o)).wait_send()
        remote(r.gls.at[0], r.glr.at[me], r.gl_sem, (o,), field_at(o)).wait_send()
        remote(r.gvs, r.gvr.at[me], r.gv_sem, (o,), field_at(o)).wait_send()
        for w in range(W):
            remote(r.xs.at[0, w], r.xr.at[w, me], r.x_sem, (w, o), field_at(o)).wait_send()
            remote(r.dxs.at[w, 0], r.dxr.at[me, w], r.dx_sem, (w, o), field_at(o)).wait_send()


SKEW_F, SKEW_H, SKEW_B, EARLY, LATER = 4, 0, 2, 24, 40


def step_call(cfg, ins):
    n, m, F, W, S, bins = cfg
    z = layout(cfg)
    CH, L, G, fields, chips = z.CH, W * 320, n * W, n * F, n // 2
    GL = max(G, 128)
    A = jax.ShapeDtypeStruct
    V = pltpu.VMEM
    D = pltpu.SemaphoreType.DMA
    outs = dict(
        dxr=A((n, W, CH, 128), BF16),
        a2r=A((m, z.CA, 128), BF16),
        b2r=A((m, z.CB, 128), BF16),
        lsr=A((n, F, 1, GL), F32),
    )
    scr = dict(
        wf=V((z.R + 16, 128), F32),
        ws=V((z.R + 16, 128), BF16),
        wr=V((n, z.R + 16, 128), BF16),
        tab=V((F, 128, 128), F32),
        hf=V((F, BAND, 128), F32),
        hs=V((F, BAND, 128), BF16),
        hr=V((fields, BAND, 128), BF16),
        row=V((F, 1, S * G), jnp.int32),
        hot=V((F, 128, S * G), BF16),
        xsf=V((G * CH, 128), F32),
        xs=V((n, W, CH, 128), BF16),
        xr=V((W, n, CH, 128), BF16),
        xf=V((G * CH, 128), F32),
        tgs=V((n, F, 1, 128), jnp.int32),
        tgt=V((fields, 1, 128), jnp.int32),
        w_in=V((128, 384), BF16),
        w_out=V((128, 128), BF16),
        w_up=V((128, 512), BF16),
        w_down=V((512, 128), BF16),
        vec=V((16, 128), F32),
        x=V((L, 128), F32),
        unit1=V((L, 128), F32),
        inv1=V((L, 128), F32),
        unit2=V((L, 128), F32),
        inv2=V((L, 128), F32),
        n1=V((L, 128), BF16),
        n2=V((L, 128), BF16),
        qm=V((W, 1280, 128), BF16),
        k=V((L, 128), BF16),
        v=V((L, 128), BF16),
        o=V((L, 128), BF16),
        pa=V((W, HEADS, 128, 256), F32),
        pd=V((W, HEADS, 128, 128), F32),
        pb=V((W, 320, 256), F32),
        a=V((L, 512), BF16),
        slope=V((L, 512), F32),
        y=V((L, 128), F32),
        dy=V((L, 128), F32),
        dx=V((L, 128), F32),
        dxf=V((G * CH, 128), F32),
        dxw=V((G * CH, 128), F32),
        dxs=V((W, n, CH, 128), BF16),
        loss=V((fields, 128), F32),
        lss=V((fields, 1, GL), F32),
        gho=V((chips, F, BAND, 128), F32),
        ghp=V((chips, F, BAND, 128), BF16),
        ghq=V((chips, F, BAND, 128), BF16),
        ghs=V((chips, F, BAND, 128), BF16),
        ghr=V((chips, F, BAND, 128), BF16),
        g_in=V((128, 384), F32),
        g_out=V((128, 128), F32),
        g_up=V((128, 512), F32),
        g_downt=V((128, 512), F32),
        g_down=V((512, 128), F32),
        g_vec=V((16, 128), F32),
        gef=V((z.RE, 128), F32),
        ges=V((n, z.RE, 128), BF16),
        ger=V((n, z.RE, 128), BF16),
        glf=V((z.RL, 128), F32),
        gls=V((n, z.RL, 128), BF16),
        glr=V((n, z.RL, 128), BF16),
        gvs=V((16, 128), BF16),
        gvr=V((n, 16, 128), BF16),
        suma=V((m * z.CA, 128), F32),
        a1s=V((m, z.CA, 128), BF16),
        a1r=V((m, z.CA, 128), BF16),
        a2s=V((z.CA, 128), BF16),
        sumb=V((m * z.CB, 128), F32),
        b1s=V((m, z.CB, 128), BF16),
        b1r=V((m, z.CB, 128), BF16),
        b2s=V((z.CB, 128), BF16),
        w_sem=D((2, chips)),
        wf_sem=D((2, chips)),
        h_sem=D((2, chips)),
        hf_sem=D((2, chips)),
        gp_sem=D((2, 1)),
        gh_sem=D((2, chips)),
        x_sem=D((2, W, n)),
        dx_sem=D((2, W, n)),
        t_sem=D((2, n)),
        ls_sem=D((2, n)),
        ge_sem=D((2, n)),
        gl_sem=D((2, n)),
        gv_sem=D((2, n)),
        a1_sem=D((2, m)),
        a2_sem=D((2, m)),
        b1_sem=D((2, m)),
        b2_sem=D((2, m)),
    )
    names = list(ins) + list(outs) + list(scr)
    vm = pl.BlockSpec(memory_space=pltpu.VMEM)
    sm = pl.BlockSpec(memory_space=pltpu.SMEM)
    res = pl.pallas_call(
        functools.partial(step_kernel, cfg, names),
        out_shape=list(outs.values()),
        in_specs=[sm if ins[k].ndim == 1 else vm for k in ins],
        out_specs=[vm] * len(outs),
        scratch_shapes=list(scr.values()),
        compiler_params=pltpu.CompilerParams(vmem_limit_bytes=VMEM_ALL, collective_id=0, has_side_effects=True),
        name="step",
    )(*ins.values())
    return types.SimpleNamespace(**dict(zip(outs, res)))


VMEM_ALL = 64 * 1024 * 1024 - 65536
RATES = (0.8, 0.6, 1.6 * 128 ** (-0.5), 128 ** (-0.5), 4 ** (-0.5), 128 ** (-0.5), 512 ** (-0.5), 0.3)
EMBED, POSITION, HEAD, BLOCK, VECTOR = 0, 1, 2, 3, 7


def adam_kernel(cfg, count_ref, dxr, a2r, b2r, lsr, *refs):
    n, m, F, W, S, bins = cfg
    z = layout(cfg)
    state, losses, input_grad, outs, suma, sumb = refs[:24], refs[24], refs[25], refs[26:58], refs[58], refs[59]
    me = lax.axis_index("field")
    half = lax.fori_loop(0, count_ref[0], lambda i, v: v * 0.5, jnp.float32(1.0))
    inv_c = 1.0 / (jnp.zeros((1, 128), F32) + (1.0 - half))

    for g in range(n * W):
        input_grad[cut(g, S * F), :] = dxr[g // W, g % W].astype(F32)[: S * F]
    for f in range(F):
        total = lsr[0, f]
        for i in range(1, n):
            total = total + lsr[i, f]
        losses[f : f + 1, :] = total[:, : n * W]

    def adam(weight, at, grad):
        c = inv_c[0:1, 0 : grad.shape[-1]]
        master = state[3 * weight][at]
        first = 0.5 * state[3 * weight + 1][at] + 0.5 * grad
        second = 0.5 * state[3 * weight + 2][at] + 0.5 * grad * grad
        new = master - RATES[weight] * (first * c / (jnp.sqrt(second * c) + 1e-08) + 0.1 * master)
        outs[4 * weight][at] = first
        outs[4 * weight + 1][at] = second
        outs[4 * weight + 2][at] = new
        outs[4 * weight + 3][at] = new.astype(BF16)

    for i in range(m):
        suma[cut(i, z.CA), :] = a2r[i].astype(F32)
        sumb[cut(i, z.CB), :] = b2r[i].astype(F32)
    every = slice(None)
    base, tokens = F * BAND, F * bins
    adam(HEAD, (every, every), suma[0:tokens, :])
    adam(EMBED, (every, every), sumb[0:tokens, :])
    adam(POSITION, (every, every), sumb[tokens : tokens + S * F, :])
    for plan, ref in ((z.early, suma), (z.late, sumb)):
        for name, row, size, block in plan:
            adam(BLOCK + name, (every, cut(block, 128)), ref[base + row : base + row + size, :])
    vecs = sumb[base + z.RL : base + z.RL + 16, :]
    pick = lane_pick(me, 128 // n).astype(F32)
    mine = lax.dot_general(
        vecs, pick, (((1,), (1,)), ((), ())), preferred_element_type=F32, precision=lax.Precision.HIGHEST
    )
    adam(VECTOR, (every, every), mine[0:12])


def adam_call(cfg, count, got, state):
    n, m, F, W, S, bins = cfg
    z = layout(cfg)
    A = jax.ShapeDtypeStruct
    outs = [A((F, n * W), F32), A((n * W * S * F, 128), F32)]
    for i in range(8):
        shape = state[3 * i].shape
        outs.extend([A(shape, F32)] * 3 + [A(shape, BF16)])
    vm = pl.BlockSpec(memory_space=pltpu.VMEM)
    sm = pl.BlockSpec(memory_space=pltpu.SMEM)
    return pl.pallas_call(
        functools.partial(adam_kernel, cfg),
        out_shape=outs,
        in_specs=[sm] + [vm] * 28,
        out_specs=[vm] * len(outs),
        scratch_shapes=[pltpu.VMEM((m * z.CA, 128), F32), pltpu.VMEM((m * z.CB, 128), F32)],
        compiler_params=pltpu.CompilerParams(vmem_limit_bytes=VMEM_ALL),
        name="adam",
    )(count, got.dxr, got.a2r, got.b2r, got.lsr, *state)


def local(n, m, bin_tokens, targets, valid_steps, step_count, *state):
    windows, S, F = bin_tokens.shape
    bins = state[0].shape[1]
    cfg = (n, m, F, windows // n, S, bins)
    by_bin = lambda v: v.transpose(1, 0, 2).reshape(bins * F, 128)
    by_class = lambda v: v.transpose(2, 0, 1).reshape(bins * F, 128)
    flat = [by_bin(v) for v in state[0:3]] + [v.reshape(S * F, 128) for v in state[3:6]]
    flat += [by_class(v) for v in state[6:9]] + list(state[9:])
    ins = dict(
        tok=bin_tokens.transpose(1, 2, 0),
        tgi=targets.transpose(1, 2, 0),
        valid=valid_steps,
        embed=flat[0],
        position=flat[3],
        head=flat[6],
        inproj=flat[9],
        outproj=flat[12],
        expand=flat[15],
        shrink=flat[18],
        vector=flat[21],
    )
    got = step_call(cfg, ins)
    losses, input_grad, *new = adam_call(cfg, step_count.reshape(1), got, flat)
    new[0:4] = [v.reshape(bins, F, 128).transpose(1, 0, 2) for v in new[0:4]]
    new[4:8] = [v.reshape(S, F, 128) for v in new[4:8]]
    new[8:12] = [v.reshape(bins, F, 128).transpose(1, 2, 0) for v in new[8:12]]
    return (losses.transpose(1, 0), input_grad.reshape(windows, S, F, 128), *new)


def solution(mesh):
    n, m = mesh.shape["field"], mesh.shape["dp"]
    stack, rows, cols = P("field", None, None), P("field", None), P(None, "field")
    by_weight = (stack, P(None, "field", None), stack, rows, rows, rows, rows, cols)
    in_specs = [P("dp", None, "field"), P("dp", None, "field"), P("dp"), P()]
    out_specs = [P("dp", "field"), P("dp", None, "field", None)]
    for spec in by_weight:
        in_specs.extend([spec] * 3)
        out_specs.extend([spec] * 4)
    return jax.shard_map(
        functools.partial(local, n, m),
        mesh=mesh,
        in_specs=tuple(in_specs),
        out_specs=tuple(out_specs),
        check_vma=False,
    )
```

```python
import functools
import types
import jax
import jax.numpy as jnp
from jax import lax
from jax.experimental import pallas as pl
from jax.experimental.pallas import tpu as pltpu
from jax.sharding import PartitionSpec as P

F32 = jnp.float32
BF16 = jnp.bfloat16
HEADS = 4
NEG = -1e30


def mm(a, b):
    return jnp.dot(a, b, preferred_element_type=F32)


def mm_nt(a, b):
    return lax.dot_general(a, b, (((1,), (1,)), ((), ())), preferred_element_type=F32)


def mm_tn(a, b):
    return lax.dot_general(a, b, (((0,), (0,)), ((), ())), preferred_element_type=F32)


def head_lanes(shape, head):
    lane = lax.broadcasted_iota(jnp.int32, shape, 1)
    return (lane >= head * 32) & (lane < (head + 1) * 32)


def spread_heads(value):
    parts = []
    for head in range(HEADS):
        parts.append(jnp.where(head_lanes((256, 128), head), value[:256], 0.0))
    for head in range(HEADS):
        parts.append(jnp.where(head_lanes((64, 128), head), value[256:], 0.0))
    return jnp.concatenate(parts, axis=0).astype(BF16)


def join_heads(tall):
    out = tall[0:64]
    for head in range(1, HEADS):
        out = jnp.where(head_lanes((64, 128), head), tall[head * 64 : (head + 1) * 64], out)
    return out


def norm_stats(v):
    mean = jnp.mean(v, axis=-1, keepdims=True)
    c = v - mean
    spread = jnp.mean(c * c, axis=-1, keepdims=True)
    inv = lax.rsqrt(spread + 1e-05)
    return c * inv, jnp.broadcast_to(inv, v.shape)


def norm_back(grad, gain, unit, inv):
    e = grad * gain
    m1 = jnp.mean(e, axis=-1, keepdims=True)
    m2 = jnp.mean(e * unit, axis=-1, keepdims=True)
    return inv * (e - m1 - unit * m2)


SCALE = 32 ** (-0.5)
LOG2E = 1.4426950408889634


def causal_square(n):
    k = lax.broadcasted_iota(jnp.int32, (n, n), 0)
    q = lax.broadcasted_iota(jnp.int32, (n, n), 1)
    return k <= q


def soft_cols(pieces):
    peak = functools.reduce(jnp.maximum, [jnp.max(p, axis=0, keepdims=True) for p in pieces])
    shift = peak * (SCALE * LOG2E)
    es = [jnp.exp2(p * (SCALE * LOG2E) - shift) for p in pieces]
    total = functools.reduce(lambda a, b: a + b, [jnp.sum(e, axis=0, keepdims=True) for e in es])
    inv = 1.0 / total
    return [e * inv for e in es]


def forward_window(w, r, take):
    rows = pl.ds(w * 320, 320)
    vec = r.vec
    take(w)
    yield
    x = r.x[rows, :]
    unit, inv = norm_stats(x)
    r.unit1[rows, :] = unit
    r.inv1[rows, :] = inv
    n1 = (unit * vec[0:1, :] + vec[1:2, :]).astype(BF16)
    r.n1[rows, :] = n1
    yield
    mixed = mm(n1, r.w_in[...])
    q = mixed[:, 0:128] + vec[2:3, :]
    k = mixed[:, 128:256]
    v = mixed[:, 256:384] + vec[3:4, :]
    yield
    qm = spread_heads(q)
    kb = k.astype(BF16)
    vb = v.astype(BF16)
    r.qm[w] = qm
    r.k[rows, :] = kb
    r.v[rows, :] = vb
    vt = v.T.astype(BF16)
    yield
    mask128 = causal_square(128)
    ot_parts = []
    for head in range(HEADS):
        s = mm_nt(kb[0:256], qm[head * 256 : (head + 1) * 256])
        yield
        s00 = jnp.where(mask128, s[0:128, 0:128], NEG)
        (p00,) = soft_cols([s00])
        r.pa[w, head, 0:128, 0:128] = p00
        yield
        s11 = jnp.where(mask128, s[128:256, 128:256], NEG)
        p01, p11 = soft_cols([s[0:128, 128:256], s11])
        r.pa[w, head, 0:128, 128:256] = p01
        r.pd[w, head] = p11
        yield
        b11 = p11.astype(BF16)
        pb = jnp.concatenate(
            [
                jnp.concatenate([p00.astype(BF16), p01.astype(BF16)], axis=1),
                jnp.concatenate([jnp.zeros((128, 128), BF16), b11], axis=1),
            ],
            axis=0,
        )
        ot_parts.append(mm(vt[head * 32 : (head + 1) * 32, 0:256], pb))
        yield
    ot = jnp.concatenate(ot_parts, axis=0)
    sb = mm_nt(kb, qm[1024:1280])
    yield
    kk = lax.broadcasted_iota(jnp.int32, (64, 256), 0)
    qq = lax.broadcasted_iota(jnp.int32, (64, 256), 1) % 64
    pbs = []
    for half in range(2):
        cols = slice(half * 128, (half + 1) * 128)
        s_low = jnp.where((kk <= qq)[:, cols], sb[256:320, cols], NEG)
        p_top, p_low = soft_cols([sb[0:256, cols], s_low])
        r.pb[w, 0:256, cols] = p_top
        r.pb[w, 256:320, cols] = p_low
        pbs.append(jnp.concatenate([p_top.astype(BF16), p_low.astype(BF16)], axis=0))
        yield
    pbb = jnp.concatenate(pbs, axis=1)
    otb = mm(vt, pbb)
    yield
    o_tail = join_heads(otb.T)
    o = jnp.concatenate([ot.T, o_tail], axis=0).astype(BF16)
    r.o[rows, :] = o
    yield
    x1 = x + mm(o, r.w_out[...]) + vec[4:5, :]
    yield
    unit, inv = norm_stats(x1)
    r.unit2[rows, :] = unit
    r.inv2[rows, :] = inv
    n2 = (unit * vec[5:6, :] + vec[6:7, :]).astype(BF16)
    r.n2[rows, :] = n2
    yield
    y = x1 + vec[7:8, :]
    for part in range(2):
        cols = cut(part, 256)
        bias = jnp.concatenate([vec[8 + 2 * part : 9 + 2 * part, :], vec[9 + 2 * part : 10 + 2 * part, :]], axis=1)
        u = mm(n2, r.w_up[:, cols]) + bias
        yield
        phi = 0.5 * (1.0 + lax.erf(u * 0.7071067811865476))
        a = (u * phi).astype(BF16)
        r.a[rows, cols] = a
        r.slope[rows, cols] = phi + u * jnp.exp2(u * u * (-0.5 * LOG2E)) * 0.3989422804014327
        yield
        y = y + mm(a, r.w_down[cols, :])
        yield
    r.y[rows, :] = y.astype(BF16).astype(F32)


def head_field(f, live, keep, r):
    W, T = r.W, live.shape[1]
    starts = [pl.ds(step * 32 + f, W, stride=320) for step in range(T // W)]
    yf = jnp.concatenate([r.y[at, :] for at in starts], axis=0).astype(BF16)
    wt = r.hr[pl.ds(pl.multiple_of(f * r.band, 16), r.band), :]
    lt = mm_nt(wt, yf)
    yield
    bins = lax.broadcasted_iota(jnp.int32, lt.shape, 0)
    lt = jnp.where(bins < r.bins, lt, NEG)
    peak = jnp.max(lt, axis=0, keepdims=True)
    e = jnp.exp(lt - peak)
    yield
    total = jnp.sum(e, axis=0, keepdims=True)
    lse = peak + jnp.log(total)
    hot = bins.astype(F32) == r.tgt[f][:, :T]
    picked = jnp.sum(jnp.where(hot, lt, 0.0), axis=0, keepdims=True)
    r.loss[pl.ds(f, 1), 0:T] = (lse - picked) * live
    yield
    dl = (jnp.exp(lt - lse) - hot.astype(F32)) * live
    yield
    keep(mm(dl.astype(BF16), yf))
    yield
    dy = mm(dl.T.astype(BF16), wt)
    yield
    dy = dy.astype(BF16).astype(F32)
    for step, at in enumerate(starts):
        r.dy[at, :] = dy[step * W : (step + 1) * W]


def colsum(v):
    return jnp.sum(v, axis=0, keepdims=True)


def backward_window(w, r, give):
    rows = pl.ds(w * 320, 320)
    vec = r.vec
    gv = r.g_vec
    dy = r.dy[rows, :]
    dyb = dy.astype(BF16)
    gv[7:8, :] += colsum(dy)
    dn2 = jnp.zeros((320, 128), F32)
    r.dyb[rows, :] = dyb
    yield
    for part in range(2):
        cols = cut(part, 256)
        da = mm_nt(dyb, r.w_down[cols, :])
        du = (da * r.slope[rows, cols]).astype(BF16)
        bias = colsum(du.astype(F32))
        gv[8 + 2 * part : 9 + 2 * part, :] += bias[:, 0:128]
        gv[9 + 2 * part : 10 + 2 * part, :] += bias[:, 128:256]
        r.du[rows, cols] = du
        dn2 = dn2 + mm_nt(du, r.w_up[:, cols])
        yield
    unit = r.unit2[rows, :]
    gv[5:6, :] += colsum(dn2 * unit)
    gv[6:7, :] += colsum(dn2)
    dx1 = dy + norm_back(dn2, vec[5:6, :], unit, r.inv2[rows, :])
    yield
    db = dx1.astype(BF16)
    gv[4:5, :] += colsum(db.astype(F32))
    r.db[rows, :] = db
    do = mm_nt(db, r.w_out[...])
    yield
    dom = spread_heads(do)
    kb = r.k[rows, :]
    vb = r.v[rows, :]
    kt = kb.astype(F32).T.astype(BF16)
    dv = jnp.zeros((256, 128), F32)
    dk = jnp.zeros((256, 128), F32)
    dqt = []
    yield
    for head in range(HEADS):
        part = slice(head * 256, (head + 1) * 256)
        p00 = r.pa[w, head, 0:128, 0:128]
        p01 = r.pa[w, head, 0:128, 128:256]
        p11 = r.pd[w, head]
        dp = mm_nt(vb[0:256], dom[part])
        yield
        d0 = p00 * dp[0:128, 0:128]
        d1a = p01 * dp[0:128, 128:256]
        d1b = p11 * dp[128:256, 128:256]
        t0 = colsum(d0)
        t1 = colsum(d1a) + colsum(d1b)
        ds00 = (d0 - p00 * t0).astype(BF16)
        ds01 = (d1a - p01 * t1).astype(BF16)
        ds11 = (d1b - p11 * t1).astype(BF16)
        yield
        zero = jnp.zeros((128, 128), BF16)
        pb = jnp.concatenate(
            [
                jnp.concatenate([p00.astype(BF16), p01.astype(BF16)], axis=1),
                jnp.concatenate([zero, p11.astype(BF16)], axis=1),
            ],
            axis=0,
        )
        dsb = jnp.concatenate(
            [jnp.concatenate([ds00, ds01], axis=1), jnp.concatenate([zero, ds11], axis=1)], axis=0
        )
        dv = dv + mm(pb, dom[part])
        dk = dk + mm(dsb, r.qm[w, part, :])
        dqt.append(mm(kt[head * 32 : (head + 1) * 32, 0:256], dsb))
        yield
    pt = r.pb[w]
    dp = mm_nt(vb, dom[1024:1280])
    yield
    d = pt * dp
    dsb = (d - pt * colsum(d)).astype(BF16)
    yield
    dvb = mm(pt.astype(BF16), dom[1024:1280])
    dkb = mm(dsb, r.qm[w, 1024:1280, :])
    yield
    dq_tail = join_heads(mm(kt, dsb).T)
    dq = jnp.concatenate([jnp.concatenate(dqt, axis=0).T, dq_tail], axis=0) * SCALE
    dv = jnp.concatenate([dv + dvb[0:256], dvb[256:320]], axis=0)
    dk = jnp.concatenate([dk + dkb[0:256], dkb[256:320]], axis=0) * SCALE
    dq = dq.astype(BF16)
    dk = dk.astype(BF16)
    dv = dv.astype(BF16)
    yield
    gv[2:3, :] += colsum(dq.astype(F32))
    gv[3:4, :] += colsum(dv.astype(F32))
    dm = jnp.concatenate([dq, dk, dv], axis=1)
    r.dm[rows, :] = dm
    dn1 = mm_nt(dm, r.w_in[...])
    yield
    unit = r.unit1[rows, :]
    gv[0:1, :] += colsum(dn1 * unit)
    gv[1:2, :] += colsum(dn1)
    dx = dx1 + norm_back(dn1, vec[0:1, :], unit, r.inv1[rows, :])
    r.dx[rows, :] = dx
    yield
    give(w)


def weave(gens, skew, hooks=()):
    live = [[g, i * skew] for i, g in enumerate(gens)]
    hooks = dict(hooks)
    turn = 0
    while live:
        if turn in hooks:
            hooks.pop(turn)()
        for item in list(live):
            if item[1] > 0:
                item[1] -= 1
                continue
            try:
                next(item[0])
            except StopIteration:
                live.remove(item)
        turn += 1
    for left in sorted(hooks):
        hooks[left]()


MESH = pl.DeviceIdType.MESH


def plan_rows(n, parts):
    plan, row = [], 0
    for name in parts:
        total, blocks = ((128, 3), (128, 1), (128, 4), (512, 1))[name]
        size = total // n
        for block in range(blocks):
            plan.append((name, row, size, block))
            row += size
    return plan, -(-row // 16) * 16


class Lane:
    def __init__(self, sems, first, anyone):
        self.sems, self.first, self.anyone = sems, first, anyone

    def copy(self, src, dst, slot, target):
        return pltpu.make_async_remote_copy(
            src_ref=src,
            dst_ref=dst,
            send_sem=self.sems.at[self.first],
            recv_sem=self.sems.at[self.first + 1 + slot],
            device_id=target,
            device_id_type=MESH,
        )

    def start(self, src, dst, target, slot=0):
        self.copy(src, dst, slot, target).start()

    def arrived(self, like, slot=0):
        self.copy(like, like, slot, self.anyone).wait_recv()

    def left(self, like):
        self.copy(like, like, 0, self.anyone).wait_send()


def lane_pick(me, width):
    row = lax.broadcasted_iota(jnp.int32, (width, 128), 0)
    lane = lax.broadcasted_iota(jnp.int32, (width, 128), 1)
    return lane == row + me * width


def cut(i, size):
    return slice(i * size, (i + 1) * size)


def layout(cfg):
    n, m, F, W, S, bins = cfg
    CH = -(-S * F // 8) * 8
    BAND = 112 if F * 112 % (8 * m) == 0 else 128
    plan, R = plan_rows(n, (0, 1, 2, 3))
    early, RE = plan_rows(n, (2, 3))
    late, RL = plan_rows(n, (0, 1))
    CB = -(-(F * BAND + RE + RL + 16) // (16 * m)) * 16
    HQ = F * BAND // m
    return types.SimpleNamespace(CH=CH, BAND=BAND, plan=plan, R=R, early=early, RE=RE, late=late, RL=RL, CB=CB, HQ=HQ)


def step_kernel(cfg, names, count, valid, *refs):
    r = types.SimpleNamespace(**dict(zip(names, refs[count:])))
    r.valid, r.outside, r.inside, r.load_sems = valid, refs[:count], refs[-1 - count : -1], refs[-1]
    n, m, F, W, S, bins = cfg
    z = layout(cfg)
    CH, T, G, fields, BAND, HQ = z.CH, S * W, n * W, n * F, z.BAND, z.HQ
    FB = F * BAND
    r.bins, r.W, r.band = bins, W, BAND
    r.xsf = r.dxf = r.rows_out
    r.xf = r.dxw = r.rows_in
    r.dx = r.y
    me, my = lax.axis_index("field"), lax.axis_index("dp")
    chips = n // 2
    core, chip = lax.rem(me, 2), me // 2
    partner = {"field": me + 1 - 2 * core}
    other = lambda k: lax.rem(chip + k, chips)
    back = lambda k: lax.rem(chip + chips - k, chips)
    far = lambda k: {"field": other(k) * 2 + core}
    peer = lambda o: lax.rem(me + o, n)
    field_at = lambda o: {"field": peer(o)}
    dp_at = lambda o: {"dp": lax.rem(my + o, m)}

    barrier = pltpu.get_barrier_semaphore()
    for o in range(1, n):
        pl.semaphore_signal(barrier, 1, device_id=field_at(o), device_id_type=MESH)
    for o in range(1, m):
        pl.semaphore_signal(barrier, 1, device_id=dp_at(o), device_id_type=MESH)

    loads = []
    for i, (there, here) in enumerate(zip(r.outside, r.inside)):
        loads.append(pltpu.make_async_copy(there, here, r.load_sems.at[i]))
        loads[-1].start()
    for load in loads:
        load.wait()

    lanes, count = {}, 0
    for name, slots in lane_slots(n, W):
        lanes[name] = Lane(r.sems, count, partner)
        count += 1 + slots
    q = types.SimpleNamespace(**lanes)

    r.inproj, r.outproj, r.expand, r.shrink, r.vector, r.embed, r.position, r.tok, r.head, r.tgi = r.inside
    masters = (r.inproj, r.outproj, r.expand, r.shrink)
    for name, row, size, block in z.plan:
        r.wf[row : row + size, :] = masters[name][:, cut(block, 128)]
    r.wf[z.R : z.R + 16, :] = jnp.zeros((16, 128), F32)
    r.wf[z.R : z.R + 12, :] = mm(r.vector[...].astype(BF16), lane_pick(me, 128 // n).astype(BF16))
    r.ws[...] = r.wf[...].astype(BF16)
    for f in range(F):
        r.tab[f, bins - 4 :, :] = jnp.zeros((132 - bins, 128), F32)
        r.tab[f, 0:bins, :] = r.embed[pl.ds(f, bins, stride=F), :]
        r.tab[f, bins : bins + S, :] = r.position[pl.ds(f, S, stride=F), :]
        r.hf[f, bins - 4 :, :] = jnp.zeros((BAND + 4 - bins, 128), F32)
        r.hf[f, 0:bins, :] = r.head[pl.ds(f, bins, stride=F), :]
        r.hs[cut(f, BAND), :] = r.hf[f].astype(BF16)

    row = lax.broadcasted_iota(jnp.int32, (128, S * G), 0)
    step_row = lax.broadcasted_iota(jnp.int32, (1, S * G), 1) // G + bins
    for s in range(S):
        r.row[:, cut(s, G)] = r.tok[s]
        r.trow[:, cut(s, G)] = r.tgi[s]
    for f in range(F):
        hot = ((row == r.row[f : f + 1, :]) | (row == step_row)).astype(F32).astype(BF16)
        r.hot[f] = hot
        made = mm_tn(hot, r.tab[f].astype(BF16))
        for s in range(S):
            for d in range(n):
                at = s * G + d * W
                r.xsf[pl.ds(d * W * CH + s * F + f, W, stride=CH), :] = made[at : at + W]
    if S * F < CH:
        for g in range(G):
            r.xsf[g * CH + S * F : (g + 1) * CH, :] = jnp.zeros((CH - S * F, 128), F32)
    for d in range(n):
        for w in range(W):
            r.xs[d, w] = r.xsf[cut(d * W + w, CH), :].astype(BF16)

    pl.semaphore_wait(barrier, n - 1 + m - 1)

    q.w.start(r.ws, r.wr.at[me], partner, 0)
    for k in range(1, chips):
        q.w.start(r.ws, r.wr.at[me], far(k), k)
    for w in range(W):
        for o in range(1, n):
            q.x.start(r.xs.at[peer(o), w], r.xr.at[w, me], field_at(o), w)
    r.wr[me] = r.ws[...]
    for w in range(W):
        r.xr[w, me] = r.xs[me, w]

    own = lax.broadcasted_iota(jnp.int32, (fields, S * G), 1) % G // W
    mine = own == lax.broadcasted_iota(jnp.int32, (fields, S * G), 0) // F
    spread = jnp.concatenate([r.trow[...].astype(F32)] * n, axis=0)
    spread = jnp.where(mine, spread, 0.0).astype(BF16)
    source = lax.broadcasted_iota(jnp.int32, (S * G, 128), 0)
    place = lax.broadcasted_iota(jnp.int32, (S * G, 128), 1)
    move = (source // G * W + source % W == place).astype(F32).astype(BF16)
    target_rows = mm(spread, move)
    for i in range(fields):
        r.tgs[i] = target_rows[i : i + 1]
    there = pl.ds(me * F, F)
    for o in range(1, n):
        q.t.start(r.tgs.at[pl.ds(peer(o) * F, F)], r.tgt.at[there], field_at(o))
    mine = pl.ds(pl.multiple_of(me * FB, 16), FB)
    q.h.start(r.hs, r.hr.at[mine], partner, 0)
    for k in range(1, chips):
        q.h.start(r.hs, r.hr.at[mine], far(k), k)
    for f in range(F):
        r.tgt[me * F + f] = r.tgs[me * F + f]
    r.hr[mine, :] = r.hs[...]

    for k in range(1, chips):
        q.w.arrived(r.ws, k)
        slot = r.wr.at[back(k) * 2 + core]
        q.wf.start(slot, slot, partner)
    q.w.arrived(r.ws, 0)
    q.wf.arrived(r.wr.at[pl.ds(0, chips - 1)])
    full = (r.w_in, r.w_out, r.w_up, r.w_down)
    wide = (r.g_in, r.g_out, r.g_up, r.g_down)
    vec = jnp.zeros((16, 128), F32)
    for i in range(n):
        shard = r.wr[i].astype(F32)
        vec = vec + shard[z.R :]
        for name, row, size, block in z.plan:
            to = full if size % 16 == 0 else wide
            piece = shard[row : row + size]
            to[name][cut(i, size), cut(block, 128)] = piece.astype(to[name].dtype)
    for name, row, size, block in z.plan:
        if size % 16:
            full[name][:, cut(block, 128)] = wide[name][:, cut(block, 128)].astype(BF16)
    r.vec[...] = vec
    r.g_vec[...] = jnp.zeros((16, 128), F32)

    def take(w):
        q.x.arrived(r.xr.at[w, pl.ds(0, n - 1)], w)
        for i in range(n):
            r.xf[cut(w * n + i, CH), :] = r.xr[w, i].astype(F32)
        for s in range(S):
            for f in range(F):
                got = r.xf[pl.ds(w * n * CH + s * F + f, n, stride=CH), :]
                r.x[pl.ds(w * 320 + s * fields + f, n, stride=F), :] = got

    weave([forward_window(w, r, take) for w in range(W)], SKEW_F)

    q.t.arrived(r.tgs.at[pl.ds(0, (n - 1) * F)])
    lane = lax.broadcasted_iota(jnp.int32, (1, T), 1)
    live = jnp.zeros((1, T), F32)
    for w in range(W):
        inside = (lane // W).astype(F32) < r.valid[me * W + w].astype(F32)
        live = jnp.where(inside & (lane % W == w), 1.0, live)
    r.loss[...] = jnp.zeros_like(r.loss)
    for k in range(1, chips):
        q.h.arrived(r.hs, k)
        slot = r.hr.at[pl.ds(pl.multiple_of((back(k) * 2 + core) * FB, 16), FB)]
        q.hf.start(slot, slot, partner)

    def keeper(ref, c, f):
        def keep(v):
            ref[c, cut(f, BAND), :] = v.astype(ref.dtype)

        return keep

    def heads(which, ref):
        gens = []
        for k in range(chips):
            c = other(k)
            for f in range(F):
                gens.append(head_field((c * 2 + which) * F + f, live, keeper(ref, c, f), r))
        weave(gens, SKEW_H)

    heads(core, r.gho)
    q.h.arrived(r.hs, 0)
    q.hf.arrived(r.hr.at[pl.ds(0, (chips - 1) * FB)])
    heads(1 - core, r.ghp)
    q.gp.start(r.ghp, r.ghq, partner)

    def send_losses():
        GL = r.lss.shape[-1]
        row = lax.broadcasted_iota(jnp.int32, (128, GL), 0)
        col = lax.broadcasted_iota(jnp.int32, (128, GL), 1)
        group = ((row < T) & (col == me * W + row % W)).astype(F32)
        sums = jnp.dot(r.loss[...], group, preferred_element_type=F32, precision=lax.Precision.HIGHEST)
        for f in range(fields):
            r.lss[f] = sums[f : f + 1, :]
        for o in range(1, n):
            q.ls.start(r.lss.at[pl.ds(peer(o) * F, F)], r.lsr.at[me], field_at(o))
        r.lsr[me] = r.lss[there]

    def give(w):
        for s in range(S):
            for f in range(F):
                got = r.dx[pl.ds(w * 320 + s * fields + f, n, stride=F), :]
                r.dxf[pl.ds(w * n * CH + s * F + f, n, stride=CH), :] = got
        for i in range(n):
            if S * F < CH:
                r.dxf[(w * n + i) * CH + S * F : (w * n + i + 1) * CH, :] = jnp.zeros((CH - S * F, 128), F32)
            r.dxs[w, i] = r.dxf[cut(w * n + i, CH), :].astype(BF16)
        for o in range(1, n):
            q.dx.start(r.dxs.at[w, peer(o)], r.dxr.at[me, w], field_at(o))
        r.dxr[me, w] = r.dxs[w, me]

    def pair_heads():
        q.gp.arrived(r.ghp)
        for c in range(chips):
            total = r.gho[c] + r.ghq[c].astype(F32)
            for j in range(m):
                r.gzs[j, c] = total[cut(j, HQ)].astype(BF16)
        for o in range(1, m):
            q.gz.start(r.gzs.at[lax.rem(my + o, m)], r.gzr.at[my], dp_at(o))
        r.gzr[my] = r.gzs[my]
        send_losses()

    def plane_heads():
        q.gz.arrived(r.gzr.at[pl.ds(0, m - 1)])
        for c in range(chips):
            total = r.gzr[0, c].astype(F32)
            for j in range(1, m):
                total = total + r.gzr[j, c].astype(F32)
            r.ghs[c] = total.astype(BF16)
        for k in range(1, chips):
            q.gh.start(r.ghs.at[other(k)], r.ghr.at[chip], far(k))
        r.ghr[chip] = r.ghs[chip]

    def share_heads():
        q.gh.arrived(r.ghr.at[pl.ds(0, chips - 1)])
        r.a2s[...] = total_of(r.ghr, chips).astype(BF16)
        for o in range(1, m):
            q.a2.start(r.a2s, r.a2r.at[my], dp_at(o))
        r.a2r[my] = r.a2s[...]

    grads = (r.g_in, r.g_out, r.g_up, r.g_down)

    def send_grads(plan, f32_ref, send, recv, lane):
        for i in range(n):
            for name, row, size, block in plan:
                f32_ref[row : row + size, :] = grads[name][cut(i, size), cut(block, 128)]
            send[i] = f32_ref[...].astype(BF16)
        for o in range(1, n):
            lane.start(send.at[peer(o)], recv.at[me], field_at(o))
        recv[me] = send[me]

    def send_early():
        r.g_up[...] = mm_tn(r.n2[...], r.du[...])
        r.g_down[...] = mm_tn(r.dyb[...], r.a[...]).T
        send_grads(z.early, r.gef, r.ges, r.ger, q.ge)

    def total_of(ref, count):
        total = ref[0].astype(F32)
        for i in range(1, count):
            total = total + ref[i].astype(F32)
        return total

    def dp_first(total, send, recv, lane):
        C = send.shape[1]
        for i in range(m):
            send[i] = total[cut(i, C), :].astype(BF16)
        for o in range(1, m):
            lane.start(send.at[lax.rem(my + o, m)], recv.at[my], dp_at(o))
        recv[my] = send[my]

    def dp_second(recv, lane, last, out, last_lane):
        lane.arrived(recv.at[pl.ds(0, m - 1)])
        last[...] = total_of(recv, m).astype(BF16)
        for o in range(1, m):
            last_lane.start(last, out.at[my], dp_at(o))
        out[my] = last[...]

    hooks = {PAIR: pair_heads, EARLY: send_early}
    weave([backward_window(w, r, give) for w in range(W)], SKEW_B, hooks)

    r.glf[z.RL :, :] = r.g_vec[...]
    r.g_out[...] = mm_tn(r.o[...], r.db[...])
    r.g_in[...] = mm_tn(r.n1[...], r.dm[...])
    send_grads(z.late, r.glf, r.gls, r.glr, q.gl)
    plane_heads()
    q.ge.arrived(r.ger.at[pl.ds(0, n - 1)])
    r.sumb[FB : FB + z.RE, :] = total_of(r.ger, n)
    q.dx.arrived(r.dxr.at[pl.ds(0, n - 1)])
    for g in range(G):
        r.dxw[cut(g, CH), :] = r.dxr[g // W, g % W].astype(F32)
    for f in range(F):
        rows = [r.dxw[pl.ds(s * F + f, G, stride=CH), :] for s in range(S)]
        total = mm(r.hot[f], jnp.concatenate(rows, axis=0).astype(BF16))
        r.sumb[pl.ds(f, BAND, stride=F), :] = total[:BAND]
    q.gl.arrived(r.glr.at[pl.ds(0, n - 1)])
    base, late_rows = FB + z.RE, z.RL + 16
    r.sumb[base : base + late_rows, :] = total_of(r.glr, n)
    if m * z.CB > base + late_rows:
        r.sumb[base + late_rows :, :] = jnp.zeros((m * z.CB - base - late_rows, 128), F32)
    dp_first(r.sumb, r.b1s, r.b1r, q.b1)
    share_heads()

    q.w.left(r.wr.at[pl.ds(0, chips)])
    q.wf.left(r.wr.at[pl.ds(0, chips - 1)])
    q.x.left(r.xr.at[:, pl.ds(0, n - 1)])
    q.t.left(r.tgs.at[pl.ds(0, (n - 1) * F)])
    q.h.left(r.hr.at[pl.ds(0, chips * FB)])
    q.hf.left(r.hr.at[pl.ds(0, (chips - 1) * FB)])
    q.gp.left(r.ghp)
    q.gh.left(r.ghr.at[pl.ds(0, chips - 1)])
    q.ls.left(r.lsr.at[pl.ds(0, n - 1)])
    q.ls.arrived(r.lsr.at[pl.ds(0, n - 1)])
    q.ge.left(r.ger.at[pl.ds(0, n - 1)])
    q.dx.left(r.dxr.at[pl.ds(0, n - 1)])
    q.gl.left(r.glr.at[pl.ds(0, n - 1)])
    q.gz.left(r.gzr.at[pl.ds(0, m - 1)])
    dp_second(r.b1r, q.b1, r.b2s, r.b2r, q.b2)
    q.a2.left(r.a2r.at[pl.ds(0, m - 1)])
    q.a2.arrived(r.a2r.at[pl.ds(0, m - 1)])
    q.b1.left(r.b1r.at[pl.ds(0, m - 1)])
    q.b2.left(r.b2r.at[pl.ds(0, m - 1)])
    q.b2.arrived(r.b2r.at[pl.ds(0, m - 1)])


def lane_slots(n, W):
    slots = dict(w=n // 2, wf=1, x=W, t=1, h=n // 2, hf=1, gp=1, gh=1, ls=1, ge=1, dx=1, gl=1, gz=1, a2=1, b1=1, b2=1)
    return list(slots.items())


SKEW_F, SKEW_H, SKEW_B, PAIR, EARLY = 4, 0, 0, 3, 9


def step_call(cfg, valid, ins):
    n, m, F, W, S, bins = cfg
    z = layout(cfg)
    CH, L, G, fields, chips, BAND, HQ = z.CH, W * 320, n * W, n * F, n // 2, z.BAND, z.HQ
    FB = F * BAND
    GL = max(G, 128)
    A = jax.ShapeDtypeStruct
    V = pltpu.VMEM
    D = pltpu.SemaphoreType.DMA
    outs = dict(
        dxr=A((n, W, CH, 128), BF16),
        a2r=A((m, HQ, 128), BF16),
        b2r=A((m, z.CB, 128), BF16),
        lsr=A((n, F, 1, GL), F32),
    )
    scr = dict(
        wf=V((z.R + 16, 128), F32),
        ws=V((z.R + 16, 128), BF16),
        wr=V((n, z.R + 16, 128), BF16),
        tab=V((F, 128, 128), F32),
        hf=V((F, BAND, 128), F32),
        hs=V((FB, 128), BF16),
        hr=V((fields * BAND, 128), BF16),
        row=V((F, S * G), jnp.int32),
        trow=V((F, S * G), jnp.int32),
        hot=V((F, 128, S * G), BF16),
        rows_out=V((G * CH, 128), F32),
        rows_in=V((G * CH, 128), F32),
        xs=V((n, W, CH, 128), BF16),
        xr=V((W, n, CH, 128), BF16),
        tgs=V((fields, 1, 128), F32),
        tgt=V((fields, 1, 128), F32),
        w_in=V((128, 384), BF16),
        w_out=V((128, 128), BF16),
        w_up=V((128, 512), BF16),
        w_down=V((512, 128), BF16),
        vec=V((16, 128), F32),
        x=V((L, 128), F32),
        unit1=V((L, 128), F32),
        inv1=V((L, 128), F32),
        unit2=V((L, 128), F32),
        inv2=V((L, 128), F32),
        n1=V((L, 128), BF16),
        n2=V((L, 128), BF16),
        qm=V((W, 1280, 128), BF16),
        k=V((L, 128), BF16),
        v=V((L, 128), BF16),
        o=V((L, 128), BF16),
        pa=V((W, HEADS, 128, 256), F32),
        pd=V((W, HEADS, 128, 128), F32),
        pb=V((W, 320, 256), F32),
        a=V((L, 512), BF16),
        slope=V((L, 512), F32),
        y=V((L, 128), F32),
        dy=V((L, 128), F32),
        du=V((L, 512), BF16),
        dyb=V((L, 128), BF16),
        db=V((L, 128), BF16),
        dm=V((L, 384), BF16),
        dxs=V((W, n, CH, 128), BF16),
        loss=V((fields, 128), F32),
        lss=V((fields, 1, GL), F32),
        gho=V((chips, FB, 128), F32),
        ghp=V((chips, FB, 128), BF16),
        ghq=V((chips, FB, 128), BF16),
        gzs=V((m, chips, HQ, 128), BF16),
        gzr=V((m, chips, HQ, 128), BF16),
        ghs=V((chips, HQ, 128), BF16),
        ghr=V((chips, HQ, 128), BF16),
        g_in=V((128, 384), F32),
        g_out=V((128, 128), F32),
        g_up=V((128, 512), F32),
        g_down=V((512, 128), F32),
        g_vec=V((16, 128), F32),
        gef=V((z.RE, 128), F32),
        ges=V((n, z.RE, 128), BF16),
        ger=V((n, z.RE, 128), BF16),
        glf=V((z.RL + 16, 128), F32),
        gls=V((n, z.RL + 16, 128), BF16),
        glr=V((n, z.RL + 16, 128), BF16),
        a2s=V((HQ, 128), BF16),
        sumb=V((m * z.CB, 128), F32),
        b1s=V((m, z.CB, 128), BF16),
        b1r=V((m, z.CB, 128), BF16),
        b2s=V((z.CB, 128), BF16),
        sems=D((sum(1 + slots for name, slots in lane_slots(n, W)),)),
    )
    names = list(outs) + list(scr)
    vm = pl.BlockSpec(memory_space=pltpu.VMEM)
    inside = [V(v.shape, v.dtype) for v in ins]
    res = pl.pallas_call(
        functools.partial(step_kernel, cfg, names, len(ins)),
        out_shape=list(outs.values()),
        in_specs=[pl.BlockSpec(memory_space=pltpu.SMEM)] + [pl.BlockSpec(memory_space=pl.ANY)] * len(ins),
        out_specs=[vm] * len(outs),
        scratch_shapes=list(scr.values()) + inside + [D((len(ins),))],
        compiler_params=pltpu.CompilerParams(vmem_limit_bytes=VMEM_ALL, collective_id=0, has_side_effects=True),
        name="step",
    )(valid, *ins)
    return types.SimpleNamespace(**dict(zip(outs, res)))


VMEM_ALL = 64 * 1024 * 1024 - 65536
RATES = (0.8, 0.6, 1.6 * 128 ** (-0.5), 128 ** (-0.5), 4 ** (-0.5), 128 ** (-0.5), 512 ** (-0.5), 0.3)
EMBED, POSITION, HEAD, BLOCK, VECTOR = 0, 1, 2, 3, 7


def adam_kernel(cfg, count_ref, dxr, a2r, b2r, lsr, *refs):
    n, m, F, W, S, bins = cfg
    z = layout(cfg)
    state, losses, input_grad, outs, (suma, sumb, sumc) = refs[:24], refs[24], refs[25], refs[26:58], refs[58:]
    me = lax.axis_index("field")
    half = lax.fori_loop(0, count_ref[0], lambda i, v: v * 0.5, jnp.float32(1.0))
    inv_c = 1.0 / (jnp.zeros((1, 128), F32) + (1.0 - half))

    for g in range(n * W):
        input_grad[cut(g, S * F), :] = dxr[g // W, g % W].astype(F32)[: S * F]
    for f in range(F):
        total = lsr[0, f]
        for i in range(1, n):
            total = total + lsr[i, f]
        losses[f : f + 1, :] = total[:, : n * W]

    def adam(weight, at, grad):
        c = inv_c[0:1, 0 : grad.shape[-1]]
        master = state[3 * weight][at]
        first = 0.5 * state[3 * weight + 1][at] + 0.5 * grad
        second = 0.5 * state[3 * weight + 2][at] + 0.5 * grad * grad
        new = master - RATES[weight] * (first * c / (jnp.sqrt(second * c) + 1e-08) + 0.1 * master)
        outs[4 * weight][at] = first
        outs[4 * weight + 1][at] = second
        outs[4 * weight + 2][at] = new
        outs[4 * weight + 3][at] = new.astype(BF16)

    BAND = z.BAND
    for i in range(m):
        sumb[cut(i, z.CB), :] = b2r[i].astype(F32)
        sumc[cut(i, z.HQ), :] = a2r[i].astype(F32)
    for f in range(F):
        suma[pl.ds(f, BAND, stride=F), :] = sumc[cut(f, BAND), :]
    every = slice(None)
    base, tokens = F * BAND, F * bins
    adam(HEAD, (every, every), suma[0:tokens, :])
    adam(EMBED, (every, every), sumb[0:tokens, :])
    adam(POSITION, (every, every), sumb[tokens : tokens + S * F, :])
    for plan, first in ((z.early, base), (z.late, base + z.RE)):
        for name, row, size, block in plan:
            adam(BLOCK + name, (every, cut(block, 128)), sumb[first + row : first + row + size, :])
    vecs = sumb[base + z.RE + z.RL : base + z.RE + z.RL + 16, :]
    pick = lane_pick(me, 128 // n).astype(F32)
    mine = lax.dot_general(
        vecs, pick, (((1,), (1,)), ((), ())), preferred_element_type=F32, precision=lax.Precision.HIGHEST
    )
    adam(VECTOR, (every, every), mine[0:12])


def adam_call(cfg, count, got, state):
    n, m, F, W, S, bins = cfg
    z = layout(cfg)
    A = jax.ShapeDtypeStruct
    outs = [A((F, n * W), F32), A((n * W * S * F, 128), F32)]
    for i in range(8):
        shape = state[3 * i].shape
        outs.extend([A(shape, F32)] * 3 + [A(shape, BF16)])
    vm = pl.BlockSpec(memory_space=pltpu.VMEM)
    sm = pl.BlockSpec(memory_space=pltpu.SMEM)
    return pl.pallas_call(
        functools.partial(adam_kernel, cfg),
        out_shape=outs,
        in_specs=[sm] + [vm] * 28,
        out_specs=[vm] * len(outs),
        scratch_shapes=[pltpu.VMEM((size, 128), F32) for size in (F * z.BAND, m * z.CB, F * z.BAND)],
        compiler_params=pltpu.CompilerParams(vmem_limit_bytes=VMEM_ALL),
        name="adam",
    )(count, got.dxr, got.a2r, got.b2r, got.lsr, *state)


def local(n, m, bin_tokens, targets, valid_steps, step_count, *state):
    windows, S, F = bin_tokens.shape
    bins = state[0].shape[1]
    cfg = (n, m, F, windows // n, S, bins)
    by_bin = lambda v: v.transpose(1, 0, 2).reshape(bins * F, 128)
    by_class = lambda v: v.transpose(2, 0, 1).reshape(bins * F, 128)
    flat = [by_bin(v) for v in state[0:3]] + [v.reshape(S * F, 128) for v in state[3:6]]
    flat += [by_class(v) for v in state[6:9]] + list(state[9:])
    blocks = [flat[i] for i in (9, 12, 15, 18, 21, 0, 3)]
    ins = [*blocks, bin_tokens.transpose(1, 2, 0), flat[6], targets.transpose(1, 2, 0)]
    got = step_call(cfg, valid_steps, ins)
    losses, input_grad, *new = adam_call(cfg, step_count.reshape(1), got, flat)
    new[0:4] = [v.reshape(bins, F, 128).transpose(1, 0, 2) for v in new[0:4]]
    new[4:8] = [v.reshape(S, F, 128) for v in new[4:8]]
    new[8:12] = [v.reshape(bins, F, 128).transpose(1, 2, 0) for v in new[8:12]]
    return (losses.transpose(1, 0), input_grad.reshape(windows, S, F, 128), *new)


def solution(mesh):
    n, m = mesh.shape["field"], mesh.shape["dp"]
    stack, rows, cols = P("field", None, None), P("field", None), P(None, "field")
    by_weight = (stack, P(None, "field", None), stack, rows, rows, rows, rows, cols)
    in_specs = [P("dp", None, "field"), P("dp", None, "field"), P("dp"), P()]
    out_specs = [P("dp", "field"), P("dp", None, "field", None)]
    for spec in by_weight:
        in_specs.extend([spec] * 3)
        out_specs.extend([spec] * 4)
    return jax.shard_map(
        functools.partial(local, n, m),
        mesh=mesh,
        in_specs=tuple(in_specs),
        out_specs=tuple(out_specs),
        check_vma=False,
    )
```

```python
import functools
import types
import jax
import jax.numpy as jnp
from jax import lax
from jax.experimental import pallas as pl
from jax.experimental.pallas import tpu as pltpu
from jax.sharding import PartitionSpec as P

F32 = jnp.float32
BF16 = jnp.bfloat16
HEADS = 4
NEG = -1e30


def mm(a, b):
    return jnp.dot(a, b, preferred_element_type=F32)


def mm_nt(a, b):
    return lax.dot_general(a, b, (((1,), (1,)), ((), ())), preferred_element_type=F32)


def mm_tn(a, b):
    return lax.dot_general(a, b, (((0,), (0,)), ((), ())), preferred_element_type=F32)


def head_lanes(shape, head):
    lane = lax.broadcasted_iota(jnp.int32, shape, 1)
    return (lane >= head * 32) & (lane < (head + 1) * 32)


def spread_heads(value):
    parts = []
    for head in range(HEADS):
        parts.append(jnp.where(head_lanes((256, 128), head), value[:256], 0.0))
    for head in range(HEADS):
        parts.append(jnp.where(head_lanes((64, 128), head), value[256:], 0.0))
    return jnp.concatenate(parts, axis=0).astype(BF16)


def join_heads(tall):
    out = tall[0:64]
    for head in range(1, HEADS):
        out = jnp.where(head_lanes((64, 128), head), tall[head * 64 : (head + 1) * 64], out)
    return out


def norm_stats(v):
    mean = jnp.mean(v, axis=-1, keepdims=True)
    c = v - mean
    spread = jnp.mean(c * c, axis=-1, keepdims=True)
    inv = lax.rsqrt(spread + 1e-05)
    return c * inv, jnp.broadcast_to(inv, v.shape)


def norm_back(grad, gain, unit, inv):
    e = grad * gain
    m1 = jnp.mean(e, axis=-1, keepdims=True)
    m2 = jnp.mean(e * unit, axis=-1, keepdims=True)
    return inv * (e - m1 - unit * m2)


SCALE = 32 ** (-0.5)
LOG2E = 1.4426950408889634


def causal_square(n):
    k = lax.broadcasted_iota(jnp.int32, (n, n), 0)
    q = lax.broadcasted_iota(jnp.int32, (n, n), 1)
    return k <= q


def soft_cols(pieces):
    peak = functools.reduce(jnp.maximum, [jnp.max(p, axis=0, keepdims=True) for p in pieces])
    shift = peak * (SCALE * LOG2E)
    es = [jnp.exp2(p * (SCALE * LOG2E) - shift) for p in pieces]
    total = functools.reduce(lambda a, b: a + b, [jnp.sum(e, axis=0, keepdims=True) for e in es])
    inv = 1.0 / total
    return [e * inv for e in es]


def forward_window(w, r, take):
    rows = pl.ds(w * 320, 320)
    vec = r.vec
    take(w)
    yield
    x = r.x[rows, :]
    unit, inv = norm_stats(x)
    r.unit1[rows, :] = unit
    r.inv1[rows, :] = inv
    n1 = (unit * vec[0:1, :] + vec[1:2, :]).astype(BF16)
    r.n1[rows, :] = n1
    yield
    mixed = mm(n1, r.w_in[...])
    q = mixed[:, 0:128] + vec[2:3, :]
    k = mixed[:, 128:256]
    v = mixed[:, 256:384] + vec[3:4, :]
    yield
    qm = spread_heads(q)
    kb = k.astype(BF16)
    vb = v.astype(BF16)
    r.qm[w] = qm
    r.k[rows, :] = kb
    r.v[rows, :] = vb
    vt = v.T.astype(BF16)
    yield
    mask128 = causal_square(128)
    ot_parts = []
    for head in range(HEADS):
        s = mm_nt(kb[0:256], qm[head * 256 : (head + 1) * 256])
        yield
        s00 = jnp.where(mask128, s[0:128, 0:128], NEG)
        (p00,) = soft_cols([s00])
        r.pa[w, head, 0:128, 0:128] = p00
        yield
        s11 = jnp.where(mask128, s[128:256, 128:256], NEG)
        p01, p11 = soft_cols([s[0:128, 128:256], s11])
        r.pa[w, head, 0:128, 128:256] = p01
        r.pd[w, head] = p11
        yield
        b11 = p11.astype(BF16)
        pb = jnp.concatenate(
            [
                jnp.concatenate([p00.astype(BF16), p01.astype(BF16)], axis=1),
                jnp.concatenate([jnp.zeros((128, 128), BF16), b11], axis=1),
            ],
            axis=0,
        )
        ot_parts.append(mm(vt[head * 32 : (head + 1) * 32, 0:256], pb))
        yield
    ot = jnp.concatenate(ot_parts, axis=0)
    sb = mm_nt(kb, qm[1024:1280])
    yield
    kk = lax.broadcasted_iota(jnp.int32, (64, 256), 0)
    qq = lax.broadcasted_iota(jnp.int32, (64, 256), 1) % 64
    pbs = []
    for half in range(2):
        cols = slice(half * 128, (half + 1) * 128)
        s_low = jnp.where((kk <= qq)[:, cols], sb[256:320, cols], NEG)
        p_top, p_low = soft_cols([sb[0:256, cols], s_low])
        r.pb[w, 0:256, cols] = p_top
        r.pb[w, 256:320, cols] = p_low
        pbs.append(jnp.concatenate([p_top.astype(BF16), p_low.astype(BF16)], axis=0))
        yield
    pbb = jnp.concatenate(pbs, axis=1)
    otb = mm(vt, pbb)
    yield
    o_tail = join_heads(otb.T)
    o = jnp.concatenate([ot.T, o_tail], axis=0).astype(BF16)
    r.o[rows, :] = o
    yield
    x1 = x + mm(o, r.w_out[...]) + vec[4:5, :]
    yield
    unit, inv = norm_stats(x1)
    r.unit2[rows, :] = unit
    r.inv2[rows, :] = inv
    n2 = (unit * vec[5:6, :] + vec[6:7, :]).astype(BF16)
    r.n2[rows, :] = n2
    yield
    y = x1 + vec[7:8, :]
    for part in range(2):
        cols = cut(part, 256)
        bias = jnp.concatenate([vec[8 + 2 * part : 9 + 2 * part, :], vec[9 + 2 * part : 10 + 2 * part, :]], axis=1)
        u = mm(n2, r.w_up[:, cols]) + bias
        yield
        phi = 0.5 * (1.0 + lax.erf(u * 0.7071067811865476))
        a = (u * phi).astype(BF16)
        r.a[rows, cols] = a
        r.slope[rows, cols] = phi + u * jnp.exp2(u * u * (-0.5 * LOG2E)) * 0.3989422804014327
        yield
        y = y + mm(a, r.w_down[cols, :])
        yield
    r.y[rows, :] = y.astype(BF16).astype(F32)


def head_field(f, live, keep, r):
    W, T = r.W, live.shape[1]
    starts = [pl.ds(step * 32 + f, W, stride=320) for step in range(T // W)]
    yf = jnp.concatenate([r.y[at, :] for at in starts], axis=0).astype(BF16)
    wt = r.hr[pl.ds(pl.multiple_of(f * r.band, 16), r.band), :]
    lt = mm_nt(wt, yf)
    yield
    bins = lax.broadcasted_iota(jnp.int32, lt.shape, 0)
    lt = jnp.where(bins < r.bins, lt, NEG)
    peak = jnp.max(lt, axis=0, keepdims=True)
    e = jnp.exp(lt - peak)
    yield
    total = jnp.sum(e, axis=0, keepdims=True)
    lse = peak + jnp.log(total)
    hot = bins.astype(F32) == r.tgt[f][:, :T]
    picked = jnp.sum(jnp.where(hot, lt, 0.0), axis=0, keepdims=True)
    r.loss[pl.ds(f, 1), 0:T] = (lse - picked) * live
    yield
    dl = (jnp.exp(lt - lse) - hot.astype(F32)) * live
    yield
    keep(mm(dl.astype(BF16), yf))
    yield
    dy = mm(dl.T.astype(BF16), wt)
    yield
    dy = dy.astype(BF16).astype(F32)
    for step, at in enumerate(starts):
        r.dy[at, :] = dy[step * W : (step + 1) * W]


def colsum(v):
    return jnp.sum(v, axis=0, keepdims=True)


def backward_window(w, r, give):
    rows = pl.ds(w * 320, 320)
    vec = r.vec
    gv = r.g_vec
    dy = r.dy[rows, :]
    dyb = dy.astype(BF16)
    gv[7:8, :] += colsum(dy)
    dn2 = jnp.zeros((320, 128), F32)
    r.dyb[rows, :] = dyb
    yield
    for part in range(2):
        cols = cut(part, 256)
        da = mm_nt(dyb, r.w_down[cols, :])
        du = (da * r.slope[rows, cols]).astype(BF16)
        bias = colsum(du.astype(F32))
        gv[8 + 2 * part : 9 + 2 * part, :] += bias[:, 0:128]
        gv[9 + 2 * part : 10 + 2 * part, :] += bias[:, 128:256]
        r.du[rows, cols] = du
        dn2 = dn2 + mm_nt(du, r.w_up[:, cols])
        yield
    unit = r.unit2[rows, :]
    gv[5:6, :] += colsum(dn2 * unit)
    gv[6:7, :] += colsum(dn2)
    dx1 = dy + norm_back(dn2, vec[5:6, :], unit, r.inv2[rows, :])
    yield
    db = dx1.astype(BF16)
    gv[4:5, :] += colsum(db.astype(F32))
    r.db[rows, :] = db
    do = mm_nt(db, r.w_out[...])
    yield
    dom = spread_heads(do)
    kb = r.k[rows, :]
    vb = r.v[rows, :]
    kt = kb.astype(F32).T.astype(BF16)
    dv = jnp.zeros((256, 128), F32)
    dk = jnp.zeros((256, 128), F32)
    dqt = []
    yield
    for head in range(HEADS):
        part = slice(head * 256, (head + 1) * 256)
        p00 = r.pa[w, head, 0:128, 0:128]
        p01 = r.pa[w, head, 0:128, 128:256]
        p11 = r.pd[w, head]
        dp = mm_nt(vb[0:256], dom[part])
        yield
        d0 = p00 * dp[0:128, 0:128]
        d1a = p01 * dp[0:128, 128:256]
        d1b = p11 * dp[128:256, 128:256]
        t0 = colsum(d0)
        t1 = colsum(d1a) + colsum(d1b)
        ds00 = (d0 - p00 * t0).astype(BF16)
        ds01 = (d1a - p01 * t1).astype(BF16)
        ds11 = (d1b - p11 * t1).astype(BF16)
        yield
        zero = jnp.zeros((128, 128), BF16)
        pb = jnp.concatenate(
            [
                jnp.concatenate([p00.astype(BF16), p01.astype(BF16)], axis=1),
                jnp.concatenate([zero, p11.astype(BF16)], axis=1),
            ],
            axis=0,
        )
        dsb = jnp.concatenate(
            [jnp.concatenate([ds00, ds01], axis=1), jnp.concatenate([zero, ds11], axis=1)], axis=0
        )
        dv = dv + mm(pb, dom[part])
        dk = dk + mm(dsb, r.qm[w, part, :])
        dqt.append(mm(kt[head * 32 : (head + 1) * 32, 0:256], dsb))
        yield
    pt = r.pb[w]
    dp = mm_nt(vb, dom[1024:1280])
    yield
    d = pt * dp
    dsb = (d - pt * colsum(d)).astype(BF16)
    yield
    dvb = mm(pt.astype(BF16), dom[1024:1280])
    dkb = mm(dsb, r.qm[w, 1024:1280, :])
    yield
    dq_tail = join_heads(mm(kt, dsb).T)
    dq = jnp.concatenate([jnp.concatenate(dqt, axis=0).T, dq_tail], axis=0) * SCALE
    dv = jnp.concatenate([dv + dvb[0:256], dvb[256:320]], axis=0)
    dk = jnp.concatenate([dk + dkb[0:256], dkb[256:320]], axis=0) * SCALE
    dq = dq.astype(BF16)
    dk = dk.astype(BF16)
    dv = dv.astype(BF16)
    yield
    gv[2:3, :] += colsum(dq.astype(F32))
    gv[3:4, :] += colsum(dv.astype(F32))
    dm = jnp.concatenate([dq, dk, dv], axis=1)
    r.dm[rows, :] = dm
    dn1 = mm_nt(dm, r.w_in[...])
    yield
    unit = r.unit1[rows, :]
    gv[0:1, :] += colsum(dn1 * unit)
    gv[1:2, :] += colsum(dn1)
    dx = dx1 + norm_back(dn1, vec[0:1, :], unit, r.inv1[rows, :])
    r.dx[rows, :] = dx
    yield
    give(w)


def weave(gens, delays, hooks=()):
    live = [[g, wait] for g, wait in zip(gens, delays)]
    hooks = dict(hooks)
    turn = 0
    while live:
        if turn in hooks:
            hooks.pop(turn)()
        for item in list(live):
            if item[1] > 0:
                item[1] -= 1
                continue
            try:
                next(item[0])
            except StopIteration:
                live.remove(item)
        turn += 1
    for left in sorted(hooks):
        hooks[left]()


MESH = pl.DeviceIdType.MESH


def plan_rows(n, parts):
    plan, row = [], 0
    for name in parts:
        total, blocks = ((128, 3), (128, 1), (128, 4), (512, 1))[name]
        size = total // n
        for block in range(blocks):
            plan.append((name, row, size, block))
            row += size
    return plan, -(-row // 16) * 16


class Lane:
    def __init__(self, sems, first, anyone):
        self.sems, self.first, self.anyone = sems, first, anyone

    def copy(self, src, dst, slot, target):
        return pltpu.make_async_remote_copy(
            src_ref=src,
            dst_ref=dst,
            send_sem=self.sems.at[self.first],
            recv_sem=self.sems.at[self.first + 1 + slot],
            device_id=target,
            device_id_type=MESH,
        )

    def start(self, src, dst, target, slot=0):
        self.copy(src, dst, slot, target).start()

    def arrived(self, like, slot=0):
        self.copy(like, like, slot, self.anyone).wait_recv()

    def left(self, like):
        self.copy(like, like, 0, self.anyone).wait_send()


def lane_pick(me, width):
    row = lax.broadcasted_iota(jnp.int32, (width, 128), 0)
    lane = lax.broadcasted_iota(jnp.int32, (width, 128), 1)
    return lane == row + me * width


def cut(i, size):
    return slice(i * size, (i + 1) * size)


def layout(cfg):
    n, m, F, W, S, bins = cfg
    CH = -(-S * F // 8) * 8
    BAND = 112 if F * 112 % (8 * m) == 0 else 128
    plan, R = plan_rows(n, (0, 1, 2, 3))
    RR = R + 16
    CB = F * BAND // m
    CC = -(-RR // (16 * m)) * 16
    HQ = F * BAND // m
    return types.SimpleNamespace(CH=CH, BAND=BAND, plan=plan, R=R, RR=RR, CB=CB, CC=CC, HQ=HQ)


def step_kernel(cfg, names, count, valid, *refs):
    r = types.SimpleNamespace(**dict(zip(names, refs[count:])))
    r.valid, r.outside, r.inside, r.load_sems = valid, refs[:count], refs[-1 - count : -1], refs[-1]
    n, m, F, W, S, bins = cfg
    z = layout(cfg)
    CH, T, G, fields, BAND, HQ = z.CH, S * W, n * W, n * F, z.BAND, z.HQ
    FB = F * BAND
    r.bins, r.W, r.band = bins, W, BAND
    r.xsf = r.dxf = r.rows_out
    r.xf = r.dxw = r.rows_in
    r.dx = r.y
    me, my = lax.axis_index("field"), lax.axis_index("dp")
    chips = n // 2
    core, chip = lax.rem(me, 2), me // 2
    partner = {"field": me + 1 - 2 * core}
    other = lambda k: lax.rem(chip + k, chips)
    back = lambda k: lax.rem(chip + chips - k, chips)
    far = lambda k: {"field": other(k) * 2 + core}
    peer = lambda o: lax.rem(me + o, n)
    field_at = lambda o: {"field": peer(o)}
    dp_at = lambda o: {"dp": lax.rem(my + o, m)}

    barrier = pltpu.get_barrier_semaphore()
    for o in range(1, n):
        pl.semaphore_signal(barrier, 1, device_id=field_at(o), device_id_type=MESH)
    for o in range(1, m):
        pl.semaphore_signal(barrier, 1, device_id=dp_at(o), device_id_type=MESH)

    loads = []
    for i, (there, here) in enumerate(zip(r.outside, r.inside)):
        loads.append(pltpu.make_async_copy(there, here, r.load_sems.at[i]))
        loads[-1].start()
    for load in loads:
        load.wait()

    lanes, count = {}, 0
    for name, slots in lane_slots(n, W):
        lanes[name] = Lane(r.sems, count, partner)
        count += 1 + slots
    q = types.SimpleNamespace(**lanes)

    r.inproj, r.outproj, r.expand, r.shrink, r.vector, r.embed, r.position, r.tok, r.head, r.tgi = r.inside
    masters = (r.inproj, r.outproj, r.expand, r.shrink)
    for name, row, size, block in z.plan:
        r.wf[row : row + size, :] = masters[name][:, cut(block, 128)]
    r.wf[z.R : z.R + 16, :] = jnp.zeros((16, 128), F32)
    r.wf[z.R : z.R + 12, :] = mm(r.vector[...].astype(BF16), lane_pick(me, 128 // n).astype(BF16))
    r.ws[...] = r.wf[...].astype(BF16)
    for f in range(F):
        r.tab[f, bins - 4 :, :] = jnp.zeros((132 - bins, 128), F32)
        r.tab[f, 0:bins, :] = r.embed[pl.ds(f, bins, stride=F), :]
        r.tab[f, bins : bins + S, :] = r.position[pl.ds(f, S, stride=F), :]
        r.hf[f, bins - 4 :, :] = jnp.zeros((BAND + 4 - bins, 128), F32)
        r.hf[f, 0:bins, :] = r.head[pl.ds(f, bins, stride=F), :]
        r.hs[cut(f, BAND), :] = r.hf[f].astype(BF16)

    row = lax.broadcasted_iota(jnp.int32, (128, S * G), 0)
    step_row = lax.broadcasted_iota(jnp.int32, (1, S * G), 1) // G + bins
    for s in range(S):
        r.row[:, cut(s, G)] = r.tok[s]
        r.trow[:, cut(s, G)] = r.tgi[s]
    for f in range(F):
        hot = ((row == r.row[f : f + 1, :]) | (row == step_row)).astype(F32).astype(BF16)
        r.hot[f] = hot
        made = mm_tn(hot, r.tab[f].astype(BF16))
        for s in range(S):
            for d in range(n):
                at = s * G + d * W
                r.xsf[pl.ds(d * W * CH + s * F + f, W, stride=CH), :] = made[at : at + W]
    if S * F < CH:
        for g in range(G):
            r.xsf[g * CH + S * F : (g + 1) * CH, :] = jnp.zeros((CH - S * F, 128), F32)
    for d in range(n):
        for w in range(W):
            r.xs[d, w] = r.xsf[cut(d * W + w, CH), :].astype(BF16)

    pl.semaphore_wait(barrier, n - 1 + m - 1)

    q.w.start(r.ws, r.wr.at[me], partner, 0)
    for k in range(1, chips):
        q.w.start(r.ws, r.wr.at[me], far(k), k)
    for w in range(W):
        for o in range(1, n):
            q.x.start(r.xs.at[peer(o), w], r.xr.at[w, me], field_at(o), w)
    r.wr[me] = r.ws[...]
    for w in range(W):
        r.xr[w, me] = r.xs[me, w]

    own = lax.broadcasted_iota(jnp.int32, (fields, S * G), 1) % G // W
    mine = own == lax.broadcasted_iota(jnp.int32, (fields, S * G), 0) // F
    spread = jnp.concatenate([r.trow[...].astype(F32)] * n, axis=0)
    spread = jnp.where(mine, spread, 0.0).astype(BF16)
    source = lax.broadcasted_iota(jnp.int32, (S * G, 128), 0)
    place = lax.broadcasted_iota(jnp.int32, (S * G, 128), 1)
    move = (source // G * W + source % W == place).astype(F32).astype(BF16)
    target_rows = mm(spread, move)
    for i in range(fields):
        r.tgs[i] = target_rows[i : i + 1]
    there = pl.ds(me * F, F)
    for o in range(1, n):
        q.t.start(r.tgs.at[pl.ds(peer(o) * F, F)], r.tgt.at[there], field_at(o))
    mine = pl.ds(pl.multiple_of(me * FB, 16), FB)
    q.h.start(r.hs, r.hr.at[mine], partner, 0)
    for k in range(1, chips):
        q.h.start(r.hs, r.hr.at[mine], far(k), k)
    for f in range(F):
        r.tgt[me * F + f] = r.tgs[me * F + f]
    r.hr[mine, :] = r.hs[...]

    for k in range(1, chips):
        q.w.arrived(r.ws, k)
        slot = r.wr.at[back(k) * 2 + core]
        q.wf.start(slot, slot, partner)
    q.w.arrived(r.ws, 0)
    q.wf.arrived(r.wr.at[pl.ds(0, chips - 1)])
    full = (r.w_in, r.w_out, r.w_up, r.w_down)
    wide = (r.g_in, r.g_out, r.g_up, r.g_down)
    vec = jnp.zeros((16, 128), F32)
    for i in range(n):
        shard = r.wr[i].astype(F32)
        vec = vec + shard[z.R :]
        for name, row, size, block in z.plan:
            to = full if size % 16 == 0 else wide
            piece = shard[row : row + size]
            to[name][cut(i, size), cut(block, 128)] = piece.astype(to[name].dtype)
    for name, row, size, block in z.plan:
        if size % 16:
            full[name][:, cut(block, 128)] = wide[name][:, cut(block, 128)].astype(BF16)
    r.vec[...] = vec
    r.g_vec[...] = jnp.zeros((16, 128), F32)

    def take(w):
        q.x.arrived(r.xr.at[w, pl.ds(0, n - 1)], w)
        for i in range(n):
            r.xf[cut(w * n + i, CH), :] = r.xr[w, i].astype(F32)
        for s in range(S):
            for f in range(F):
                got = r.xf[pl.ds(w * n * CH + s * F + f, n, stride=CH), :]
                r.x[pl.ds(w * 320 + s * fields + f, n, stride=F), :] = got

    weave([forward_window(w, r, take) for w in range(W)], [FORWARD_LAG * w for w in range(W)])

    q.t.arrived(r.tgs.at[pl.ds(0, (n - 1) * F)])
    lane = lax.broadcasted_iota(jnp.int32, (1, T), 1)
    live = jnp.zeros((1, T), F32)
    for w in range(W):
        inside = (lane // W).astype(F32) < r.valid[me * W + w].astype(F32)
        live = jnp.where(inside & (lane % W == w), 1.0, live)
    r.loss[...] = jnp.zeros_like(r.loss)

    def keeper(ref, c, f):
        def keep(v):
            ref[c, cut(f, BAND), :] = v.astype(ref.dtype)

        return keep

    def heads(*places):
        gens = []
        for c, which, ref in places:
            gens.extend(head_field((c * 2 + which) * F + f, live, keeper(ref, c, f), r) for f in range(F))
        weave(gens, [0] * len(gens))

    for k in range(1, chips):
        q.h.arrived(r.hs, k)
        slot = r.hr.at[pl.ds(pl.multiple_of((back(k) * 2 + core) * FB, 16), FB)]
        q.hf.start(slot, slot, partner)
    heads(*[(other(k), core, r.gho) for k in range(chips)])
    q.h.arrived(r.hs, 0)
    q.hf.arrived(r.hr.at[pl.ds(0, (chips - 1) * FB)])
    heads(*[(other(k), 1 - core, r.ghp) for k in range(chips)])
    q.gp.start(r.ghp, r.ghq, partner)

    def send_losses():
        GL = r.lss.shape[-1]
        row = lax.broadcasted_iota(jnp.int32, (128, GL), 0)
        col = lax.broadcasted_iota(jnp.int32, (128, GL), 1)
        group = ((row < T) & (col == me * W + row % W)).astype(F32)
        sums = jnp.dot(r.loss[...], group, preferred_element_type=F32, precision=lax.Precision.HIGHEST)
        for f in range(fields):
            r.lss[f] = sums[f : f + 1, :]
        for o in range(1, n):
            q.ls.start(r.lss.at[pl.ds(peer(o) * F, F)], r.lsr.at[me], field_at(o))
        r.lsr[me] = r.lss[there]

    def give(w):
        for s in range(S):
            for f in range(F):
                got = r.dx[pl.ds(w * 320 + s * fields + f, n, stride=F), :]
                r.dxf[pl.ds(w * n * CH + s * F + f, n, stride=CH), :] = got
        for i in range(n):
            if S * F < CH:
                r.dxf[(w * n + i) * CH + S * F : (w * n + i + 1) * CH, :] = jnp.zeros((CH - S * F, 128), F32)
            r.dxs[w, i] = r.dxf[cut(w * n + i, CH), :].astype(BF16)
        for o in range(1, n):
            q.dx.start(r.dxs.at[w, peer(o)], r.dxr.at[me, w], field_at(o))
        r.dxr[me, w] = r.dxs[w, me]

    def pair_heads():
        q.gp.arrived(r.ghp)
        for c in range(chips):
            total = r.gho[c] + r.ghq[c].astype(F32)
            for j in range(m):
                r.gzs[j, c] = total[cut(j, HQ)].astype(BF16)
        for o in range(1, m):
            q.gz.start(r.gzs.at[lax.rem(my + o, m)], r.gzr.at[my], dp_at(o))
        r.gzr[my] = r.gzs[my]
        send_losses()

    def plane_heads():
        q.gz.arrived(r.gzr.at[pl.ds(0, m - 1)])
        for c in range(chips):
            total = r.gzr[0, c].astype(F32)
            for j in range(1, m):
                total = total + r.gzr[j, c].astype(F32)
            r.ghs[c] = total.astype(BF16)
        for k in range(1, chips):
            q.gh.start(r.ghs.at[other(k)], r.ghr.at[chip], far(k))
        r.ghr[chip] = r.ghs[chip]

    def share_heads():
        q.gh.arrived(r.ghr.at[pl.ds(0, chips - 1)])
        r.a2s[...] = total_of(r.ghr, chips).astype(BF16)
        for o in range(1, m):
            q.a2.start(r.a2s, r.a2r.at[my], dp_at(o))
        r.a2r[my] = r.a2s[...]

    grads = (r.g_in, r.g_out, r.g_up, r.g_down)

    def total_of(ref, count):
        total = ref[0].astype(F32)
        for i in range(1, count):
            total = total + ref[i].astype(F32)
        return total

    def dp_first(total, send, recv, lane):
        C = send.shape[1]
        for i in range(m):
            send[i] = total[cut(i, C), :].astype(BF16)
        for o in range(1, m):
            lane.start(send.at[lax.rem(my + o, m)], recv.at[my], dp_at(o))
        recv[my] = send[my]

    def dp_second(recv, lane, last, out, last_lane):
        lane.arrived(recv.at[pl.ds(0, m - 1)])
        last[...] = total_of(recv, m).astype(BF16)
        for o in range(1, m):
            last_lane.start(last, out.at[my], dp_at(o))
        out[my] = last[...]

    hooks = {PAIR: pair_heads}
    weave([backward_window(w, r, give) for w in range(W)], [BACKWARD_LAG * (2 * w // W) for w in range(W)], hooks)

    r.g_up[...] = mm_tn(r.n2[...], r.du[...])
    r.g_down[...] = mm_tn(r.dyb[...], r.a[...]).T
    r.g_out[...] = mm_tn(r.o[...], r.db[...])
    r.g_in[...] = mm_tn(r.n1[...], r.dm[...])
    r.gbf[z.R :, :] = r.g_vec[...]
    for i in range(n):
        for name, row, size, block in z.plan:
            r.gbf[row : row + size, :] = grads[name][cut(i, size), cut(block, 128)]
        r.gbs[i % 2, i // 2] = r.gbf[...].astype(BF16)
    q.gc.start(r.gbs.at[1 - core], r.gbq, partner)
    q.gc.arrived(r.gbq)
    for c in range(chips):
        r.gbt[c] = (r.gbs[core, c].astype(F32) + r.gbq[c].astype(F32)).astype(BF16)
    for k in range(1, chips):
        q.gb.start(r.gbt.at[other(k)], r.gbr.at[chip], far(k))
    r.gbr[chip] = r.gbt[chip]

    q.dx.arrived(r.dxr.at[pl.ds(0, n - 1)])
    outs = [pltpu.make_async_copy(r.dxr, r.dx_out, r.load_sems.at[0])]
    outs[0].start()
    for g in range(G):
        r.dxw[cut(g, CH), :] = r.dxr[g // W, g % W].astype(F32)
    for f in range(F):
        rows = [r.dxw[pl.ds(s * F + f, G, stride=CH), :] for s in range(S)]
        total = mm(r.hot[f], jnp.concatenate(rows, axis=0).astype(BF16))
        r.sumb[pl.ds(f, BAND, stride=F), :] = total[:BAND]
    dp_first(r.sumb, r.b1s, r.b1r, q.b1)
    q.gb.arrived(r.gbr.at[pl.ds(0, chips - 1)])
    r.sumc[0 : z.RR, :] = total_of(r.gbr, chips)
    if m * z.CC > z.RR:
        r.sumc[z.RR :, :] = jnp.zeros((m * z.CC - z.RR, 128), F32)
    dp_first(r.sumc, r.c1s, r.c1r, q.c1)
    plane_heads()

    q.w.left(r.wr.at[pl.ds(0, chips)])
    q.wf.left(r.wr.at[pl.ds(0, chips - 1)])
    q.x.left(r.xr.at[:, pl.ds(0, n - 1)])
    q.t.left(r.tgs.at[pl.ds(0, (n - 1) * F)])
    q.h.left(r.hr.at[pl.ds(0, chips * FB)])
    q.hf.left(r.hr.at[pl.ds(0, (chips - 1) * FB)])
    q.gp.left(r.ghp)
    q.ls.left(r.lsr.at[pl.ds(0, n - 1)])
    q.ls.arrived(r.lsr.at[pl.ds(0, n - 1)])
    outs.append(pltpu.make_async_copy(r.lsr, r.ls_out, r.load_sems.at[1]))
    outs[1].start()
    q.gc.left(r.gbq)
    q.gb.left(r.gbr.at[pl.ds(0, chips - 1)])
    q.dx.left(r.dxr.at[pl.ds(0, n - 1)])
    q.gz.left(r.gzr.at[pl.ds(0, m - 1)])
    dp_second(r.b1r, q.b1, r.b2s, r.b2r, q.b2)
    dp_second(r.c1r, q.c1, r.c2s, r.c2r, q.c2)
    share_heads()
    q.gh.left(r.ghr.at[pl.ds(0, chips - 1)])
    others = pl.ds(0, m - 1)
    q.b1.left(r.b1r.at[others])
    q.c1.left(r.c1r.at[others])
    for lane, ref, out in ((q.b2, r.b2r, r.b2_out), (q.c2, r.c2r, r.c2_out), (q.a2, r.a2r, r.a2_out)):
        lane.arrived(ref.at[others])
        outs.append(pltpu.make_async_copy(ref, out, r.load_sems.at[len(outs)]))
        outs[-1].start()
        lane.left(ref.at[others])
    for out in outs:
        out.wait()


def lane_slots(n, W):
    slots = dict(w=n // 2, wf=1, x=W, t=1, h=n // 2, hf=1, gp=1, gh=1, ls=1, dx=1, gc=1, gb=1, gz=1, a2=1, b1=1, b2=1, c1=1, c2=1)
    return list(slots.items())


FORWARD_LAG, BACKWARD_LAG, PAIR = 4, 28, 5


def step_call(cfg, valid, ins):
    n, m, F, W, S, bins = cfg
    z = layout(cfg)
    CH, L, G, fields, chips, BAND, HQ = z.CH, W * 320, n * W, n * F, n // 2, z.BAND, z.HQ
    FB = F * BAND
    GL = max(G, 128)
    A = jax.ShapeDtypeStruct
    V = pltpu.VMEM
    D = pltpu.SemaphoreType.DMA
    outs = dict(
        dx_out=A((n, W, CH, 128), BF16),
        a2_out=A((m, HQ, 128), BF16),
        b2_out=A((m, z.CB, 128), BF16),
        c2_out=A((m, z.CC, 128), BF16),
        ls_out=A((n, F, 1, GL), F32),
    )
    scr = dict(
        dxr=V((n, W, CH, 128), BF16),
        a2r=V((m, HQ, 128), BF16),
        b2r=V((m, z.CB, 128), BF16),
        c2r=V((m, z.CC, 128), BF16),
        sumc=V((m * z.CC, 128), F32),
        c1s=V((m, z.CC, 128), BF16),
        c1r=V((m, z.CC, 128), BF16),
        c2s=V((z.CC, 128), BF16),
        lsr=V((n, F, 1, GL), F32),
        wf=V((z.R + 16, 128), F32),
        ws=V((z.R + 16, 128), BF16),
        wr=V((n, z.R + 16, 128), BF16),
        tab=V((F, 128, 128), F32),
        hf=V((F, BAND, 128), F32),
        hs=V((FB, 128), BF16),
        hr=V((fields * BAND, 128), BF16),
        row=V((F, S * G), jnp.int32),
        trow=V((F, S * G), jnp.int32),
        hot=V((F, 128, S * G), BF16),
        rows_out=V((G * CH, 128), F32),
        rows_in=V((G * CH, 128), F32),
        xs=V((n, W, CH, 128), BF16),
        xr=V((W, n, CH, 128), BF16),
        tgs=V((fields, 1, 128), F32),
        tgt=V((fields, 1, 128), F32),
        w_in=V((128, 384), BF16),
        w_out=V((128, 128), BF16),
        w_up=V((128, 512), BF16),
        w_down=V((512, 128), BF16),
        vec=V((16, 128), F32),
        x=V((L, 128), F32),
        unit1=V((L, 128), F32),
        inv1=V((L, 128), F32),
        unit2=V((L, 128), F32),
        inv2=V((L, 128), F32),
        n1=V((L, 128), BF16),
        n2=V((L, 128), BF16),
        qm=V((W, 1280, 128), BF16),
        k=V((L, 128), BF16),
        v=V((L, 128), BF16),
        o=V((L, 128), BF16),
        pa=V((W, HEADS, 128, 256), F32),
        pd=V((W, HEADS, 128, 128), F32),
        pb=V((W, 320, 256), F32),
        a=V((L, 512), BF16),
        slope=V((L, 512), F32),
        y=V((L, 128), F32),
        dy=V((L, 128), F32),
        du=V((L, 512), BF16),
        dyb=V((L, 128), BF16),
        db=V((L, 128), BF16),
        dm=V((L, 384), BF16),
        dxs=V((W, n, CH, 128), BF16),
        loss=V((fields, 128), F32),
        lss=V((fields, 1, GL), F32),
        gho=V((chips, FB, 128), F32),
        ghp=V((chips, FB, 128), BF16),
        ghq=V((chips, FB, 128), BF16),
        gzs=V((m, chips, HQ, 128), BF16),
        gzr=V((m, chips, HQ, 128), BF16),
        ghs=V((chips, HQ, 128), BF16),
        ghr=V((chips, HQ, 128), BF16),
        g_in=V((128, 384), F32),
        g_out=V((128, 128), F32),
        g_up=V((128, 512), F32),
        g_down=V((512, 128), F32),
        g_vec=V((16, 128), F32),
        gbf=V((z.RR, 128), F32),
        gbs=V((2, chips, z.RR, 128), BF16),
        gbq=V((chips, z.RR, 128), BF16),
        gbt=V((chips, z.RR, 128), BF16),
        gbr=V((chips, z.RR, 128), BF16),
        a2s=V((HQ, 128), BF16),
        sumb=V((m * z.CB, 128), F32),
        b1s=V((m, z.CB, 128), BF16),
        b1r=V((m, z.CB, 128), BF16),
        b2s=V((z.CB, 128), BF16),
        sems=D((sum(1 + slots for name, slots in lane_slots(n, W)),)),
    )
    names = list(outs) + list(scr)
    hbm = pl.BlockSpec(memory_space=pltpu.HBM)
    inside = [V(v.shape, v.dtype) for v in ins]
    res = pl.pallas_call(
        functools.partial(step_kernel, cfg, names, len(ins)),
        out_shape=list(outs.values()),
        in_specs=[pl.BlockSpec(memory_space=pltpu.SMEM)] + [hbm] * len(ins),
        out_specs=[hbm] * len(outs),
        scratch_shapes=list(scr.values()) + inside + [D((len(ins),))],
        compiler_params=pltpu.CompilerParams(vmem_limit_bytes=VMEM_STEP, collective_id=0, has_side_effects=True),
        cost_estimate=pl.CostEstimate(flops=40_000_000_000, bytes_accessed=4_000_000, transcendentals=0),
        name="step",
    )(valid, *ins)
    return res


VMEM_STEP, VMEM_ADAM = 56 * 1024 * 1024, 10 * 1024 * 1024
RATES = (0.8, 0.6, 1.6 * 128 ** (-0.5), 128 ** (-0.5), 4 ** (-0.5), 128 ** (-0.5), 512 ** (-0.5), 0.3)
EMBED, POSITION, HEAD, BLOCK, VECTOR = 0, 1, 2, 3, 7


def adam_kernel(cfg, count_ref, *refs):
    n, m, F, W, S, bins = cfg
    z = layout(cfg)
    given, state, losses, input_out, outs = refs[:5], refs[5:29], refs[29], refs[30], refs[31:63]
    suma, sumb, sumc, sumd, input_grad, dxr, a2r, b2r, c2r, lsr, sems = refs[63:]
    loads = []
    for i, (there, here) in enumerate(zip(given, (dxr, a2r, b2r, c2r, lsr))):
        loads.append(pltpu.make_async_copy(there, here, sems.at[i]))
        loads[i].start()
    me = lax.axis_index("field")
    half = lax.fori_loop(0, count_ref[0], lambda i, v: v * 0.5, jnp.float32(1.0))
    inv_c = 1.0 / (jnp.zeros((1, 128), F32) + (1.0 - half))

    def adam(weight, at, grad):
        c = inv_c[0:1, 0 : grad.shape[-1]]
        master = state[3 * weight][at]
        first = 0.5 * state[3 * weight + 1][at] + 0.5 * grad
        second = 0.5 * state[3 * weight + 2][at] + 0.5 * grad * grad
        new = master - RATES[weight] * (first * c / (jnp.sqrt(second * c) + 1e-08) + 0.1 * master)
        outs[4 * weight][at] = first
        outs[4 * weight + 1][at] = second
        outs[4 * weight + 2][at] = new
        outs[4 * weight + 3][at] = new.astype(BF16)

    BAND = z.BAND
    loads[0].wait()
    for g in range(n * W):
        input_grad[cut(g, S * F), :] = dxr[g // W, g % W].astype(F32)[: S * F]
    leave = pltpu.make_async_copy(input_grad, input_out, sems.at[5])
    leave.start()
    for load in loads[1:]:
        load.wait()
    for i in range(m):
        sumd[cut(i, z.CC), :] = c2r[i].astype(F32)
        sumb[cut(i, z.CB), :] = b2r[i].astype(F32)
        sumc[cut(i, z.HQ), :] = a2r[i].astype(F32)
    for f in range(F):
        suma[pl.ds(f, BAND, stride=F), :] = sumc[cut(f, BAND), :]
    every = slice(None)
    tokens = F * bins
    adam(HEAD, (every, every), suma[0:tokens, :])
    adam(EMBED, (every, every), sumb[0:tokens, :])
    adam(POSITION, (every, every), sumb[tokens : tokens + S * F, :])
    for name, row, size, block in z.plan:
        adam(BLOCK + name, (every, cut(block, 128)), sumd[row : row + size, :])
    vecs = sumd[z.R : z.R + 16, :]
    pick = lane_pick(me, 128 // n).astype(F32)
    mine = lax.dot_general(
        vecs, pick, (((1,), (1,)), ((), ())), preferred_element_type=F32, precision=lax.Precision.HIGHEST
    )
    adam(VECTOR, (every, every), mine[0:12])
    for f in range(F):
        total = lsr[0, f]
        for i in range(1, n):
            total = total + lsr[i, f]
        losses[f : f + 1, :] = total[:, : n * W]
    leave.wait()


def adam_call(cfg, count, got, state):
    n, m, F, W, S, bins = cfg
    z = layout(cfg)
    A = jax.ShapeDtypeStruct
    given = [pltpu.with_memory_space_constraint(v, pltpu.HBM) for v in got]
    outs = [A((F, n * W), F32), A((n * W * S * F, 128), F32)]
    for i in range(8):
        shape = state[3 * i].shape
        outs.extend([A(shape, F32)] * 3 + [A(shape, BF16)])
    vm = pl.BlockSpec(memory_space=pltpu.VMEM)
    hbm = pl.BlockSpec(memory_space=pltpu.HBM)
    sm = pl.BlockSpec(memory_space=pltpu.SMEM)
    return pl.pallas_call(
        functools.partial(adam_kernel, cfg),
        out_shape=outs,
        in_specs=[sm] + [hbm] * 5 + [vm] * 24,
        out_specs=[vm, hbm] + [vm] * 32,
        scratch_shapes=[pltpu.VMEM((size, 128), F32) for size in (F * z.BAND, m * z.CB, F * z.BAND, m * z.CC, n * W * S * F)]
        + [pltpu.VMEM(v.shape, v.dtype) for v in given]
        + [pltpu.SemaphoreType.DMA((6,))],
        compiler_params=pltpu.CompilerParams(vmem_limit_bytes=VMEM_ADAM),
        name="adam",
    )(count, *given, *state)


def local(n, m, bin_tokens, targets, valid_steps, step_count, *state):
    windows, S, F = bin_tokens.shape
    bins = state[0].shape[1]
    cfg = (n, m, F, windows // n, S, bins)
    by_bin = lambda v: v.transpose(1, 0, 2).reshape(bins * F, 128)
    by_class = lambda v: v.transpose(2, 0, 1).reshape(bins * F, 128)
    flat = [by_bin(v) for v in state[0:3]] + [v.reshape(S * F, 128) for v in state[3:6]]
    flat += [by_class(v) for v in state[6:9]] + list(state[9:])
    blocks = [flat[i] for i in (9, 12, 15, 18, 21, 0, 3)]
    ins = [*blocks, bin_tokens.transpose(1, 2, 0), flat[6], targets.transpose(1, 2, 0)]
    got = step_call(cfg, valid_steps, ins)
    losses, input_grad, *new = adam_call(cfg, step_count.reshape(1), got, flat)
    new[0:4] = [v.reshape(bins, F, 128).transpose(1, 0, 2) for v in new[0:4]]
    new[4:8] = [v.reshape(S, F, 128) for v in new[4:8]]
    new[8:12] = [v.reshape(bins, F, 128).transpose(1, 2, 0) for v in new[8:12]]
    return (losses.transpose(1, 0), input_grad.reshape(windows, S, F, 128), *new)


def solution(mesh):
    n, m = mesh.shape["field"], mesh.shape["dp"]
    stack, rows, cols = P("field", None, None), P("field", None), P(None, "field")
    by_weight = (stack, P(None, "field", None), stack, rows, rows, rows, rows, cols)
    in_specs = [P("dp", None, "field"), P("dp", None, "field"), P("dp"), P()]
    out_specs = [P("dp", "field"), P("dp", None, "field", None)]
    for spec in by_weight:
        in_specs.extend([spec] * 3)
        out_specs.extend([spec] * 4)
    return jax.shard_map(
        functools.partial(local, n, m),
        mesh=mesh,
        in_specs=tuple(in_specs),
        out_specs=tuple(out_specs),
        check_vma=False,
    )
```

```python
import functools
import types
import jax
import jax.numpy as jnp
from jax import lax
from jax.experimental import pallas as pl
from jax.experimental.pallas import tpu as pltpu
from jax.sharding import PartitionSpec as P

F32 = jnp.float32
BF16 = jnp.bfloat16
HEADS = 4
NEG = -1e30


def mm(a, b):
    return jnp.dot(a, b, preferred_element_type=F32)


def mm_nt(a, b):
    return lax.dot_general(a, b, (((1,), (1,)), ((), ())), preferred_element_type=F32)


def mm_tn(a, b):
    return lax.dot_general(a, b, (((0,), (0,)), ((), ())), preferred_element_type=F32)


def head_lanes(shape, head):
    lane = lax.broadcasted_iota(jnp.int32, shape, 1)
    return (lane >= head * 32) & (lane < (head + 1) * 32)


def spread_heads(value):
    parts = []
    for head in range(HEADS):
        parts.append(jnp.where(head_lanes((256, 128), head), value[:256], 0.0))
    for head in range(HEADS):
        parts.append(jnp.where(head_lanes((64, 128), head), value[256:], 0.0))
    return jnp.concatenate(parts, axis=0).astype(BF16)


def join_heads(tall):
    out = tall[0:64]
    for head in range(1, HEADS):
        out = jnp.where(head_lanes((64, 128), head), tall[head * 64 : (head + 1) * 64], out)
    return out


def norm_stats(v):
    mean = jnp.mean(v, axis=-1, keepdims=True)
    c = v - mean
    spread = jnp.mean(c * c, axis=-1, keepdims=True)
    inv = lax.rsqrt(spread + 1e-05)
    return c * inv, jnp.broadcast_to(inv, v.shape)


def norm_back(grad, gain, unit, inv):
    e = grad * gain
    m1 = jnp.mean(e, axis=-1, keepdims=True)
    m2 = jnp.mean(e * unit, axis=-1, keepdims=True)
    return inv * (e - m1 - unit * m2)


SCALE = 32 ** (-0.5)
LOG2E = 1.4426950408889634


def causal_square(n):
    k = lax.broadcasted_iota(jnp.int32, (n, n), 0)
    q = lax.broadcasted_iota(jnp.int32, (n, n), 1)
    return k <= q


def soft_cols(pieces):
    peak = functools.reduce(jnp.maximum, [jnp.max(p, axis=0, keepdims=True) for p in pieces])
    shift = peak * (SCALE * LOG2E)
    es = [jnp.exp2(p * (SCALE * LOG2E) - shift) for p in pieces]
    total = functools.reduce(lambda a, b: a + b, [jnp.sum(e, axis=0, keepdims=True) for e in es])
    inv = 1.0 / total
    return [e * inv for e in es]


def forward_window(w, r, take):
    rows = pl.ds(w * 320, 320)
    vec = r.vec
    take(w)
    yield
    x = r.x[rows, :]
    unit, inv = norm_stats(x)
    r.unit1[rows, :] = unit
    r.inv1[rows, :] = inv
    n1 = (unit * vec[0:1, :] + vec[1:2, :]).astype(BF16)
    r.n1[rows, :] = n1
    yield
    mixed = mm(n1, r.w_in[...])
    q = mixed[:, 0:128] + vec[2:3, :]
    k = mixed[:, 128:256]
    v = mixed[:, 256:384] + vec[3:4, :]
    yield
    qm = spread_heads(q)
    kb = k.astype(BF16)
    vb = v.astype(BF16)
    r.qm[w] = qm
    r.k[rows, :] = kb
    r.v[rows, :] = vb
    vt = v.T.astype(BF16)
    yield
    mask128 = causal_square(128)
    ot_parts = []
    for head in range(HEADS):
        s = mm_nt(kb[0:256], qm[head * 256 : (head + 1) * 256])
        yield
        s00 = jnp.where(mask128, s[0:128, 0:128], NEG)
        (p00,) = soft_cols([s00])
        r.pa[w, head, 0:128, 0:128] = p00
        yield
        s11 = jnp.where(mask128, s[128:256, 128:256], NEG)
        p01, p11 = soft_cols([s[0:128, 128:256], s11])
        r.pa[w, head, 0:128, 128:256] = p01
        r.pd[w, head] = p11
        yield
        b11 = p11.astype(BF16)
        pb = jnp.concatenate(
            [
                jnp.concatenate([p00.astype(BF16), p01.astype(BF16)], axis=1),
                jnp.concatenate([jnp.zeros((128, 128), BF16), b11], axis=1),
            ],
            axis=0,
        )
        ot_parts.append(mm(vt[head * 32 : (head + 1) * 32, 0:256], pb))
        yield
    ot = jnp.concatenate(ot_parts, axis=0)
    sb = mm_nt(kb, qm[1024:1280])
    yield
    kk = lax.broadcasted_iota(jnp.int32, (64, 256), 0)
    qq = lax.broadcasted_iota(jnp.int32, (64, 256), 1) % 64
    pbs = []
    for half in range(2):
        cols = slice(half * 128, (half + 1) * 128)
        s_low = jnp.where((kk <= qq)[:, cols], sb[256:320, cols], NEG)
        p_top, p_low = soft_cols([sb[0:256, cols], s_low])
        r.pb[w, 0:256, cols] = p_top
        r.pb[w, 256:320, cols] = p_low
        pbs.append(jnp.concatenate([p_top.astype(BF16), p_low.astype(BF16)], axis=0))
        yield
    pbb = jnp.concatenate(pbs, axis=1)
    otb = mm(vt, pbb)
    yield
    o_tail = join_heads(otb.T)
    o = jnp.concatenate([ot.T, o_tail], axis=0).astype(BF16)
    r.o[rows, :] = o
    yield
    x1 = x + mm(o, r.w_out[...]) + vec[4:5, :]
    yield
    unit, inv = norm_stats(x1)
    r.unit2[rows, :] = unit
    r.inv2[rows, :] = inv
    n2 = (unit * vec[5:6, :] + vec[6:7, :]).astype(BF16)
    r.n2[rows, :] = n2
    yield
    y = x1 + vec[7:8, :]
    for part in range(2):
        cols = cut(part, 256)
        bias = jnp.concatenate([vec[8 + 2 * part : 9 + 2 * part, :], vec[9 + 2 * part : 10 + 2 * part, :]], axis=1)
        u = mm(n2, r.w_up[:, cols]) + bias
        yield
        phi = 0.5 * (1.0 + lax.erf(u * 0.7071067811865476))
        a = (u * phi).astype(BF16)
        r.a[rows, cols] = a
        r.slope[rows, cols] = phi + u * jnp.exp2(u * u * (-0.5 * LOG2E)) * 0.3989422804014327
        yield
        y = y + mm(a, r.w_down[cols, :])
        yield
    r.y[rows, :] = y.astype(BF16).astype(F32)


def head_field(f, live, keep, r):
    W, T = r.W, live.shape[1]
    starts = [pl.ds(step * 32 + f, W, stride=320) for step in range(T // W)]
    yf = jnp.concatenate([r.y[at, :] for at in starts], axis=0).astype(BF16)
    wt = r.hr[pl.ds(pl.multiple_of(f * r.band, 16), r.band), :]
    lt = mm_nt(wt, yf)
    yield
    bins = lax.broadcasted_iota(jnp.int32, lt.shape, 0)
    lt = jnp.where(bins < r.bins, lt, NEG)
    peak = jnp.max(lt, axis=0, keepdims=True)
    e = jnp.exp(lt - peak)
    yield
    total = jnp.sum(e, axis=0, keepdims=True)
    lse = peak + jnp.log(total)
    hot = bins.astype(F32) == r.tgt[f][:, :T]
    picked = jnp.sum(jnp.where(hot, lt, 0.0), axis=0, keepdims=True)
    r.loss[pl.ds(f, 1), 0:T] = (lse - picked) * live
    yield
    dl = (jnp.exp(lt - lse) - hot.astype(F32)) * live
    yield
    keep(mm(dl.astype(BF16), yf))
    yield
    dy = mm(dl.T.astype(BF16), wt)
    yield
    dy = dy.astype(BF16).astype(F32)
    for step, at in enumerate(starts):
        r.dy[at, :] = dy[step * W : (step + 1) * W]


def colsum(v):
    return jnp.sum(v, axis=0, keepdims=True)


def backward_window(w, r, give):
    rows = pl.ds(w * 320, 320)
    vec = r.vec
    gv = r.g_vec
    dy = r.dy[rows, :]
    dyb = dy.astype(BF16)
    gv[7:8, :] += colsum(dy)
    dn2 = jnp.zeros((320, 128), F32)
    r.dyb[rows, :] = dyb
    yield
    for part in range(2):
        cols = cut(part, 256)
        da = mm_nt(dyb, r.w_down[cols, :])
        du = (da * r.slope[rows, cols]).astype(BF16)
        bias = colsum(du.astype(F32))
        gv[8 + 2 * part : 9 + 2 * part, :] += bias[:, 0:128]
        gv[9 + 2 * part : 10 + 2 * part, :] += bias[:, 128:256]
        r.du[rows, cols] = du
        dn2 = dn2 + mm_nt(du, r.w_up[:, cols])
        yield
    unit = r.unit2[rows, :]
    gv[5:6, :] += colsum(dn2 * unit)
    gv[6:7, :] += colsum(dn2)
    dx1 = dy + norm_back(dn2, vec[5:6, :], unit, r.inv2[rows, :])
    yield
    db = dx1.astype(BF16)
    gv[4:5, :] += colsum(db.astype(F32))
    r.db[rows, :] = db
    do = mm_nt(db, r.w_out[...])
    yield
    dom = spread_heads(do)
    kb = r.k[rows, :]
    vb = r.v[rows, :]
    kt = kb.astype(F32).T.astype(BF16)
    dv = jnp.zeros((256, 128), F32)
    dk = jnp.zeros((256, 128), F32)
    dqt = []
    yield
    for head in range(HEADS):
        part = slice(head * 256, (head + 1) * 256)
        p00 = r.pa[w, head, 0:128, 0:128]
        p01 = r.pa[w, head, 0:128, 128:256]
        p11 = r.pd[w, head]
        dp = mm_nt(vb[0:256], dom[part])
        yield
        d0 = p00 * dp[0:128, 0:128]
        d1a = p01 * dp[0:128, 128:256]
        d1b = p11 * dp[128:256, 128:256]
        t0 = colsum(d0)
        t1 = colsum(d1a) + colsum(d1b)
        ds00 = (d0 - p00 * t0).astype(BF16)
        ds01 = (d1a - p01 * t1).astype(BF16)
        ds11 = (d1b - p11 * t1).astype(BF16)
        yield
        zero = jnp.zeros((128, 128), BF16)
        pb = jnp.concatenate(
            [
                jnp.concatenate([p00.astype(BF16), p01.astype(BF16)], axis=1),
                jnp.concatenate([zero, p11.astype(BF16)], axis=1),
            ],
            axis=0,
        )
        dsb = jnp.concatenate(
            [jnp.concatenate([ds00, ds01], axis=1), jnp.concatenate([zero, ds11], axis=1)], axis=0
        )
        dv = dv + mm(pb, dom[part])
        dk = dk + mm(dsb, r.qm[w, part, :])
        dqt.append(mm(kt[head * 32 : (head + 1) * 32, 0:256], dsb))
        yield
    pt = r.pb[w]
    dp = mm_nt(vb, dom[1024:1280])
    yield
    d = pt * dp
    dsb = (d - pt * colsum(d)).astype(BF16)
    yield
    dvb = mm(pt.astype(BF16), dom[1024:1280])
    dkb = mm(dsb, r.qm[w, 1024:1280, :])
    yield
    dq_tail = join_heads(mm(kt, dsb).T)
    dq = jnp.concatenate([jnp.concatenate(dqt, axis=0).T, dq_tail], axis=0) * SCALE
    dv = jnp.concatenate([dv + dvb[0:256], dvb[256:320]], axis=0)
    dk = jnp.concatenate([dk + dkb[0:256], dkb[256:320]], axis=0) * SCALE
    dq = dq.astype(BF16)
    dk = dk.astype(BF16)
    dv = dv.astype(BF16)
    yield
    gv[2:3, :] += colsum(dq.astype(F32))
    gv[3:4, :] += colsum(dv.astype(F32))
    dm = jnp.concatenate([dq, dk, dv], axis=1)
    r.dm[rows, :] = dm
    dn1 = mm_nt(dm, r.w_in[...])
    yield
    unit = r.unit1[rows, :]
    gv[0:1, :] += colsum(dn1 * unit)
    gv[1:2, :] += colsum(dn1)
    dx = dx1 + norm_back(dn1, vec[0:1, :], unit, r.inv1[rows, :])
    r.dx[rows, :] = dx
    yield
    give(w)


def weave(gens, delays, hooks=()):
    live = [[g, wait] for g, wait in zip(gens, delays)]
    hooks = dict(hooks)
    turn = 0
    while live:
        if turn in hooks:
            hooks.pop(turn)()
        for item in list(live):
            if item[1] > 0:
                item[1] -= 1
                continue
            try:
                next(item[0])
            except StopIteration:
                live.remove(item)
        turn += 1
    for left in sorted(hooks):
        hooks[left]()


MESH = pl.DeviceIdType.MESH


def plan_rows(n, parts):
    plan, row = [], 0
    for name in parts:
        total, blocks = ((128, 3), (128, 1), (128, 4), (512, 1))[name]
        size = total // n
        for block in range(blocks):
            plan.append((name, row, size, block))
            row += size
    return plan, -(-row // 16) * 16


class Lane:
    def __init__(self, sems, first, anyone):
        self.sems, self.first, self.anyone = sems, first, anyone

    def copy(self, src, dst, slot, target):
        return pltpu.make_async_remote_copy(
            src_ref=src,
            dst_ref=dst,
            send_sem=self.sems.at[self.first],
            recv_sem=self.sems.at[self.first + 1 + slot],
            device_id=target,
            device_id_type=MESH,
        )

    def start(self, src, dst, target, slot=0):
        self.copy(src, dst, slot, target).start()

    def arrived(self, like, slot=0):
        self.copy(like, like, slot, self.anyone).wait_recv()

    def left(self, like):
        self.copy(like, like, 0, self.anyone).wait_send()


def lane_pick(me, width):
    row = lax.broadcasted_iota(jnp.int32, (width, 128), 0)
    lane = lax.broadcasted_iota(jnp.int32, (width, 128), 1)
    return lane == row + me * width


def cut(i, size):
    return slice(i * size, (i + 1) * size)


def layout(cfg):
    n, m, F, W, S, bins = cfg
    CH = -(-S * F // 8) * 8
    BAND = 112 if F * 112 % (8 * m) == 0 else 128
    plan, R = plan_rows(n, (0, 1, 2, 3))
    RR = R + 16
    CB = F * BAND // m
    CC = -(-RR // (16 * m)) * 16
    HQ = F * BAND // m
    return types.SimpleNamespace(CH=CH, BAND=BAND, plan=plan, R=R, RR=RR, CB=CB, CC=CC, HQ=HQ)


def step_kernel(cfg, names, count, valid, *refs):
    r = types.SimpleNamespace(**dict(zip(names, refs[count:])))
    r.valid, r.outside, r.inside, r.load_sems = valid, refs[:count], refs[-1 - count : -1], refs[-1]
    n, m, F, W, S, bins = cfg
    z = layout(cfg)
    CH, T, G, fields, BAND, HQ = z.CH, S * W, n * W, n * F, z.BAND, z.HQ
    FB = F * BAND
    r.bins, r.W, r.band = bins, W, BAND
    r.xsf = r.dxf = r.rows_out
    r.xf = r.dxw = r.rows_in
    r.dx = r.y
    me, my = lax.axis_index("field"), lax.axis_index("dp")
    chips = n // 2
    core, chip = lax.rem(me, 2), me // 2
    partner = {"field": me + 1 - 2 * core}
    other = lambda k: lax.rem(chip + k, chips)
    back = lambda k: lax.rem(chip + chips - k, chips)
    far = lambda k: {"field": other(k) * 2 + core}
    peer = lambda o: lax.rem(me + o, n)
    field_at = lambda o: {"field": peer(o)}
    dp_at = lambda o: {"dp": lax.rem(my + o, m)}

    barrier = pltpu.get_barrier_semaphore()
    for o in range(1, n):
        pl.semaphore_signal(barrier, 1, device_id=field_at(o), device_id_type=MESH)
    for o in range(1, m):
        pl.semaphore_signal(barrier, 1, device_id=dp_at(o), device_id_type=MESH)

    loads = []
    for i, (there, here) in enumerate(zip(r.outside, r.inside)):
        loads.append(pltpu.make_async_copy(there, here, r.load_sems.at[i]))
        loads[-1].start()
    for load in loads:
        load.wait()

    lanes, count = {}, 0
    for name, slots in lane_slots(n, W):
        lanes[name] = Lane(r.sems, count, partner)
        count += 1 + slots
    q = types.SimpleNamespace(**lanes)

    r.inproj, r.outproj, r.expand, r.shrink, r.vector, r.embed, r.position, r.tok, r.head, r.tgi = r.inside
    masters = (r.inproj, r.outproj, r.expand, r.shrink)
    for name, row, size, block in z.plan:
        r.wf[row : row + size, :] = masters[name][:, cut(block, 128)]
    r.wf[z.R : z.R + 16, :] = jnp.zeros((16, 128), F32)
    r.wf[z.R : z.R + 12, :] = mm(r.vector[...].astype(BF16), lane_pick(me, 128 // n).astype(BF16))
    r.ws[...] = r.wf[...].astype(BF16)
    for f in range(F):
        r.tab[f, bins - 4 :, :] = jnp.zeros((132 - bins, 128), F32)
        r.tab[f, 0:bins, :] = r.embed[pl.ds(f, bins, stride=F), :]
        r.tab[f, bins : bins + S, :] = r.position[pl.ds(f, S, stride=F), :]
        r.hf[f, bins - 4 :, :] = jnp.zeros((BAND + 4 - bins, 128), F32)
        r.hf[f, 0:bins, :] = r.head[pl.ds(f, bins, stride=F), :]
        r.hs[cut(f, BAND), :] = r.hf[f].astype(BF16)

    row = lax.broadcasted_iota(jnp.int32, (128, S * G), 0)
    step_row = lax.broadcasted_iota(jnp.int32, (1, S * G), 1) // G + bins
    for s in range(S):
        r.row[:, cut(s, G)] = r.tok[s]
        r.trow[:, cut(s, G)] = r.tgi[s]
    for f in range(F):
        hot = ((row == r.row[f : f + 1, :]) | (row == step_row)).astype(F32).astype(BF16)
        r.hot[f] = hot
        made = mm_tn(hot, r.tab[f].astype(BF16))
        for s in range(S):
            for d in range(n):
                at = s * G + d * W
                r.xsf[pl.ds(d * W * CH + s * F + f, W, stride=CH), :] = made[at : at + W]
    if S * F < CH:
        for g in range(G):
            r.xsf[g * CH + S * F : (g + 1) * CH, :] = jnp.zeros((CH - S * F, 128), F32)
    for d in range(n):
        for w in range(W):
            r.xs[d, w] = r.xsf[cut(d * W + w, CH), :].astype(BF16)

    pl.semaphore_wait(barrier, n - 1 + m - 1)

    q.w.start(r.ws, r.wr.at[me], partner, 0)
    for k in range(1, chips):
        q.w.start(r.ws, r.wr.at[me], far(k), k)
    for w in range(W):
        for o in range(1, n):
            q.x.start(r.xs.at[peer(o), w], r.xr.at[w, me], field_at(o), w)
    r.wr[me] = r.ws[...]
    for w in range(W):
        r.xr[w, me] = r.xs[me, w]

    own = lax.broadcasted_iota(jnp.int32, (fields, S * G), 1) % G // W
    mine = own == lax.broadcasted_iota(jnp.int32, (fields, S * G), 0) // F
    spread = jnp.concatenate([r.trow[...].astype(F32)] * n, axis=0)
    spread = jnp.where(mine, spread, 0.0).astype(BF16)
    source = lax.broadcasted_iota(jnp.int32, (S * G, 128), 0)
    place = lax.broadcasted_iota(jnp.int32, (S * G, 128), 1)
    move = (source // G * W + source % W == place).astype(F32).astype(BF16)
    target_rows = mm(spread, move)
    for i in range(fields):
        r.tgs[i] = target_rows[i : i + 1]
    there = pl.ds(me * F, F)
    for o in range(1, n):
        q.t.start(r.tgs.at[pl.ds(peer(o) * F, F)], r.tgt.at[there], field_at(o))
    mine = pl.ds(pl.multiple_of(me * FB, 16), FB)
    q.h.start(r.hs, r.hr.at[mine], partner, 0)
    for k in range(1, chips):
        q.h.start(r.hs, r.hr.at[mine], far(k), k)
    for f in range(F):
        r.tgt[me * F + f] = r.tgs[me * F + f]
    r.hr[mine, :] = r.hs[...]

    for k in range(1, chips):
        q.w.arrived(r.ws, k)
        slot = r.wr.at[back(k) * 2 + core]
        q.wf.start(slot, slot, partner)
    q.w.arrived(r.ws, 0)
    q.wf.arrived(r.wr.at[pl.ds(0, chips - 1)])
    full = (r.w_in, r.w_out, r.w_up, r.w_down)
    wide = (r.g_in, r.g_out, r.g_up, r.g_down)
    vec = jnp.zeros((16, 128), F32)
    for i in range(n):
        shard = r.wr[i].astype(F32)
        vec = vec + shard[z.R :]
        for name, row, size, block in z.plan:
            to = full if size % 16 == 0 else wide
            piece = shard[row : row + size]
            to[name][cut(i, size), cut(block, 128)] = piece.astype(to[name].dtype)
    for name, row, size, block in z.plan:
        if size % 16:
            full[name][:, cut(block, 128)] = wide[name][:, cut(block, 128)].astype(BF16)
    r.vec[...] = vec
    r.g_vec[...] = jnp.zeros((16, 128), F32)

    def take(w):
        q.x.arrived(r.xr.at[w, pl.ds(0, n - 1)], w)
        for i in range(n):
            r.xf[cut(w * n + i, CH), :] = r.xr[w, i].astype(F32)
        for s in range(S):
            for f in range(F):
                got = r.xf[pl.ds(w * n * CH + s * F + f, n, stride=CH), :]
                r.x[pl.ds(w * 320 + s * fields + f, n, stride=F), :] = got

    weave([forward_window(w, r, take) for w in range(W)], [FORWARD_LAG * w for w in range(W)])

    q.t.arrived(r.tgs.at[pl.ds(0, (n - 1) * F)])
    lane = lax.broadcasted_iota(jnp.int32, (1, T), 1)
    live = jnp.zeros((1, T), F32)
    for w in range(W):
        inside = (lane // W).astype(F32) < r.valid[me * W + w].astype(F32)
        live = jnp.where(inside & (lane % W == w), 1.0, live)
    r.loss[...] = jnp.zeros_like(r.loss)

    def keeper(ref, c, f):
        def keep(v):
            ref[c, cut(f, BAND), :] = v.astype(ref.dtype)

        return keep

    def heads(*places):
        gens = []
        for c, which, ref in places:
            gens.extend(head_field((c * 2 + which) * F + f, live, keeper(ref, c, f), r) for f in range(F))
        weave(gens, [0] * len(gens))

    for k in range(1, chips):
        q.h.arrived(r.hs, k)
        slot = r.hr.at[pl.ds(pl.multiple_of((back(k) * 2 + core) * FB, 16), FB)]
        q.hf.start(slot, slot, partner)
    heads(*[(other(k), core, r.gho) for k in range(chips)])
    q.h.arrived(r.hs, 0)
    q.hf.arrived(r.hr.at[pl.ds(0, (chips - 1) * FB)])
    heads(*[(other(k), 1 - core, r.ghp) for k in range(chips)])
    q.gp.start(r.ghp, r.ghq, partner)

    def send_losses():
        GL = r.lss.shape[-1]
        row = lax.broadcasted_iota(jnp.int32, (128, GL), 0)
        col = lax.broadcasted_iota(jnp.int32, (128, GL), 1)
        group = ((row < T) & (col == me * W + row % W)).astype(F32)
        sums = jnp.dot(r.loss[...], group, preferred_element_type=F32, precision=lax.Precision.HIGHEST)
        for f in range(fields):
            r.lss[f] = sums[f : f + 1, :]
        for o in range(1, n):
            q.ls.start(r.lss.at[pl.ds(peer(o) * F, F)], r.lsr.at[me], field_at(o))
        r.lsr[me] = r.lss[there]

    def give(w):
        for s in range(S):
            for f in range(F):
                got = r.dx[pl.ds(w * 320 + s * fields + f, n, stride=F), :]
                r.dxf[pl.ds(w * n * CH + s * F + f, n, stride=CH), :] = got
        for i in range(n):
            if S * F < CH:
                r.dxf[(w * n + i) * CH + S * F : (w * n + i + 1) * CH, :] = jnp.zeros((CH - S * F, 128), F32)
            r.dxs[w, i] = r.dxf[cut(w * n + i, CH), :].astype(BF16)
        for o in range(1, n):
            q.dx.start(r.dxs.at[w, peer(o)], r.dxr.at[me, w], field_at(o))
        r.dxr[me, w] = r.dxs[w, me]

    def pair_heads():
        q.gp.arrived(r.ghp)
        for c in range(chips):
            total = r.gho[c] + r.ghq[c].astype(F32)
            for j in range(m):
                r.gzs[j, c] = total[cut(j, HQ)].astype(BF16)
        for o in range(1, m):
            q.gz.start(r.gzs.at[lax.rem(my + o, m)], r.gzr.at[my], dp_at(o))
        r.gzr[my] = r.gzs[my]
        send_losses()

    def plane_heads():
        q.gz.arrived(r.gzr.at[pl.ds(0, m - 1)])
        for c in range(chips):
            total = r.gzr[0, c].astype(F32)
            for j in range(1, m):
                total = total + r.gzr[j, c].astype(F32)
            r.ghs[c] = total.astype(BF16)
        for k in range(1, chips):
            q.gh.start(r.ghs.at[other(k)], r.ghr.at[chip], far(k))
        r.ghr[chip] = r.ghs[chip]

    def share_heads():
        q.gh.arrived(r.ghr.at[pl.ds(0, chips - 1)])
        r.a2s[...] = total_of(r.ghr, chips).astype(BF16)
        for o in range(1, m):
            q.a2.start(r.a2s, r.a2r.at[my], dp_at(o))
        r.a2r[my] = r.a2s[...]

    grads = (r.g_in, r.g_out, r.g_up, r.g_down)

    def total_of(ref, count):
        total = ref[0].astype(F32)
        for i in range(1, count):
            total = total + ref[i].astype(F32)
        return total

    def dp_first(total, send, recv, lane):
        C = send.shape[1]
        for i in range(m):
            send[i] = total[cut(i, C), :].astype(BF16)
        for o in range(1, m):
            lane.start(send.at[lax.rem(my + o, m)], recv.at[my], dp_at(o))
        recv[my] = send[my]

    def dp_second(recv, lane, last, out, last_lane):
        lane.arrived(recv.at[pl.ds(0, m - 1)])
        last[...] = total_of(recv, m).astype(BF16)
        for o in range(1, m):
            last_lane.start(last, out.at[my], dp_at(o))
        out[my] = last[...]

    hooks = {PAIR: pair_heads}
    weave([backward_window(w, r, give) for w in range(W)], [BACKWARD_LAG * (2 * w // W) for w in range(W)], hooks)

    r.g_up[...] = mm_tn(r.n2[...], r.du[...])
    r.g_down[...] = mm_tn(r.dyb[...], r.a[...]).T
    r.g_out[...] = mm_tn(r.o[...], r.db[...])
    r.g_in[...] = mm_tn(r.n1[...], r.dm[...])
    r.gbf[z.R :, :] = r.g_vec[...]
    for i in range(n):
        for name, row, size, block in z.plan:
            r.gbf[row : row + size, :] = grads[name][cut(i, size), cut(block, 128)]
        r.gbs[i % 2, i // 2] = r.gbf[...].astype(BF16)
    q.gc.start(r.gbs.at[1 - core], r.gbq, partner)
    q.gc.arrived(r.gbq)
    for c in range(chips):
        r.gbt[c] = (r.gbs[core, c].astype(F32) + r.gbq[c].astype(F32)).astype(BF16)
    for k in range(1, chips):
        q.gb.start(r.gbt.at[other(k)], r.gbr.at[chip], far(k))
    r.gbr[chip] = r.gbt[chip]

    q.dx.arrived(r.dxr.at[pl.ds(0, n - 1)])
    outs = [pltpu.make_async_copy(r.dxr, r.dx_out, r.load_sems.at[0])]
    outs[0].start()
    for g in range(G):
        r.dxw[cut(g, CH), :] = r.dxr[g // W, g % W].astype(F32)
    for f in range(F):
        rows = [r.dxw[pl.ds(s * F + f, G, stride=CH), :] for s in range(S)]
        total = mm(r.hot[f], jnp.concatenate(rows, axis=0).astype(BF16))
        r.sumb[pl.ds(f, BAND, stride=F), :] = total[:BAND]
    dp_first(r.sumb, r.b1s, r.b1r, q.b1)
    q.gb.arrived(r.gbr.at[pl.ds(0, chips - 1)])
    r.sumc[0 : z.RR, :] = total_of(r.gbr, chips)
    if m * z.CC > z.RR:
        r.sumc[z.RR :, :] = jnp.zeros((m * z.CC - z.RR, 128), F32)
    dp_first(r.sumc, r.c1s, r.c1r, q.c1)
    plane_heads()

    q.w.left(r.wr.at[pl.ds(0, chips)])
    q.wf.left(r.wr.at[pl.ds(0, chips - 1)])
    q.x.left(r.xr.at[:, pl.ds(0, n - 1)])
    q.t.left(r.tgs.at[pl.ds(0, (n - 1) * F)])
    q.h.left(r.hr.at[pl.ds(0, chips * FB)])
    q.hf.left(r.hr.at[pl.ds(0, (chips - 1) * FB)])
    q.gp.left(r.ghp)
    q.ls.left(r.lsr.at[pl.ds(0, n - 1)])
    q.ls.arrived(r.lsr.at[pl.ds(0, n - 1)])
    outs.append(pltpu.make_async_copy(r.lsr, r.ls_out, r.load_sems.at[1]))
    outs[1].start()
    q.gc.left(r.gbq)
    q.gb.left(r.gbr.at[pl.ds(0, chips - 1)])
    q.dx.left(r.dxr.at[pl.ds(0, n - 1)])
    q.gz.left(r.gzr.at[pl.ds(0, m - 1)])
    dp_second(r.b1r, q.b1, r.b2s, r.b2r, q.b2)
    dp_second(r.c1r, q.c1, r.c2s, r.c2r, q.c2)
    share_heads()
    q.gh.left(r.ghr.at[pl.ds(0, chips - 1)])
    others = pl.ds(0, m - 1)
    q.b1.left(r.b1r.at[others])
    q.c1.left(r.c1r.at[others])
    for lane, ref, out in ((q.b2, r.b2r, r.b2_out), (q.c2, r.c2r, r.c2_out), (q.a2, r.a2r, r.a2_out)):
        lane.arrived(ref.at[others])
        outs.append(pltpu.make_async_copy(ref, out, r.load_sems.at[len(outs)]))
        outs[-1].start()
        lane.left(ref.at[others])
    for out in outs:
        out.wait()


def lane_slots(n, W):
    slots = dict(w=n // 2, wf=1, x=W, t=1, h=n // 2, hf=1, gp=1, gh=1, ls=1, dx=1, gc=1, gb=1, gz=1, a2=1, b1=1, b2=1, c1=1, c2=1)
    return list(slots.items())


FORWARD_LAG, BACKWARD_LAG, PAIR = 6, 28, 12


def step_call(cfg, valid, ins):
    n, m, F, W, S, bins = cfg
    z = layout(cfg)
    CH, L, G, fields, chips, BAND, HQ = z.CH, W * 320, n * W, n * F, n // 2, z.BAND, z.HQ
    FB = F * BAND
    GL = max(G, 128)
    A = jax.ShapeDtypeStruct
    V = pltpu.VMEM
    D = pltpu.SemaphoreType.DMA
    outs = dict(
        dx_out=A((n, W, CH, 128), BF16),
        a2_out=A((m, HQ, 128), BF16),
        b2_out=A((m, z.CB, 128), BF16),
        c2_out=A((m, z.CC, 128), BF16),
        ls_out=A((n, F, 1, GL), F32),
    )
    scr = dict(
        dxr=V((n, W, CH, 128), BF16),
        a2r=V((m, HQ, 128), BF16),
        b2r=V((m, z.CB, 128), BF16),
        c2r=V((m, z.CC, 128), BF16),
        sumc=V((m * z.CC, 128), F32),
        c1s=V((m, z.CC, 128), BF16),
        c1r=V((m, z.CC, 128), BF16),
        c2s=V((z.CC, 128), BF16),
        lsr=V((n, F, 1, GL), F32),
        wf=V((z.R + 16, 128), F32),
        ws=V((z.R + 16, 128), BF16),
        wr=V((n, z.R + 16, 128), BF16),
        tab=V((F, 128, 128), F32),
        hf=V((F, BAND, 128), F32),
        hs=V((FB, 128), BF16),
        hr=V((fields * BAND, 128), BF16),
        row=V((F, S * G), jnp.int32),
        trow=V((F, S * G), jnp.int32),
        hot=V((F, 128, S * G), BF16),
        rows_out=V((G * CH, 128), F32),
        rows_in=V((G * CH, 128), F32),
        xs=V((n, W, CH, 128), BF16),
        xr=V((W, n, CH, 128), BF16),
        tgs=V((fields, 1, 128), F32),
        tgt=V((fields, 1, 128), F32),
        w_in=V((128, 384), BF16),
        w_out=V((128, 128), BF16),
        w_up=V((128, 512), BF16),
        w_down=V((512, 128), BF16),
        vec=V((16, 128), F32),
        x=V((L, 128), F32),
        unit1=V((L, 128), F32),
        inv1=V((L, 128), F32),
        unit2=V((L, 128), F32),
        inv2=V((L, 128), F32),
        n1=V((L, 128), BF16),
        n2=V((L, 128), BF16),
        qm=V((W, 1280, 128), BF16),
        k=V((L, 128), BF16),
        v=V((L, 128), BF16),
        o=V((L, 128), BF16),
        pa=V((W, HEADS, 128, 256), F32),
        pd=V((W, HEADS, 128, 128), F32),
        pb=V((W, 320, 256), F32),
        a=V((L, 512), BF16),
        slope=V((L, 512), F32),
        y=V((L, 128), F32),
        dy=V((L, 128), F32),
        du=V((L, 512), BF16),
        dyb=V((L, 128), BF16),
        db=V((L, 128), BF16),
        dm=V((L, 384), BF16),
        dxs=V((W, n, CH, 128), BF16),
        loss=V((fields, 128), F32),
        lss=V((fields, 1, GL), F32),
        gho=V((chips, FB, 128), F32),
        ghp=V((chips, FB, 128), BF16),
        ghq=V((chips, FB, 128), BF16),
        gzs=V((m, chips, HQ, 128), BF16),
        gzr=V((m, chips, HQ, 128), BF16),
        ghs=V((chips, HQ, 128), BF16),
        ghr=V((chips, HQ, 128), BF16),
        g_in=V((128, 384), F32),
        g_out=V((128, 128), F32),
        g_up=V((128, 512), F32),
        g_down=V((512, 128), F32),
        g_vec=V((16, 128), F32),
        gbf=V((z.RR, 128), F32),
        gbs=V((2, chips, z.RR, 128), BF16),
        gbq=V((chips, z.RR, 128), BF16),
        gbt=V((chips, z.RR, 128), BF16),
        gbr=V((chips, z.RR, 128), BF16),
        a2s=V((HQ, 128), BF16),
        sumb=V((m * z.CB, 128), F32),
        b1s=V((m, z.CB, 128), BF16),
        b1r=V((m, z.CB, 128), BF16),
        b2s=V((z.CB, 128), BF16),
        sems=D((sum(1 + slots for name, slots in lane_slots(n, W)),)),
    )
    names = list(outs) + list(scr)
    hbm = pl.BlockSpec(memory_space=pltpu.HBM)
    inside = [V(v.shape, v.dtype) for v in ins]
    res = pl.pallas_call(
        functools.partial(step_kernel, cfg, names, len(ins)),
        out_shape=list(outs.values()),
        in_specs=[pl.BlockSpec(memory_space=pltpu.SMEM)] + [hbm] * len(ins),
        out_specs=[hbm] * len(outs),
        scratch_shapes=list(scr.values()) + inside + [D((len(ins),))],
        compiler_params=pltpu.CompilerParams(vmem_limit_bytes=VMEM_STEP, collective_id=0, has_side_effects=True),
        cost_estimate=pl.CostEstimate(flops=40_000_000_000, bytes_accessed=4_000_000, transcendentals=0),
        name="step",
    )(valid, *ins)
    return res


VMEM_STEP, VMEM_ADAM = 56 * 1024 * 1024, 10 * 1024 * 1024
RATES = (0.8, 0.6, 1.6 * 128 ** (-0.5), 128 ** (-0.5), 4 ** (-0.5), 128 ** (-0.5), 512 ** (-0.5), 0.3)
EMBED, POSITION, HEAD, BLOCK, VECTOR = 0, 1, 2, 3, 7


def adam_kernel(cfg, count_ref, *refs):
    n, m, F, W, S, bins = cfg
    z = layout(cfg)
    given, state, losses, input_out, outs = refs[:5], refs[5:29], refs[29], refs[30], refs[31:63]
    suma, sumb, sumc, sumd, input_grad, dxr, a2r, b2r, c2r, lsr, sems = refs[63:]
    loads = []
    for i, (there, here) in enumerate(zip(given, (dxr, a2r, b2r, c2r, lsr))):
        loads.append(pltpu.make_async_copy(there, here, sems.at[i]))
        loads[i].start()
    me = lax.axis_index("field")
    half = lax.fori_loop(0, count_ref[0], lambda i, v: v * 0.5, jnp.float32(1.0))
    inv_c = 1.0 / (jnp.zeros((1, 128), F32) + (1.0 - half))

    def adam(weight, at, grad):
        c = inv_c[0:1, 0 : grad.shape[-1]]
        master = state[3 * weight][at]
        first = 0.5 * state[3 * weight + 1][at] + 0.5 * grad
        second = 0.5 * state[3 * weight + 2][at] + 0.5 * grad * grad
        new = master - RATES[weight] * (first * c / (jnp.sqrt(second * c) + 1e-08) + 0.1 * master)
        outs[4 * weight][at] = first
        outs[4 * weight + 1][at] = second
        outs[4 * weight + 2][at] = new
        outs[4 * weight + 3][at] = new.astype(BF16)

    BAND = z.BAND
    loads[0].wait()
    for g in range(n * W):
        input_grad[cut(g, S * F), :] = dxr[g // W, g % W].astype(F32)[: S * F]
    leave = pltpu.make_async_copy(input_grad, input_out, sems.at[5])
    leave.start()
    for load in loads[1:]:
        load.wait()
    for i in range(m):
        sumd[cut(i, z.CC), :] = c2r[i].astype(F32)
        sumb[cut(i, z.CB), :] = b2r[i].astype(F32)
        sumc[cut(i, z.HQ), :] = a2r[i].astype(F32)
    for f in range(F):
        suma[pl.ds(f, BAND, stride=F), :] = sumc[cut(f, BAND), :]
    every = slice(None)
    tokens = F * bins
    adam(HEAD, (every, every), suma[0:tokens, :])
    adam(EMBED, (every, every), sumb[0:tokens, :])
    adam(POSITION, (every, every), sumb[tokens : tokens + S * F, :])
    for name, row, size, block in z.plan:
        adam(BLOCK + name, (every, cut(block, 128)), sumd[row : row + size, :])
    vecs = sumd[z.R : z.R + 16, :]
    pick = lane_pick(me, 128 // n).astype(F32)
    mine = lax.dot_general(
        vecs, pick, (((1,), (1,)), ((), ())), preferred_element_type=F32, precision=lax.Precision.HIGHEST
    )
    adam(VECTOR, (every, every), mine[0:12])
    for f in range(F):
        total = lsr[0, f]
        for i in range(1, n):
            total = total + lsr[i, f]
        losses[f : f + 1, :] = total[:, : n * W]
    leave.wait()


def adam_call(cfg, count, got, state):
    n, m, F, W, S, bins = cfg
    z = layout(cfg)
    A = jax.ShapeDtypeStruct
    given = [pltpu.with_memory_space_constraint(v, pltpu.HBM) for v in got]
    outs = [A((F, n * W), F32), A((n * W * S * F, 128), F32)]
    for i in range(8):
        shape = state[3 * i].shape
        outs.extend([A(shape, F32)] * 3 + [A(shape, BF16)])
    vm = pl.BlockSpec(memory_space=pltpu.VMEM)
    hbm = pl.BlockSpec(memory_space=pltpu.HBM)
    sm = pl.BlockSpec(memory_space=pltpu.SMEM)
    return pl.pallas_call(
        functools.partial(adam_kernel, cfg),
        out_shape=outs,
        in_specs=[sm] + [hbm] * 5 + [vm] * 24,
        out_specs=[vm, hbm] + [vm] * 32,
        scratch_shapes=[pltpu.VMEM((size, 128), F32) for size in (F * z.BAND, m * z.CB, F * z.BAND, m * z.CC, n * W * S * F)]
        + [pltpu.VMEM(v.shape, v.dtype) for v in given]
        + [pltpu.SemaphoreType.DMA((6,))],
        compiler_params=pltpu.CompilerParams(vmem_limit_bytes=VMEM_ADAM),
        name="adam",
    )(count, *given, *state)


def local(n, m, bin_tokens, targets, valid_steps, step_count, *state):
    windows, S, F = bin_tokens.shape
    bins = state[0].shape[1]
    cfg = (n, m, F, windows // n, S, bins)
    by_bin = lambda v: v.transpose(1, 0, 2).reshape(bins * F, 128)
    by_class = lambda v: v.transpose(2, 0, 1).reshape(bins * F, 128)
    flat = [by_bin(v) for v in state[0:3]] + [v.reshape(S * F, 128) for v in state[3:6]]
    flat += [by_class(v) for v in state[6:9]] + list(state[9:])
    blocks = [flat[i] for i in (9, 12, 15, 18, 21, 0, 3)]
    ins = [*blocks, bin_tokens.transpose(1, 2, 0), flat[6], targets.transpose(1, 2, 0)]
    got = step_call(cfg, valid_steps, ins)
    losses, input_grad, *new = adam_call(cfg, step_count.reshape(1), got, flat)
    new[0:4] = [v.reshape(bins, F, 128).transpose(1, 0, 2) for v in new[0:4]]
    new[4:8] = [v.reshape(S, F, 128) for v in new[4:8]]
    new[8:12] = [v.reshape(bins, F, 128).transpose(1, 2, 0) for v in new[8:12]]
    return (losses.transpose(1, 0), input_grad.reshape(windows, S, F, 128), *new)


def solution(mesh):
    n, m = mesh.shape["field"], mesh.shape["dp"]
    stack, rows, cols = P("field", None, None), P("field", None), P(None, "field")
    by_weight = (stack, P(None, "field", None), stack, rows, rows, rows, rows, cols)
    in_specs = [P("dp", None, "field"), P("dp", None, "field"), P("dp"), P()]
    out_specs = [P("dp", "field"), P("dp", None, "field", None)]
    for spec in by_weight:
        in_specs.extend([spec] * 3)
        out_specs.extend([spec] * 4)
    return jax.shard_map(
        functools.partial(local, n, m),
        mesh=mesh,
        in_specs=tuple(in_specs),
        out_specs=tuple(out_specs),
        check_vma=False,
    )
```

```python
import functools
import types
import jax
import jax.numpy as jnp
from jax import lax
from jax.experimental import pallas as pl
from jax.experimental.pallas import tpu as pltpu
from jax.sharding import PartitionSpec as P

F32 = jnp.float32
BF16 = jnp.bfloat16
HEADS = 4
NEG = -1e30


def mm(a, b):
    return jnp.dot(a, b, preferred_element_type=F32)


def mm_nt(a, b):
    return lax.dot_general(a, b, (((1,), (1,)), ((), ())), preferred_element_type=F32)


def mm_tn(a, b):
    return lax.dot_general(a, b, (((0,), (0,)), ((), ())), preferred_element_type=F32)


def head_lanes(shape, head):
    lane = lax.broadcasted_iota(jnp.int32, shape, 1)
    return (lane >= head * 32) & (lane < (head + 1) * 32)


def spread_heads(value):
    parts = []
    for head in range(HEADS):
        parts.append(jnp.where(head_lanes((256, 128), head), value[:256], 0.0))
    for head in range(HEADS):
        parts.append(jnp.where(head_lanes((64, 128), head), value[256:], 0.0))
    return jnp.concatenate(parts, axis=0).astype(BF16)


def join_heads(tall):
    out = tall[0:64]
    for head in range(1, HEADS):
        out = jnp.where(head_lanes((64, 128), head), tall[head * 64 : (head + 1) * 64], out)
    return out


def norm_stats(v):
    mean = jnp.mean(v, axis=-1, keepdims=True)
    c = v - mean
    spread = jnp.mean(c * c, axis=-1, keepdims=True)
    inv = lax.rsqrt(spread + 1e-05)
    return c * inv, jnp.broadcast_to(inv, v.shape)


def norm_back(grad, gain, unit, inv):
    e = grad * gain
    m1 = jnp.mean(e, axis=-1, keepdims=True)
    m2 = jnp.mean(e * unit, axis=-1, keepdims=True)
    return inv * (e - m1 - unit * m2)


SCALE = 32 ** (-0.5)
LOG2E = 1.4426950408889634


def causal_square(n):
    k = lax.broadcasted_iota(jnp.int32, (n, n), 0)
    q = lax.broadcasted_iota(jnp.int32, (n, n), 1)
    return k <= q


def soft_cols(pieces):
    peak = functools.reduce(jnp.maximum, [jnp.max(p, axis=0, keepdims=True) for p in pieces])
    shift = peak * (SCALE * LOG2E)
    es = [jnp.exp2(p * (SCALE * LOG2E) - shift) for p in pieces]
    total = functools.reduce(lambda a, b: a + b, [jnp.sum(e, axis=0, keepdims=True) for e in es])
    inv = 1.0 / total
    return [e * inv for e in es]


def forward_window(w, r, take):
    rows = pl.ds(w * 320, 320)
    vec = r.vec
    take(w)
    yield
    x = r.x[rows, :]
    unit, inv = norm_stats(x)
    r.unit1[rows, :] = unit
    r.inv1[rows, :] = inv
    n1 = (unit * vec[0:1, :] + vec[1:2, :]).astype(BF16)
    r.n1[rows, :] = n1
    yield
    mixed = mm(n1, r.w_in[...])
    q = mixed[:, 0:128] + vec[2:3, :]
    k = mixed[:, 128:256]
    v = mixed[:, 256:384] + vec[3:4, :]
    yield
    qm = spread_heads(q)
    kb = k.astype(BF16)
    vb = v.astype(BF16)
    r.qm[w] = qm
    r.k[rows, :] = kb
    r.v[rows, :] = vb
    vt = v.T.astype(BF16)
    yield
    mask128 = causal_square(128)
    ot_parts = []
    for head in range(HEADS):
        s = mm_nt(kb[0:256], qm[head * 256 : (head + 1) * 256])
        yield
        s00 = jnp.where(mask128, s[0:128, 0:128], NEG)
        (p00,) = soft_cols([s00])
        r.pa[w, head, 0:128, 0:128] = p00
        yield
        s11 = jnp.where(mask128, s[128:256, 128:256], NEG)
        p01, p11 = soft_cols([s[0:128, 128:256], s11])
        r.pa[w, head, 0:128, 128:256] = p01
        r.pd[w, head] = p11
        yield
        b11 = p11.astype(BF16)
        pb = jnp.concatenate(
            [
                jnp.concatenate([p00.astype(BF16), p01.astype(BF16)], axis=1),
                jnp.concatenate([jnp.zeros((128, 128), BF16), b11], axis=1),
            ],
            axis=0,
        )
        ot_parts.append(mm(vt[head * 32 : (head + 1) * 32, 0:256], pb))
        yield
    ot = jnp.concatenate(ot_parts, axis=0)
    sb = mm_nt(kb, qm[1024:1280])
    yield
    kk = lax.broadcasted_iota(jnp.int32, (64, 256), 0)
    qq = lax.broadcasted_iota(jnp.int32, (64, 256), 1) % 64
    pbs = []
    for half in range(2):
        cols = slice(half * 128, (half + 1) * 128)
        s_low = jnp.where((kk <= qq)[:, cols], sb[256:320, cols], NEG)
        p_top, p_low = soft_cols([sb[0:256, cols], s_low])
        r.pb[w, 0:256, cols] = p_top
        r.pb[w, 256:320, cols] = p_low
        pbs.append(jnp.concatenate([p_top.astype(BF16), p_low.astype(BF16)], axis=0))
        yield
    pbb = jnp.concatenate(pbs, axis=1)
    otb = mm(vt, pbb)
    yield
    o_tail = join_heads(otb.T)
    o = jnp.concatenate([ot.T, o_tail], axis=0).astype(BF16)
    r.o[rows, :] = o
    yield
    x1 = x + mm(o, r.w_out[...]) + vec[4:5, :]
    yield
    unit, inv = norm_stats(x1)
    r.unit2[rows, :] = unit
    r.inv2[rows, :] = inv
    n2 = (unit * vec[5:6, :] + vec[6:7, :]).astype(BF16)
    r.n2[rows, :] = n2
    yield
    y = x1 + vec[7:8, :]
    for part in range(2):
        cols = cut(part, 256)
        bias = jnp.concatenate([vec[8 + 2 * part : 9 + 2 * part, :], vec[9 + 2 * part : 10 + 2 * part, :]], axis=1)
        u = mm(n2, r.w_up[:, cols]) + bias
        yield
        phi = 0.5 * (1.0 + lax.erf(u * 0.7071067811865476))
        a = (u * phi).astype(BF16)
        r.a[rows, cols] = a
        r.slope[rows, cols] = phi + u * jnp.exp2(u * u * (-0.5 * LOG2E)) * 0.3989422804014327
        yield
        y = y + mm(a, r.w_down[cols, :])
        yield
    r.y[rows, :] = y.astype(BF16).astype(F32)


def head_field(f, live, keep, r):
    W, T = r.W, live.shape[1]
    starts = [pl.ds(step * 32 + f, W, stride=320) for step in range(T // W)]
    yf = jnp.concatenate([r.y[at, :] for at in starts], axis=0).astype(BF16)
    wt = r.hr[pl.ds(pl.multiple_of(f * r.band, 16), r.band), :]
    lt = mm_nt(wt, yf)
    yield
    bins = lax.broadcasted_iota(jnp.int32, lt.shape, 0)
    lt = jnp.where(bins < r.bins, lt, NEG)
    peak = jnp.max(lt, axis=0, keepdims=True)
    e = jnp.exp(lt - peak)
    yield
    total = jnp.sum(e, axis=0, keepdims=True)
    lse = peak + jnp.log(total)
    hot = bins.astype(F32) == r.tgt[f][:, :T]
    picked = jnp.sum(jnp.where(hot, lt, 0.0), axis=0, keepdims=True)
    r.loss[pl.ds(f, 1), 0:T] = (lse - picked) * live
    yield
    dl = (jnp.exp(lt - lse) - hot.astype(F32)) * live
    yield
    keep(mm(dl.astype(BF16), yf))
    yield
    dy = mm(dl.T.astype(BF16), wt)
    yield
    dy = dy.astype(BF16).astype(F32)
    for step, at in enumerate(starts):
        r.dy[at, :] = dy[step * W : (step + 1) * W]


def colsum(v):
    return jnp.sum(v, axis=0, keepdims=True)


def backward_window(w, r, give):
    rows = pl.ds(w * 320, 320)
    vec = r.vec
    gv = r.g_vec
    dy = r.dy[rows, :]
    dyb = dy.astype(BF16)
    gv[7:8, :] += colsum(dy)
    dn2 = jnp.zeros((320, 128), F32)
    r.dyb[rows, :] = dyb
    yield
    for part in range(2):
        cols = cut(part, 256)
        da = mm_nt(dyb, r.w_down[cols, :])
        du = (da * r.slope[rows, cols]).astype(BF16)
        bias = colsum(du.astype(F32))
        gv[8 + 2 * part : 9 + 2 * part, :] += bias[:, 0:128]
        gv[9 + 2 * part : 10 + 2 * part, :] += bias[:, 128:256]
        r.du[rows, cols] = du
        dn2 = dn2 + mm_nt(du, r.w_up[:, cols])
        yield
    unit = r.unit2[rows, :]
    gv[5:6, :] += colsum(dn2 * unit)
    gv[6:7, :] += colsum(dn2)
    dx1 = dy + norm_back(dn2, vec[5:6, :], unit, r.inv2[rows, :])
    yield
    db = dx1.astype(BF16)
    gv[4:5, :] += colsum(db.astype(F32))
    r.db[rows, :] = db
    do = mm_nt(db, r.w_out[...])
    yield
    dom = spread_heads(do)
    kb = r.k[rows, :]
    vb = r.v[rows, :]
    kt = kb.astype(F32).T.astype(BF16)
    dv = jnp.zeros((256, 128), F32)
    dk = jnp.zeros((256, 128), F32)
    dqt = []
    yield
    for head in range(HEADS):
        part = slice(head * 256, (head + 1) * 256)
        p00 = r.pa[w, head, 0:128, 0:128]
        p01 = r.pa[w, head, 0:128, 128:256]
        p11 = r.pd[w, head]
        dp = mm_nt(vb[0:256], dom[part])
        yield
        d0 = p00 * dp[0:128, 0:128]
        d1a = p01 * dp[0:128, 128:256]
        d1b = p11 * dp[128:256, 128:256]
        t0 = colsum(d0)
        t1 = colsum(d1a) + colsum(d1b)
        ds00 = (d0 - p00 * t0).astype(BF16)
        ds01 = (d1a - p01 * t1).astype(BF16)
        ds11 = (d1b - p11 * t1).astype(BF16)
        yield
        zero = jnp.zeros((128, 128), BF16)
        pb = jnp.concatenate(
            [
                jnp.concatenate([p00.astype(BF16), p01.astype(BF16)], axis=1),
                jnp.concatenate([zero, p11.astype(BF16)], axis=1),
            ],
            axis=0,
        )
        dsb = jnp.concatenate(
            [jnp.concatenate([ds00, ds01], axis=1), jnp.concatenate([zero, ds11], axis=1)], axis=0
        )
        dv = dv + mm(pb, dom[part])
        dk = dk + mm(dsb, r.qm[w, part, :])
        dqt.append(mm(kt[head * 32 : (head + 1) * 32, 0:256], dsb))
        yield
    pt = r.pb[w]
    dp = mm_nt(vb, dom[1024:1280])
    yield
    d = pt * dp
    dsb = (d - pt * colsum(d)).astype(BF16)
    yield
    dvb = mm(pt.astype(BF16), dom[1024:1280])
    dkb = mm(dsb, r.qm[w, 1024:1280, :])
    yield
    dq_tail = join_heads(mm(kt, dsb).T)
    dq = jnp.concatenate([jnp.concatenate(dqt, axis=0).T, dq_tail], axis=0) * SCALE
    dv = jnp.concatenate([dv + dvb[0:256], dvb[256:320]], axis=0)
    dk = jnp.concatenate([dk + dkb[0:256], dkb[256:320]], axis=0) * SCALE
    dq = dq.astype(BF16)
    dk = dk.astype(BF16)
    dv = dv.astype(BF16)
    yield
    gv[2:3, :] += colsum(dq.astype(F32))
    gv[3:4, :] += colsum(dv.astype(F32))
    dm = jnp.concatenate([dq, dk, dv], axis=1)
    r.dm[rows, :] = dm
    dn1 = mm_nt(dm, r.w_in[...])
    yield
    unit = r.unit1[rows, :]
    gv[0:1, :] += colsum(dn1 * unit)
    gv[1:2, :] += colsum(dn1)
    dx = dx1 + norm_back(dn1, vec[0:1, :], unit, r.inv1[rows, :])
    r.dx[rows, :] = dx
    yield
    give(w)


def weave(gens, delays, hooks=()):
    live = [[g, wait] for g, wait in zip(gens, delays)]
    hooks = dict(hooks)
    turn = 0
    while live:
        if turn in hooks:
            hooks.pop(turn)()
        for item in list(live):
            if item[1] > 0:
                item[1] -= 1
                continue
            try:
                next(item[0])
            except StopIteration:
                live.remove(item)
        turn += 1
    for left in sorted(hooks):
        hooks[left]()


MESH = pl.DeviceIdType.MESH


def plan_rows(n, parts):
    plan, row = [], 0
    for name in parts:
        total, blocks = ((128, 3), (128, 1), (128, 4), (512, 1))[name]
        size = total // n
        for block in range(blocks):
            plan.append((name, row, size, block))
            row += size
    return plan, -(-row // 16) * 16


class Lane:
    def __init__(self, sems, first, anyone):
        self.sems, self.first, self.anyone = sems, first, anyone

    def copy(self, src, dst, slot, target):
        return pltpu.make_async_remote_copy(
            src_ref=src,
            dst_ref=dst,
            send_sem=self.sems.at[self.first],
            recv_sem=self.sems.at[self.first + 1 + slot],
            device_id=target,
            device_id_type=MESH,
        )

    def start(self, src, dst, target, slot=0):
        self.copy(src, dst, slot, target).start()

    def arrived(self, like, slot=0):
        self.copy(like, like, slot, self.anyone).wait_recv()

    def left(self, like):
        self.copy(like, like, 0, self.anyone).wait_send()


def lane_pick(me, width):
    row = lax.broadcasted_iota(jnp.int32, (width, 128), 0)
    lane = lax.broadcasted_iota(jnp.int32, (width, 128), 1)
    return lane == row + me * width


def cut(i, size):
    return slice(i * size, (i + 1) * size)


def layout(cfg):
    n, m, F, W, S, bins = cfg
    CH = -(-S * F // 8) * 8
    BAND = 112 if F * 112 % (8 * m) == 0 else 128
    plan, R = plan_rows(n, (0, 1, 2, 3))
    RR = R + 16
    CB = F * BAND // m
    CC = -(-RR // (16 * m)) * 16
    HQ = F * BAND // m
    return types.SimpleNamespace(CH=CH, BAND=BAND, plan=plan, R=R, RR=RR, CB=CB, CC=CC, HQ=HQ)


def step_kernel(cfg, names, count, valid, *refs):
    r = types.SimpleNamespace(**dict(zip(names, refs[count:])))
    r.valid, r.outside, r.inside, r.load_sems = valid, refs[:count], refs[-1 - count : -1], refs[-1]
    n, m, F, W, S, bins = cfg
    z = layout(cfg)
    CH, T, G, fields, BAND, HQ = z.CH, S * W, n * W, n * F, z.BAND, z.HQ
    FB = F * BAND
    r.bins, r.W, r.band = bins, W, BAND
    r.xsf = r.dxf = r.rows_out
    r.xf = r.dxw = r.rows_in
    r.dx = r.y
    me, my = lax.axis_index("field"), lax.axis_index("dp")
    chips = n // 2
    core, chip = lax.rem(me, 2), me // 2
    partner = {"field": me + 1 - 2 * core}
    other = lambda k: lax.rem(chip + k, chips)
    back = lambda k: lax.rem(chip + chips - k, chips)
    far = lambda k: {"field": other(k) * 2 + core}
    peer = lambda o: lax.rem(me + o, n)
    field_at = lambda o: {"field": peer(o)}
    dp_at = lambda o: {"dp": lax.rem(my + o, m)}

    barrier = pltpu.get_barrier_semaphore()
    for o in range(1, n):
        pl.semaphore_signal(barrier, 1, device_id=field_at(o), device_id_type=MESH)
    for o in range(1, m):
        pl.semaphore_signal(barrier, 1, device_id=dp_at(o), device_id_type=MESH)

    loads = []
    for i, (there, here) in enumerate(zip(r.outside, r.inside)):
        loads.append(pltpu.make_async_copy(there, here, r.load_sems.at[i]))
        loads[-1].start()
    for load in loads:
        load.wait()

    lanes, count = {}, 0
    for name, slots in lane_slots(n, W):
        lanes[name] = Lane(r.sems, count, partner)
        count += 1 + slots
    q = types.SimpleNamespace(**lanes)

    r.inproj, r.outproj, r.expand, r.shrink, r.vector, r.embed, r.position, r.tok, r.head, r.tgi = r.inside
    masters = (r.inproj, r.outproj, r.expand, r.shrink)
    for name, row, size, block in z.plan:
        r.wf[row : row + size, :] = masters[name][:, cut(block, 128)]
    r.wf[z.R : z.R + 16, :] = jnp.zeros((16, 128), F32)
    r.wf[z.R : z.R + 12, :] = mm(r.vector[...].astype(BF16), lane_pick(me, 128 // n).astype(BF16))
    r.ws[...] = r.wf[...].astype(BF16)
    for f in range(F):
        r.tab[f, bins - 4 :, :] = jnp.zeros((132 - bins, 128), F32)
        r.tab[f, 0:bins, :] = r.embed[pl.ds(f, bins, stride=F), :]
        r.tab[f, bins : bins + S, :] = r.position[pl.ds(f, S, stride=F), :]
        r.hf[f, bins - 4 :, :] = jnp.zeros((BAND + 4 - bins, 128), F32)
        r.hf[f, 0:bins, :] = r.head[pl.ds(f, bins, stride=F), :]
        r.hs[cut(f, BAND), :] = r.hf[f].astype(BF16)

    row = lax.broadcasted_iota(jnp.int32, (128, S * G), 0)
    step_row = lax.broadcasted_iota(jnp.int32, (1, S * G), 1) // G + bins
    for s in range(S):
        r.row[:, cut(s, G)] = r.tok[s]
        r.trow[:, cut(s, G)] = r.tgi[s]
    for f in range(F):
        hot = ((row == r.row[f : f + 1, :]) | (row == step_row)).astype(F32).astype(BF16)
        r.hot[f] = hot
        made = mm_tn(hot, r.tab[f].astype(BF16))
        for s in range(S):
            for d in range(n):
                at = s * G + d * W
                r.xsf[pl.ds(d * W * CH + s * F + f, W, stride=CH), :] = made[at : at + W]
    if S * F < CH:
        for g in range(G):
            r.xsf[g * CH + S * F : (g + 1) * CH, :] = jnp.zeros((CH - S * F, 128), F32)
    for d in range(n):
        for w in range(W):
            r.xs[d, w] = r.xsf[cut(d * W + w, CH), :].astype(BF16)

    pl.semaphore_wait(barrier, n - 1 + m - 1)

    q.w.start(r.ws, r.wr.at[me], partner, 0)
    for k in range(1, chips):
        q.w.start(r.ws, r.wr.at[me], far(k), k)
    for w in range(W):
        for o in range(1, n):
            q.x.start(r.xs.at[peer(o), w], r.xr.at[w, me], field_at(o), w)
    r.wr[me] = r.ws[...]
    for w in range(W):
        r.xr[w, me] = r.xs[me, w]

    own = lax.broadcasted_iota(jnp.int32, (fields, S * G), 1) % G // W
    mine = own == lax.broadcasted_iota(jnp.int32, (fields, S * G), 0) // F
    spread = jnp.concatenate([r.trow[...].astype(F32)] * n, axis=0)
    spread = jnp.where(mine, spread, 0.0).astype(BF16)
    source = lax.broadcasted_iota(jnp.int32, (S * G, 128), 0)
    place = lax.broadcasted_iota(jnp.int32, (S * G, 128), 1)
    move = (source // G * W + source % W == place).astype(F32).astype(BF16)
    target_rows = mm(spread, move)
    for i in range(fields):
        r.tgs[i] = target_rows[i : i + 1]
    there = pl.ds(me * F, F)
    for o in range(1, n):
        q.t.start(r.tgs.at[pl.ds(peer(o) * F, F)], r.tgt.at[there], field_at(o))
    mine = pl.ds(pl.multiple_of(me * FB, 16), FB)
    q.h.start(r.hs, r.hr.at[mine], partner, 0)
    for k in range(1, chips):
        q.h.start(r.hs, r.hr.at[mine], far(k), k)
    for f in range(F):
        r.tgt[me * F + f] = r.tgs[me * F + f]
    r.hr[mine, :] = r.hs[...]

    for k in range(1, chips):
        q.w.arrived(r.ws, k)
        slot = r.wr.at[back(k) * 2 + core]
        q.wf.start(slot, slot, partner)
    q.w.arrived(r.ws, 0)
    q.wf.arrived(r.wr.at[pl.ds(0, chips - 1)])
    full = (r.w_in, r.w_out, r.w_up, r.w_down)
    wide = (r.g_in, r.g_out, r.g_up, r.g_down)
    vec = jnp.zeros((16, 128), F32)
    for i in range(n):
        shard = r.wr[i].astype(F32)
        vec = vec + shard[z.R :]
        for name, row, size, block in z.plan:
            to = full if size % 16 == 0 else wide
            piece = shard[row : row + size]
            to[name][cut(i, size), cut(block, 128)] = piece.astype(to[name].dtype)
    for name, row, size, block in z.plan:
        if size % 16:
            full[name][:, cut(block, 128)] = wide[name][:, cut(block, 128)].astype(BF16)
    r.vec[...] = vec
    r.g_vec[...] = jnp.zeros((16, 128), F32)

    def take(w):
        q.x.arrived(r.xr.at[w, pl.ds(0, n - 1)], w)
        for i in range(n):
            r.xf[cut(w * n + i, CH), :] = r.xr[w, i].astype(F32)
        for s in range(S):
            for f in range(F):
                got = r.xf[pl.ds(w * n * CH + s * F + f, n, stride=CH), :]
                r.x[pl.ds(w * 320 + s * fields + f, n, stride=F), :] = got

    weave([forward_window(w, r, take) for w in range(W)], [FORWARD_LAG * w for w in range(W)])

    q.t.arrived(r.tgs.at[pl.ds(0, (n - 1) * F)])
    lane = lax.broadcasted_iota(jnp.int32, (1, T), 1)
    live = jnp.zeros((1, T), F32)
    for w in range(W):
        inside = (lane // W).astype(F32) < r.valid[me * W + w].astype(F32)
        live = jnp.where(inside & (lane % W == w), 1.0, live)
    r.loss[...] = jnp.zeros_like(r.loss)

    def keeper(ref, c, f):
        def keep(v):
            ref[c, cut(f, BAND), :] = v.astype(ref.dtype)

        return keep

    def heads(*places):
        gens = []
        for c, which, ref in places:
            gens.extend(head_field((c * 2 + which) * F + f, live, keeper(ref, c, f), r) for f in range(F))
        weave(gens, [0] * len(gens))

    for k in range(1, chips):
        q.h.arrived(r.hs, k)
        slot = r.hr.at[pl.ds(pl.multiple_of((back(k) * 2 + core) * FB, 16), FB)]
        q.hf.start(slot, slot, partner)
    heads(*[(other(k), core, r.gho) for k in range(chips)])
    q.h.arrived(r.hs, 0)
    q.hf.arrived(r.hr.at[pl.ds(0, (chips - 1) * FB)])
    heads(*[(other(k), 1 - core, r.ghp) for k in range(chips)])
    q.gp.start(r.ghp, r.ghq, partner)

    def send_losses():
        GL = r.lss.shape[-1]
        row = lax.broadcasted_iota(jnp.int32, (128, GL), 0)
        col = lax.broadcasted_iota(jnp.int32, (128, GL), 1)
        group = ((row < T) & (col == me * W + row % W)).astype(F32)
        sums = jnp.dot(r.loss[...], group, preferred_element_type=F32, precision=lax.Precision.HIGHEST)
        for f in range(fields):
            r.lss[f] = sums[f : f + 1, :]
        for o in range(1, n):
            q.ls.start(r.lss.at[pl.ds(peer(o) * F, F)], r.lsr.at[me], field_at(o))
        r.lsr[me] = r.lss[there]

    def give(w):
        for s in range(S):
            for f in range(F):
                got = r.dx[pl.ds(w * 320 + s * fields + f, n, stride=F), :]
                r.dxf[pl.ds(w * n * CH + s * F + f, n, stride=CH), :] = got
        for i in range(n):
            if S * F < CH:
                r.dxf[(w * n + i) * CH + S * F : (w * n + i + 1) * CH, :] = jnp.zeros((CH - S * F, 128), F32)
            r.dxs[w, i] = r.dxf[cut(w * n + i, CH), :].astype(BF16)
        for o in range(1, n):
            q.dx.start(r.dxs.at[w, peer(o)], r.dxr.at[me, w], field_at(o))
        r.dxr[me, w] = r.dxs[w, me]

    def pair_heads():
        q.gp.arrived(r.ghp)
        for c in range(chips):
            total = r.gho[c] + r.ghq[c].astype(F32)
            for j in range(m):
                r.gzs[j, c] = total[cut(j, HQ)].astype(BF16)
        for o in range(1, m):
            q.gz.start(r.gzs.at[lax.rem(my + o, m)], r.gzr.at[my], dp_at(o))
        r.gzr[my] = r.gzs[my]
        send_losses()

    def plane_heads():
        q.gz.arrived(r.gzr.at[pl.ds(0, m - 1)])
        for c in range(chips):
            total = r.gzr[0, c].astype(F32)
            for j in range(1, m):
                total = total + r.gzr[j, c].astype(F32)
            r.ghs[c] = total.astype(BF16)
        for k in range(1, chips):
            q.gh.start(r.ghs.at[other(k)], r.ghr.at[chip], far(k))
        r.ghr[chip] = r.ghs[chip]

    def share_heads():
        q.gh.arrived(r.ghr.at[pl.ds(0, chips - 1)])
        r.a2s[...] = total_of(r.ghr, chips).astype(BF16)
        for o in range(1, m):
            q.a2.start(r.a2s, r.a2r.at[my], dp_at(o))
        r.a2r[my] = r.a2s[...]

    grads = (r.g_in, r.g_out, r.g_up, r.g_down)

    def total_of(ref, count):
        total = ref[0].astype(F32)
        for i in range(1, count):
            total = total + ref[i].astype(F32)
        return total

    def dp_first(total, send, recv, lane):
        C = send.shape[1]
        for i in range(m):
            send[i] = total[cut(i, C), :].astype(BF16)
        for o in range(1, m):
            lane.start(send.at[lax.rem(my + o, m)], recv.at[my], dp_at(o))
        recv[my] = send[my]

    def dp_second(recv, lane, last, out, last_lane):
        lane.arrived(recv.at[pl.ds(0, m - 1)])
        last[...] = total_of(recv, m).astype(BF16)
        for o in range(1, m):
            last_lane.start(last, out.at[my], dp_at(o))
        out[my] = last[...]

    hooks = {PAIR: pair_heads}
    weave([backward_window(w, r, give) for w in range(W)], [BACKWARD_LAG * (2 * w // W) for w in range(W)], hooks)

    r.g_up[...] = mm_tn(r.n2[...], r.du[...])
    r.g_down[...] = mm_tn(r.dyb[...], r.a[...]).T
    r.g_out[...] = mm_tn(r.o[...], r.db[...])
    r.g_in[...] = mm_tn(r.n1[...], r.dm[...])
    r.gbf[z.R :, :] = r.g_vec[...]
    for i in range(n):
        for name, row, size, block in z.plan:
            r.gbf[row : row + size, :] = grads[name][cut(i, size), cut(block, 128)]
        r.gbs[i % 2, i // 2] = r.gbf[...].astype(BF16)
    q.gc.start(r.gbs.at[1 - core], r.gbq, partner)
    q.gc.arrived(r.gbq)
    for c in range(chips):
        r.gbt[c] = (r.gbs[core, c].astype(F32) + r.gbq[c].astype(F32)).astype(BF16)
    for k in range(1, chips):
        q.gb.start(r.gbt.at[other(k)], r.gbr.at[chip], far(k))
    r.gbr[chip] = r.gbt[chip]

    q.dx.arrived(r.dxr.at[pl.ds(0, n - 1)])
    outs = [pltpu.make_async_copy(r.dxr, r.dx_out, r.load_sems.at[0])]
    outs[0].start()
    for g in range(G):
        r.dxw[cut(g, CH), :] = r.dxr[g // W, g % W].astype(F32)
    for f in range(F):
        rows = [r.dxw[pl.ds(s * F + f, G, stride=CH), :] for s in range(S)]
        total = mm(r.hot[f], jnp.concatenate(rows, axis=0).astype(BF16))
        r.sumb[pl.ds(f, BAND, stride=F), :] = total[:BAND]
    dp_first(r.sumb, r.b1s, r.b1r, q.b1)
    plane_heads()
    q.gb.arrived(r.gbr.at[pl.ds(0, chips - 1)])
    r.sumc[0 : z.RR, :] = total_of(r.gbr, chips)
    if m * z.CC > z.RR:
        r.sumc[z.RR :, :] = jnp.zeros((m * z.CC - z.RR, 128), F32)
    dp_first(r.sumc, r.c1s, r.c1r, q.c1)

    q.w.left(r.wr.at[pl.ds(0, chips)])
    q.wf.left(r.wr.at[pl.ds(0, chips - 1)])
    q.x.left(r.xr.at[:, pl.ds(0, n - 1)])
    q.t.left(r.tgs.at[pl.ds(0, (n - 1) * F)])
    q.h.left(r.hr.at[pl.ds(0, chips * FB)])
    q.hf.left(r.hr.at[pl.ds(0, (chips - 1) * FB)])
    q.gp.left(r.ghp)
    q.ls.left(r.lsr.at[pl.ds(0, n - 1)])
    q.ls.arrived(r.lsr.at[pl.ds(0, n - 1)])
    outs.append(pltpu.make_async_copy(r.lsr, r.ls_out, r.load_sems.at[1]))
    outs[1].start()
    q.gc.left(r.gbq)
    q.gb.left(r.gbr.at[pl.ds(0, chips - 1)])
    q.dx.left(r.dxr.at[pl.ds(0, n - 1)])
    q.gz.left(r.gzr.at[pl.ds(0, m - 1)])
    dp_second(r.b1r, q.b1, r.b2s, r.b2r, q.b2)
    share_heads()
    dp_second(r.c1r, q.c1, r.c2s, r.c2r, q.c2)
    q.gh.left(r.ghr.at[pl.ds(0, chips - 1)])
    others = pl.ds(0, m - 1)
    q.b1.left(r.b1r.at[others])
    q.c1.left(r.c1r.at[others])
    for lane, ref, out in ((q.b2, r.b2r, r.b2_out), (q.c2, r.c2r, r.c2_out), (q.a2, r.a2r, r.a2_out)):
        lane.arrived(ref.at[others])
        outs.append(pltpu.make_async_copy(ref, out, r.load_sems.at[len(outs)]))
        outs[-1].start()
        lane.left(ref.at[others])
    for out in outs:
        out.wait()


def lane_slots(n, W):
    slots = dict(w=n // 2, wf=1, x=W, t=1, h=n // 2, hf=1, gp=1, gh=1, ls=1, dx=1, gc=1, gb=1, gz=1, a2=1, b1=1, b2=1, c1=1, c2=1)
    return list(slots.items())


FORWARD_LAG, BACKWARD_LAG, PAIR = 6, 28, 12


def step_call(cfg, valid, ins):
    n, m, F, W, S, bins = cfg
    z = layout(cfg)
    CH, L, G, fields, chips, BAND, HQ = z.CH, W * 320, n * W, n * F, n // 2, z.BAND, z.HQ
    FB = F * BAND
    GL = max(G, 128)
    A = jax.ShapeDtypeStruct
    V = pltpu.VMEM
    D = pltpu.SemaphoreType.DMA
    outs = dict(
        dx_out=A((n, W, CH, 128), BF16),
        a2_out=A((m, HQ, 128), BF16),
        b2_out=A((m, z.CB, 128), BF16),
        c2_out=A((m, z.CC, 128), BF16),
        ls_out=A((n, F, 1, GL), F32),
    )
    scr = dict(
        dxr=V((n, W, CH, 128), BF16),
        a2r=V((m, HQ, 128), BF16),
        b2r=V((m, z.CB, 128), BF16),
        c2r=V((m, z.CC, 128), BF16),
        sumc=V((m * z.CC, 128), F32),
        c1s=V((m, z.CC, 128), BF16),
        c1r=V((m, z.CC, 128), BF16),
        c2s=V((z.CC, 128), BF16),
        lsr=V((n, F, 1, GL), F32),
        wf=V((z.R + 16, 128), F32),
        ws=V((z.R + 16, 128), BF16),
        wr=V((n, z.R + 16, 128), BF16),
        tab=V((F, 128, 128), F32),
        hf=V((F, BAND, 128), F32),
        hs=V((FB, 128), BF16),
        hr=V((fields * BAND, 128), BF16),
        row=V((F, S * G), jnp.int32),
        trow=V((F, S * G), jnp.int32),
        hot=V((F, 128, S * G), BF16),
        rows_out=V((G * CH, 128), F32),
        rows_in=V((G * CH, 128), F32),
        xs=V((n, W, CH, 128), BF16),
        xr=V((W, n, CH, 128), BF16),
        tgs=V((fields, 1, 128), F32),
        tgt=V((fields, 1, 128), F32),
        w_in=V((128, 384), BF16),
        w_out=V((128, 128), BF16),
        w_up=V((128, 512), BF16),
        w_down=V((512, 128), BF16),
        vec=V((16, 128), F32),
        x=V((L, 128), F32),
        unit1=V((L, 128), F32),
        inv1=V((L, 128), F32),
        unit2=V((L, 128), F32),
        inv2=V((L, 128), F32),
        n1=V((L, 128), BF16),
        n2=V((L, 128), BF16),
        qm=V((W, 1280, 128), BF16),
        k=V((L, 128), BF16),
        v=V((L, 128), BF16),
        o=V((L, 128), BF16),
        pa=V((W, HEADS, 128, 256), F32),
        pd=V((W, HEADS, 128, 128), F32),
        pb=V((W, 320, 256), F32),
        a=V((L, 512), BF16),
        slope=V((L, 512), F32),
        y=V((L, 128), F32),
        dy=V((L, 128), F32),
        du=V((L, 512), BF16),
        dyb=V((L, 128), BF16),
        db=V((L, 128), BF16),
        dm=V((L, 384), BF16),
        dxs=V((W, n, CH, 128), BF16),
        loss=V((fields, 128), F32),
        lss=V((fields, 1, GL), F32),
        gho=V((chips, FB, 128), F32),
        ghp=V((chips, FB, 128), BF16),
        ghq=V((chips, FB, 128), BF16),
        gzs=V((m, chips, HQ, 128), BF16),
        gzr=V((m, chips, HQ, 128), BF16),
        ghs=V((chips, HQ, 128), BF16),
        ghr=V((chips, HQ, 128), BF16),
        g_in=V((128, 384), F32),
        g_out=V((128, 128), F32),
        g_up=V((128, 512), F32),
        g_down=V((512, 128), F32),
        g_vec=V((16, 128), F32),
        gbf=V((z.RR, 128), F32),
        gbs=V((2, chips, z.RR, 128), BF16),
        gbq=V((chips, z.RR, 128), BF16),
        gbt=V((chips, z.RR, 128), BF16),
        gbr=V((chips, z.RR, 128), BF16),
        a2s=V((HQ, 128), BF16),
        sumb=V((m * z.CB, 128), F32),
        b1s=V((m, z.CB, 128), BF16),
        b1r=V((m, z.CB, 128), BF16),
        b2s=V((z.CB, 128), BF16),
        sems=D((sum(1 + slots for name, slots in lane_slots(n, W)),)),
    )
    names = list(outs) + list(scr)
    hbm = pl.BlockSpec(memory_space=pltpu.HBM)
    inside = [V(v.shape, v.dtype) for v in ins]
    res = pl.pallas_call(
        functools.partial(step_kernel, cfg, names, len(ins)),
        out_shape=list(outs.values()),
        in_specs=[pl.BlockSpec(memory_space=pltpu.SMEM)] + [hbm] * len(ins),
        out_specs=[hbm] * len(outs),
        scratch_shapes=list(scr.values()) + inside + [D((len(ins),))],
        compiler_params=pltpu.CompilerParams(vmem_limit_bytes=VMEM_STEP, collective_id=0, has_side_effects=True),
        cost_estimate=pl.CostEstimate(flops=40_000_000_000, bytes_accessed=4_000_000, transcendentals=0),
        name="step",
    )(valid, *ins)
    return res


VMEM_STEP, VMEM_ADAM = 56 * 1024 * 1024, 10 * 1024 * 1024
RATES = (0.8, 0.6, 1.6 * 128 ** (-0.5), 128 ** (-0.5), 4 ** (-0.5), 128 ** (-0.5), 512 ** (-0.5), 0.3)
EMBED, POSITION, HEAD, BLOCK, VECTOR = 0, 1, 2, 3, 7


def adam_kernel(cfg, count_ref, *refs):
    n, m, F, W, S, bins = cfg
    z = layout(cfg)
    given, state, losses, input_out, outs = refs[:5], refs[5:29], refs[29], refs[30], refs[31:63]
    suma, sumb, sumc, sumd, input_grad, dxr, a2r, b2r, c2r, lsr, sems = refs[63:]
    loads = []
    for i, (there, here) in enumerate(zip(given, (dxr, a2r, b2r, c2r, lsr))):
        loads.append(pltpu.make_async_copy(there, here, sems.at[i]))
        loads[i].start()
    me = lax.axis_index("field")
    half = lax.fori_loop(0, count_ref[0], lambda i, v: v * 0.5, jnp.float32(1.0))
    inv_c = 1.0 / (jnp.zeros((1, 128), F32) + (1.0 - half))

    def adam(weight, at, grad):
        c = inv_c[0:1, 0 : grad.shape[-1]]
        master = state[3 * weight][at]
        first = 0.5 * state[3 * weight + 1][at] + 0.5 * grad
        second = 0.5 * state[3 * weight + 2][at] + 0.5 * grad * grad
        new = master - RATES[weight] * (first * c / (jnp.sqrt(second * c) + 1e-08) + 0.1 * master)
        outs[4 * weight][at] = first
        outs[4 * weight + 1][at] = second
        outs[4 * weight + 2][at] = new
        outs[4 * weight + 3][at] = new.astype(BF16)

    BAND = z.BAND
    loads[0].wait()
    for g in range(n * W):
        input_grad[cut(g, S * F), :] = dxr[g // W, g % W].astype(F32)[: S * F]
    leave = pltpu.make_async_copy(input_grad, input_out, sems.at[5])
    leave.start()
    for load in loads[1:]:
        load.wait()
    for i in range(m):
        sumd[cut(i, z.CC), :] = c2r[i].astype(F32)
        sumb[cut(i, z.CB), :] = b2r[i].astype(F32)
        sumc[cut(i, z.HQ), :] = a2r[i].astype(F32)
    for f in range(F):
        suma[pl.ds(f, BAND, stride=F), :] = sumc[cut(f, BAND), :]
    every = slice(None)
    tokens = F * bins
    adam(HEAD, (every, every), suma[0:tokens, :])
    adam(EMBED, (every, every), sumb[0:tokens, :])
    adam(POSITION, (every, every), sumb[tokens : tokens + S * F, :])
    for name, row, size, block in z.plan:
        adam(BLOCK + name, (every, cut(block, 128)), sumd[row : row + size, :])
    vecs = sumd[z.R : z.R + 16, :]
    pick = lane_pick(me, 128 // n).astype(F32)
    mine = lax.dot_general(
        vecs, pick, (((1,), (1,)), ((), ())), preferred_element_type=F32, precision=lax.Precision.HIGHEST
    )
    adam(VECTOR, (every, every), mine[0:12])
    for f in range(F):
        total = lsr[0, f]
        for i in range(1, n):
            total = total + lsr[i, f]
        losses[f : f + 1, :] = total[:, : n * W]
    leave.wait()


def adam_call(cfg, count, got, state):
    n, m, F, W, S, bins = cfg
    z = layout(cfg)
    A = jax.ShapeDtypeStruct
    given = [pltpu.with_memory_space_constraint(v, pltpu.HBM) for v in got]
    outs = [A((F, n * W), F32), A((n * W * S * F, 128), F32)]
    for i in range(8):
        shape = state[3 * i].shape
        outs.extend([A(shape, F32)] * 3 + [A(shape, BF16)])
    vm = pl.BlockSpec(memory_space=pltpu.VMEM)
    hbm = pl.BlockSpec(memory_space=pltpu.HBM)
    sm = pl.BlockSpec(memory_space=pltpu.SMEM)
    return pl.pallas_call(
        functools.partial(adam_kernel, cfg),
        out_shape=outs,
        in_specs=[sm] + [hbm] * 5 + [vm] * 24,
        out_specs=[vm, hbm] + [vm] * 32,
        scratch_shapes=[pltpu.VMEM((size, 128), F32) for size in (F * z.BAND, m * z.CB, F * z.BAND, m * z.CC, n * W * S * F)]
        + [pltpu.VMEM(v.shape, v.dtype) for v in given]
        + [pltpu.SemaphoreType.DMA((6,))],
        compiler_params=pltpu.CompilerParams(vmem_limit_bytes=VMEM_ADAM),
        name="adam",
    )(count, *given, *state)


def local(n, m, bin_tokens, targets, valid_steps, step_count, *state):
    windows, S, F = bin_tokens.shape
    bins = state[0].shape[1]
    cfg = (n, m, F, windows // n, S, bins)
    by_bin = lambda v: v.transpose(1, 0, 2).reshape(bins * F, 128)
    by_class = lambda v: v.transpose(2, 0, 1).reshape(bins * F, 128)
    flat = [by_bin(v) for v in state[0:3]] + [v.reshape(S * F, 128) for v in state[3:6]]
    flat += [by_class(v) for v in state[6:9]] + list(state[9:])
    blocks = [flat[i] for i in (9, 12, 15, 18, 21, 0, 3)]
    ins = [*blocks, bin_tokens.transpose(1, 2, 0), flat[6], targets.transpose(1, 2, 0)]
    got = step_call(cfg, valid_steps, ins)
    losses, input_grad, *new = adam_call(cfg, step_count.reshape(1), got, flat)
    new[0:4] = [v.reshape(bins, F, 128).transpose(1, 0, 2) for v in new[0:4]]
    new[4:8] = [v.reshape(S, F, 128) for v in new[4:8]]
    new[8:12] = [v.reshape(bins, F, 128).transpose(1, 2, 0) for v in new[8:12]]
    return (losses.transpose(1, 0), input_grad.reshape(windows, S, F, 128), *new)


def solution(mesh):
    n, m = mesh.shape["field"], mesh.shape["dp"]
    stack, rows, cols = P("field", None, None), P("field", None), P(None, "field")
    by_weight = (stack, P(None, "field", None), stack, rows, rows, rows, rows, cols)
    in_specs = [P("dp", None, "field"), P("dp", None, "field"), P("dp"), P()]
    out_specs = [P("dp", "field"), P("dp", None, "field", None)]
    for spec in by_weight:
        in_specs.extend([spec] * 3)
        out_specs.extend([spec] * 4)
    return jax.shard_map(
        functools.partial(local, n, m),
        mesh=mesh,
        in_specs=tuple(in_specs),
        out_specs=tuple(out_specs),
        check_vma=False,
    )
```
